128 devices in a mesh: seq: 32 (over x, y, core), head: 4 (over z).
Axes of the slice: x: 4, y: 4, z: 4, core: 2. Of those that a mesh axis runs over, the one named last changes fastest.
Arguments:
- queries: bfloat16 [32768, 7168], P('seq', 'head'), may hold values from -9 to 9
- token_keys: bfloat16 [32768, 7168], P('seq', 'head'), may hold values from -9 to 9
- token_values: bfloat16 [32768, 7168], P('seq', 'head'), may hold values from -6 to 6
- mem_keys: bfloat16 [16384, 7168], P('seq', 'head'), may hold values from -9 to 9
- mem_values: bfloat16 [16384, 7168], P('seq', 'head'), may hold values from -6 to 6
- retrieved: int32 [64, 56, 2], P('seq', 'head'), may hold values from 0 to 127, as said below
- gate_bias: float32 [56], P('head'), may hold values from -2 to 2
Outputs:
- attended: bfloat16 [32768, 7168], P('seq', 'head')
The draws below stay inside these ranges and needn't reach their ends.
Inputs may be any that keep to these rules, and one draw needn't show every extreme that they name: `retrieved`: block i belongs to shard i // 4. The 2 ids of one list differ. One shard, the same for all devices, is named exactly 7 times among the ids of one device (its query blocks and its heads); every other shard is named at most 3 times there, and some other shard exactly 3 times.
All inputs are finite; a program needn't handle non-finite values.
Results may differ from the reference program's by a relative error of at most 0.011.
Values may be sent and summed in bfloat16 or wider, within the bound.
No kernel may reach another device: no remote copies, remote signals or barrier semaphores. Data moves between devices by JAX's collectives and lax.ppermute only.
A program may use at most 256 MiB of HBM per device.

```python
import jax
import jax.numpy as jnp
from jax import lax

H = 56
DH = 128
TOK_DEV = 1024
MEM_BLOCKS = 128
QB = 512
MB = 128
TOPK = 2
WIN = 512
TOKENS = 32768
CAP = 7
REST_CAP = 3
N_SEQ = 32
N_HEAD = 4


def rough_field(draw_key, row_total, col_total):
    base_key = jax.random.fold_in(draw_key, 0)
    return jax.random.truncated_normal(base_key, -6.0, 6.0, (row_total, col_total), jnp.float32)


def draw_queries(key, part):
    field = rough_field(jax.random.fold_in(key, 11), TOKENS, H * DH)
    return field.astype(jnp.bfloat16)


def draw_token_keys(key, part):
    field = rough_field(jax.random.fold_in(key, 12), TOKENS, H * DH)
    return field.astype(jnp.bfloat16)


def draw_mem_keys(key, part):
    field = rough_field(jax.random.fold_in(key, 13), MEM_BLOCKS * MB, H * DH)
    return field.astype(jnp.bfloat16)


def draw_retrieved(key, part):
    heads_dev = H // N_HEAD
    blocks_dev = TOK_DEV // QB
    request_total = heads_dev * blocks_dev * TOPK
    memory_dev = MEM_BLOCKS // N_SEQ
    other_slots = (N_SEQ - 1) * REST_CAP
    popular = jax.random.randint(jax.random.fold_in(key, 7001), (), 0, N_SEQ)

    def one_device(device_index):
        device_key = jax.random.fold_in(jax.random.fold_in(key, 7002), device_index)
        key_parts = jax.random.split(device_key, 4)
        second = jax.random.randint(key_parts[0], (), 0, N_SEQ - 1)
        shuffled = jax.random.permutation(key_parts[1], other_slots)
        slot_rank = jnp.argsort(shuffled)
        candidate = jnp.arange(other_slots)
        sort_key = jnp.where(candidate // REST_CAP == second, candidate % REST_CAP - REST_CAP, slot_rank)
        chosen = jnp.argsort(sort_key)[:request_total - CAP]
        owner_rest = (popular + 1 + chosen // REST_CAP) % N_SEQ
        owners = jnp.concatenate([jnp.full((CAP,), popular, jnp.int32), owner_rest.astype(jnp.int32)])
        owners = jax.random.permutation(key_parts[2], owners)
        base_slot = jax.random.randint(key_parts[3], (blocks_dev * heads_dev, 1), 0, memory_dev)
        slot_index = (base_slot + jnp.arange(TOPK)[None, :]) % memory_dev
        block_ids = owners.reshape(blocks_dev * heads_dev, TOPK) * memory_dev + slot_index
        return block_ids.reshape(blocks_dev, heads_dev, TOPK)
    all_devices = jax.vmap(one_device)(jnp.arange(N_SEQ * N_HEAD))
    all_devices = all_devices.reshape(N_SEQ, N_HEAD, blocks_dev, heads_dev, TOPK)
    all_devices = jnp.transpose(all_devices, (0, 2, 1, 3, 4))
    return all_devices.reshape(N_SEQ * blocks_dev, N_HEAD * heads_dev, TOPK).astype(jnp.int32)


def shard_levels(stream_key, shape, pieces, least, largest):
    level = 1.0
    for dim, shards_of in pieces:
        heights = jax.random.uniform(jax.random.fold_in(jax.random.fold_in(stream_key, 6), dim), (shards_of,), jnp.float32, least / len(pieces), largest / len(pieces))
        level = level * jnp.repeat(jnp.exp(heights), shape[dim] // shards_of).reshape((-1,) + (1,) * (len(shape) - 1 - dim))
    return level


def gaussian(own_key, extent, scale, reach, pieces=(), kind=jnp.bfloat16):
    level = shard_levels(own_key, extent, pieces, -0.22, 0.18) if pieces else 1.0
    drawn = jax.random.normal(own_key, extent, jnp.float32) * scale * level
    return jnp.minimum(jnp.maximum(drawn, -reach), reach).astype(kind)


def setup_inputs(seed: int = 0) -> dict:
    arg_keys = jax.random.split(jax.random.key(seed), 8)
    return {
        "queries": draw_queries(jax.random.fold_in(arg_keys[7], 71), 0),
        "token_keys": draw_token_keys(jax.random.fold_in(arg_keys[7], 71), 0),
        "token_values": gaussian(arg_keys[2], (TOKENS, H * DH), 1.0, 6.0, ((0, 32), (1, 4))),
        "mem_keys": draw_mem_keys(jax.random.fold_in(arg_keys[7], 71), 0),
        "mem_values": gaussian(arg_keys[4], (MEM_BLOCKS * MB, H * DH), 1.0, 6.0, ((0, 32), (1, 4))),
        "retrieved": draw_retrieved(jax.random.fold_in(arg_keys[7], 71), 0),
        "gate_bias": jnp.clip(jax.random.uniform(arg_keys[6], (H,), jnp.float32, -2.0, 2.0) * shard_levels(arg_keys[6], (H,), ((0, 4),), -0.4, 0.0), -2.0, 2.0),
    }


def soft_weights(scores, allowed):
    masked = jnp.where(allowed, scores, -1e30)
    row_top = jnp.max(masked, axis=-1, keepdims=True)
    expo_terms = jnp.exp(masked - row_top)
    return (expo_terms / jnp.sum(expo_terms, axis=-1, keepdims=True)).astype(jnp.bfloat16)


def reference(queries, token_keys, token_values, mem_keys, mem_values, retrieved, gate_bias):
    total_rows = queries.shape[0]
    score_scale = DH ** -0.5
    query_grid = queries.reshape(total_rows, H, DH)
    zero_rows = jnp.zeros((WIN, H * DH), jnp.bfloat16)
    padded_keys = jnp.concatenate([zero_rows, token_keys], axis=0).reshape(total_rows + WIN, H, DH)
    padded_values = jnp.concatenate([zero_rows, token_values], axis=0).reshape(total_rows + WIN, H, DH)
    block_rows = min(512, TOK_DEV)

    def local_block(block_index):
        row_start = (block_index * block_rows).astype(jnp.int32)
        block_query = lax.dynamic_slice_in_dim(query_grid, row_start, block_rows, 0)
        block_keys = lax.dynamic_slice_in_dim(padded_keys, row_start, block_rows + WIN, 0)
        block_values = lax.dynamic_slice_in_dim(padded_values, row_start, block_rows + WIN, 0)
        scores = jnp.einsum("qhd,khd->hqk", block_query.astype(jnp.float32), block_keys.astype(jnp.float32)) * score_scale
        query_pos = row_start + jnp.arange(block_rows, dtype=jnp.int32)[:, None]
        key_pos = row_start - WIN + jnp.arange(block_rows + WIN, dtype=jnp.int32)[None, :]
        allowed = (key_pos <= query_pos) & (query_pos - key_pos < WIN) & (key_pos >= 0)
        weights = soft_weights(scores, allowed[None])
        return jnp.einsum("hqk,khd->qhd", weights.astype(jnp.float32), block_values.astype(jnp.float32))

    local_out = lax.map(local_block, jnp.arange(total_rows // block_rows, dtype=jnp.int32)).reshape(total_rows, H, DH)

    memory_grid_keys = mem_keys.reshape(MEM_BLOCKS, MB, H, DH)
    memory_grid_values = mem_values.reshape(MEM_BLOCKS, MB, H, DH)
    head_ids = jnp.arange(H, dtype=jnp.int32)[:, None]

    def memory_block(block_index):
        row_start = (block_index * QB).astype(jnp.int32)
        block_query = lax.dynamic_slice_in_dim(query_grid, row_start, QB, 0)
        chosen = retrieved[block_index].astype(jnp.int32)
        picked_keys = memory_grid_keys[chosen, :, head_ids, :].reshape(H, TOPK * MB, DH)
        picked_values = memory_grid_values[chosen, :, head_ids, :].reshape(H, TOPK * MB, DH)
        scores = jnp.einsum("qhd,hkd->hqk", block_query.astype(jnp.float32), picked_keys.astype(jnp.float32)) * score_scale
        weights = soft_weights(scores, True)
        return jnp.einsum("hqk,hkd->qhd", weights.astype(jnp.float32), picked_values.astype(jnp.float32))

    remote_out = lax.map(memory_block, jnp.arange(total_rows // QB, dtype=jnp.int32)).reshape(total_rows, H, DH)
    gate_share = (1.0 / (1.0 + jnp.exp(-gate_bias)))[None, :, None]
    mixed = gate_share * remote_out + (1.0 - gate_share) * local_out
    return mixed.reshape(total_rows, H * DH).astype(jnp.bfloat16)
```

```python
import functools

import jax
import jax.numpy as jnp
from jax import lax
from jax.experimental import pallas as pl
from jax.experimental.pallas import tpu as pltpu
from jax.sharding import PartitionSpec as P

QB = 512
MB = 128
TOPK = 2
WIN = 512
DH = 128
PIECE = 8
EDGE = 256
LOG2E = 1.4426950408889634
NEG = -1e30
BF = jnp.bfloat16
F32 = jnp.float32


def pack_kernel(blocks, heads, keys_ref, values_ref, ids_ref, out_ref):
    pieces = MB // PIECE
    for block in range(blocks):
        rows = pl.ds(block * pieces, pieces)
        for head in range(heads):
            cols = pl.ds(head * DH, DH)
            out_ref[0:pieces, block * heads + head] = keys_ref[rows, :, cols]
            out_ref[pieces : 2 * pieces, block * heads + head] = values_ref[rows, :, cols]
    for device in range(2 * pieces):
        out_ref[device, blocks * heads] = ids_ref[...]


def pack(mem_keys, mem_values, ids_tile, blocks, heads):
    rows, width = mem_keys.shape
    shape = (rows // PIECE, PIECE, width)
    return pl.pallas_call(
        functools.partial(pack_kernel, blocks, heads),
        out_shape=jax.ShapeDtypeStruct((2 * MB // PIECE, blocks * heads + 1, PIECE, DH), BF),
        in_specs=[pl.BlockSpec(memory_space=pltpu.VMEM)] * 3,
        out_specs=pl.BlockSpec(memory_space=pltpu.VMEM),
        compiler_params=pltpu.CompilerParams(vmem_limit_bytes=32 << 20),
        name="pack_pieces",
    )(mem_keys.reshape(shape), mem_values.reshape(shape), ids_tile)


def gather_kernel(wanted, group, rows_ref, store_ref, out_ref):
    first = pl.program_id(0) * group

    @pl.loop(0, group)
    def _(device):
        base = (first + device) * wanted
        for request in range(wanted):
            out_ref[device, request] = store_ref[rows_ref[base + request]]


def gather(rows, store, devices, wanted):
    group = 8
    return pl.pallas_call(
        functools.partial(gather_kernel, wanted, group),
        out_shape=jax.ShapeDtypeStruct((devices, wanted, PIECE, DH), BF),
        grid_spec=pltpu.PrefetchScalarGridSpec(
            num_scalar_prefetch=1,
            grid=(devices // group,),
            in_specs=[pl.BlockSpec(store.shape, lambda i, rows: (0, 0, 0))],
            out_specs=pl.BlockSpec((group, wanted, PIECE, DH), lambda i, rows: (i, 0, 0, 0)),
        ),
        compiler_params=pltpu.CompilerParams(vmem_limit_bytes=32 << 20),
        name="gather_pieces",
    )(rows, store)


def dot_t(a, b):
    return lax.dot_general(a, b, (((1,), (1,)), ((), ())), preferred_element_type=F32)


def dot(a, b):
    return jnp.dot(a, b, preferred_element_type=F32)


def triangle():
    row = lax.broadcasted_iota(jnp.int32, (EDGE, EDGE), 0)
    col = lax.broadcasted_iota(jnp.int32, (EDGE, EDGE), 1)
    return col <= row


def spread_lane(stat, lane, store_ref, rows):
    lanes = lax.broadcasted_iota(jnp.int32, (EDGE, DH), 1)
    store_ref[rows, :] = jnp.where(lanes == lane, stat, store_ref[rows, :])


def own_kernel(scale, q_ref, k_ref, v_ref, out_ref, lse_ref):
    head = pl.program_id(0)
    lower = triangle()
    c = scale * LOG2E
    blocks = q_ref.shape[0] // EDGE
    near = WIN // EDGE
    for i in range(blocks):
        rows = pl.ds(i * EDGE, EDGE)
        q = q_ref[rows, :]
        diag = dot_t(q, k_ref[rows, :])
        whole = i >= near
        if whole:
            edge_rows = pl.ds((i - near) * EDGE, EDGE)
            diag = jnp.where(lower, diag, dot_t(q, k_ref[edge_rows, :]))
        else:
            diag = jnp.where(lower, diag, NEG)
        inner = range(max(0, i - near + 1), i)
        parts = [dot_t(q, k_ref[pl.ds(j * EDGE, EDGE), :]) for j in inner]
        top = jnp.max(diag, axis=1, keepdims=True)
        for part in parts:
            top = jnp.maximum(top, jnp.max(part, axis=1, keepdims=True))
        p = jnp.exp2((diag - top) * c)
        total = jnp.sum(p, axis=1, keepdims=True)
        if whole:
            acc = dot(jnp.where(lower, p, 0.0).astype(BF), v_ref[rows, :])
            acc += dot(jnp.where(lower, 0.0, p).astype(BF), v_ref[edge_rows, :])
        else:
            acc = dot(p.astype(BF), v_ref[rows, :])
        for j, part in zip(inner, parts):
            p = jnp.exp2((part - top) * c)
            total += jnp.sum(p, axis=1, keepdims=True)
            acc += dot(p.astype(BF), v_ref[pl.ds(j * EDGE, EDGE), :])
        out_ref[rows, :] = acc / total
        if not whole:
            spread_lane(top * c + jnp.log2(total), head, lse_ref, rows)


def own_attention(queries, keys, values, heads, scale):
    tokens = queries.shape[0]
    column = pl.BlockSpec((tokens, DH), lambda h: (0, h))
    return pl.pallas_call(
        functools.partial(own_kernel, scale),
        out_shape=(
            jax.ShapeDtypeStruct(queries.shape, F32),
            jax.ShapeDtypeStruct((WIN, DH), F32),
        ),
        grid=(heads,),
        in_specs=[column] * 3,
        out_specs=(column, pl.BlockSpec((WIN, DH), lambda h: (0, 0))),
        compiler_params=pltpu.CompilerParams(vmem_limit_bytes=32 << 20),
        name="own_attention",
    )(queries, keys, values)


def next_kernel(scale, heads, q_ref, k_ref, v_ref, out_ref, lse_ref):
    head = pl.program_id(0)
    c = scale * LOG2E

    @pl.when(head < heads)
    def _():
        lower = triangle()
        blocks = q_ref.shape[0] // EDGE
        for i in range(blocks):
            rows = pl.ds(i * EDGE, EDGE)
            q = q_ref[rows, :]
            edge = jnp.where(lower, NEG, dot_t(q, k_ref[rows, :]))
            inner = range(i + 1, blocks)
            parts = [dot_t(q, k_ref[pl.ds(j * EDGE, EDGE), :]) for j in inner]
            top = jnp.max(edge, axis=1, keepdims=True)
            for part in parts:
                top = jnp.maximum(top, jnp.max(part, axis=1, keepdims=True))
            p = jnp.exp2((edge - top) * c)
            total = jnp.sum(p, axis=1, keepdims=True)
            acc = dot(p.astype(BF), v_ref[rows, :])
            for j, part in zip(inner, parts):
                p = jnp.exp2((part - top) * c)
                total += jnp.sum(p, axis=1, keepdims=True)
                acc += dot(p.astype(BF), v_ref[pl.ds(j * EDGE, EDGE), :])
            out_ref[rows, :] = (acc / total).astype(BF)
            spread_lane(top * c + jnp.log2(total), head, lse_ref, rows)

    @pl.when(head == heads)
    def _():
        lanes = lax.broadcasted_iota(jnp.int32, lse_ref.shape, 1)
        stat = jnp.where(lanes < heads, lse_ref[...], 0.0)
        high = stat.astype(BF)
        rest = stat - high.astype(F32)
        mid = rest.astype(BF)
        low = (rest - mid.astype(F32)).astype(BF)
        out_ref[...] = (
            high.astype(F32)
            + pltpu.roll(mid.astype(F32), heads, 1)
            + pltpu.roll(low.astype(F32), 2 * heads, 1)
        ).astype(BF)


def next_attention(queries, keys, values, heads, scale):
    column = pl.BlockSpec((WIN, DH), lambda h: (0, jnp.minimum(h, heads - 1)))
    tail = pl.BlockSpec((WIN, DH), lambda h: (keys.shape[0] // WIN - 1, jnp.minimum(h, heads - 1)))
    return pl.pallas_call(
        functools.partial(next_kernel, scale, heads),
        out_shape=jax.ShapeDtypeStruct((WIN, (heads + 1) * DH), BF),
        grid=(heads + 1,),
        in_specs=[column, tail, tail],
        out_specs=pl.BlockSpec((WIN, DH), lambda h: (0, h)),
        scratch_shapes=[pltpu.VMEM((WIN, DH), F32)],
        compiler_params=pltpu.CompilerParams(vmem_limit_bytes=32 << 20),
        name="next_attention",
    )(queries, keys, values)


def final_kernel(
    scale, heads, first_ref, gate_ref, q_ref, kv_ref, own_ref, lse_ref, back_ref, stat_ref, out_ref
):
    head = pl.program_id(0)
    c = scale * LOG2E
    gate = gate_ref[head]
    pieces = MB // PIECE
    blocks = q_ref.shape[0] // QB
    for b in range(blocks):
        rows = pl.ds(b * QB, QB)
        mine = slice(b * TOPK, (b + 1) * TOPK)
        keys = kv_ref[0:pieces, mine].astype(F32).reshape(TOPK * MB, DH).astype(BF)
        values = kv_ref[pieces : 2 * pieces, mine].astype(F32).reshape(TOPK * MB, DH).astype(BF)
        s = dot_t(q_ref[rows, :], keys)
        top = jnp.max(s, axis=1, keepdims=True)
        p = jnp.exp2((s - top) * c)
        total = jnp.sum(p, axis=1, keepdims=True)
        remote = dot(p.astype(BF), values) / total
        local = own_ref[rows, :]
        if b == 0:
            lanes = lax.broadcasted_iota(jnp.int32, (WIN, DH), 1)
            lse = jnp.sum(jnp.where(lanes == head, lse_ref[...], 0.0), axis=1, keepdims=True)
            hit = (lanes == head) | (lanes == head + heads) | (lanes == head + 2 * heads)
            other = jnp.sum(
                jnp.where(hit, stat_ref[...].astype(F32), 0.0), axis=1, keepdims=True
            )
            other = jnp.where(first_ref[0] == 0, NEG, other)
            share = 1.0 / (1.0 + jnp.exp2(other - lse))
            back = back_ref[...].astype(F32)
            local = local * share + back * (1.0 - share)
        out_ref[rows, :] = (gate * remote + (1.0 - gate) * local).astype(BF)


def final_attention(first, gate, queries, kv, own, lse, back, heads, scale):
    tokens = queries.shape[0]
    blocks = tokens // QB
    column = pl.BlockSpec((tokens, DH), lambda h, *_: (0, h))
    return pl.pallas_call(
        functools.partial(final_kernel, scale, heads),
        out_shape=jax.ShapeDtypeStruct(queries.shape, BF),
        grid_spec=pltpu.PrefetchScalarGridSpec(
            num_scalar_prefetch=2,
            grid=(heads,),
            in_specs=[
                column,
                pl.BlockSpec((kv.shape[0], blocks * TOPK, PIECE, DH), lambda h, *_: (0, h, 0, 0)),
                column,
                pl.BlockSpec((WIN, DH), lambda h, *_: (0, 0)),
                pl.BlockSpec((WIN, DH), lambda h, *_: (0, h)),
                pl.BlockSpec((WIN, DH), lambda h, *_: (0, heads)),
            ],
            out_specs=column,
        ),
        compiler_params=pltpu.CompilerParams(vmem_limit_bytes=32 << 20),
        name="final_attention",
    )(first, gate, queries, kv, own, lse, back, back)


def body(queries, token_keys, token_values, mem_keys, mem_values, retrieved, gate_bias):
    tokens = queries.shape[0]
    heads = gate_bias.shape[0]
    scale = DH ** (-0.5)
    devices = lax.axis_size("seq")
    blocks = mem_keys.shape[0] // MB
    q_blocks = tokens // QB
    wanted = q_blocks * heads * TOPK
    head_q = queries[:WIN]
    ids = retrieved.transpose(1, 0, 2).reshape(-1)
    ids_tile = jnp.zeros((PIECE * DH,), BF).at[:wanted].set(ids.astype(BF)).reshape(PIECE, DH)
    sent = pack(mem_keys, mem_values, ids_tile, blocks, heads)
    store = lax.all_to_all(sent, "seq", split_axis=0, concat_axis=0, tiled=True)
    next_q = lax.ppermute(head_q, "seq", [(i, i - 1) for i in range(1, devices)])
    own, lse = own_attention(queries, token_keys, token_values, heads, scale)
    partial = next_attention(next_q, token_keys, token_values, heads, scale)
    back = lax.ppermute(partial, "seq", [(i, i + 1) for i in range(devices - 1)])
    all_ids = store[:, blocks * heads, 0, :wanted].astype(jnp.int32)
    stride = blocks * heads + 1
    request_head = jnp.arange(wanted, dtype=jnp.int32) // (q_blocks * TOPK)
    rows = (all_ids // blocks) * stride + (all_ids % blocks) * heads + request_head[None, :]
    pieces = gather(
        rows.reshape(-1), store.reshape(devices * stride, PIECE, DH), devices, wanted
    )
    kv = lax.all_to_all(pieces, "seq", split_axis=0, concat_axis=0, tiled=True)
    gate_share = 1.0 / (1.0 + jnp.exp(-gate_bias))
    first = lax.axis_index("seq").reshape(1).astype(jnp.int32)
    return final_attention(first, gate_share, queries, kv, own, lse, back, heads, scale)


def solution(mesh):
    in_specs = (
        P("seq", "head"),
        P("seq", "head"),
        P("seq", "head"),
        P("seq", "head"),
        P("seq", "head"),
        P("seq", "head", None),
        P("head"),
    )
    return jax.shard_map(
        body, mesh=mesh, in_specs=in_specs, out_specs=P("seq", "head"), check_vma=False
    )
```

```python
import functools

import jax
import jax.numpy as jnp
from jax import lax
from jax.experimental import pallas as pl
from jax.experimental.pallas import tpu as pltpu
from jax.sharding import PartitionSpec as P

QB = 512
MB = 128
TOPK = 2
WIN = 512
DH = 128
PIECE = 8
EDGE = 256
LOG2E = 1.4426950408889634
NEG = -1e30
VMEM_LIMIT = 16 << 20


def params():
    return pltpu.CompilerParams(vmem_limit_bytes=VMEM_LIMIT)


def cost(micros):
    return pl.CostEstimate(flops=int(micros * 1e9), transcendentals=0, bytes_accessed=0)
BF = jnp.bfloat16
F32 = jnp.float32


def pack_kernel(blocks, heads, keys_ref, values_ref, ids_ref, out_ref):
    pieces = MB // PIECE
    for block in range(blocks):
        rows = pl.ds(block * pieces, pieces)
        for head in range(heads):
            cols = pl.ds(head * DH, DH)
            out_ref[0:pieces, block * heads + head] = keys_ref[rows, :, cols]
            out_ref[pieces : 2 * pieces, block * heads + head] = values_ref[rows, :, cols]
    for device in range(2 * pieces):
        out_ref[device, blocks * heads] = ids_ref[...]


def pack(mem_keys, mem_values, ids_tile, blocks, heads):
    rows, width = mem_keys.shape
    shape = (rows // PIECE, PIECE, width)
    return pl.pallas_call(
        functools.partial(pack_kernel, blocks, heads),
        out_shape=jax.ShapeDtypeStruct((2 * MB // PIECE, blocks * heads + 1, PIECE, DH), BF),
        in_specs=[pl.BlockSpec(memory_space=pltpu.VMEM)] * 3,
        out_specs=pl.BlockSpec(memory_space=pltpu.VMEM),
        compiler_params=params(),
        cost_estimate=cost(2),
        name="pack_pieces",
    )(mem_keys.reshape(shape), mem_values.reshape(shape), ids_tile)


def gather_kernel(wanted, group, rows_ref, store_ref, out_ref):
    first = pl.program_id(0) * group

    @pl.loop(0, group)
    def _(device):
        base = (first + device) * wanted
        for request in range(wanted):
            out_ref[device, request] = store_ref[rows_ref[base + request]]


def gather(rows, store, devices, wanted):
    group = 8
    return pl.pallas_call(
        functools.partial(gather_kernel, wanted, group),
        out_shape=jax.ShapeDtypeStruct((devices, wanted, PIECE, DH), BF),
        grid_spec=pltpu.PrefetchScalarGridSpec(
            num_scalar_prefetch=1,
            grid=(devices // group,),
            in_specs=[pl.BlockSpec(store.shape, lambda i, rows: (0, 0, 0))],
            out_specs=pl.BlockSpec((group, wanted, PIECE, DH), lambda i, rows: (i, 0, 0, 0)),
        ),
        compiler_params=params(),
        cost_estimate=cost(6),
        name="gather_pieces",
    )(rows, store)


def dot_t(a, b):
    return lax.dot_general(a, b, (((1,), (1,)), ((), ())), preferred_element_type=F32)


def dot(a, b):
    return jnp.dot(a, b, preferred_element_type=F32)


def triangle():
    row = lax.broadcasted_iota(jnp.int32, (EDGE, EDGE), 0)
    col = lax.broadcasted_iota(jnp.int32, (EDGE, EDGE), 1)
    return col <= row


def spread_lane(stat, lane, store_ref, rows):
    lanes = lax.broadcasted_iota(jnp.int32, (EDGE, DH), 1)
    store_ref[rows, :] = jnp.where(lanes == lane, stat, store_ref[rows, :])


def own_kernel(scale, q_ref, k_ref, v_ref, out_ref, lse_ref):
    head = pl.program_id(0)
    lower = triangle()
    c = scale * LOG2E
    blocks = q_ref.shape[0] // EDGE
    near = WIN // EDGE
    for i in range(blocks):
        rows = pl.ds(i * EDGE, EDGE)
        q = q_ref[rows, :]
        diag = dot_t(q, k_ref[rows, :])
        whole = i >= near
        if whole:
            edge_rows = pl.ds((i - near) * EDGE, EDGE)
            diag = jnp.where(lower, diag, dot_t(q, k_ref[edge_rows, :]))
        else:
            diag = jnp.where(lower, diag, NEG)
        inner = range(max(0, i - near + 1), i)
        parts = [dot_t(q, k_ref[pl.ds(j * EDGE, EDGE), :]) for j in inner]
        top = jnp.max(diag, axis=1, keepdims=True)
        for part in parts:
            top = jnp.maximum(top, jnp.max(part, axis=1, keepdims=True))
        p = jnp.exp2((diag - top) * c)
        total = jnp.sum(p, axis=1, keepdims=True)
        if whole:
            acc = dot(jnp.where(lower, p, 0.0).astype(BF), v_ref[rows, :])
            acc += dot(jnp.where(lower, 0.0, p).astype(BF), v_ref[edge_rows, :])
        else:
            acc = dot(p.astype(BF), v_ref[rows, :])
        for j, part in zip(inner, parts):
            p = jnp.exp2((part - top) * c)
            total += jnp.sum(p, axis=1, keepdims=True)
            acc += dot(p.astype(BF), v_ref[pl.ds(j * EDGE, EDGE), :])
        out_ref[rows, :] = acc / total
        if not whole:
            spread_lane(top * c + jnp.log2(total), head, lse_ref, rows)


def own_attention(queries, keys, values, heads, scale):
    tokens = queries.shape[0]
    column = pl.BlockSpec((tokens, DH), lambda h: (0, h))
    return pl.pallas_call(
        functools.partial(own_kernel, scale),
        out_shape=(
            jax.ShapeDtypeStruct(queries.shape, F32),
            jax.ShapeDtypeStruct((WIN, DH), F32),
        ),
        grid=(heads,),
        in_specs=[column] * 3,
        out_specs=(column, pl.BlockSpec((WIN, DH), lambda h: (0, 0))),
        compiler_params=params(),
        cost_estimate=cost(20),
        name="own_attention",
    )(queries, keys, values)


def next_kernel(scale, heads, q_ref, k_ref, v_ref, out_ref, lse_ref):
    head = pl.program_id(0)
    c = scale * LOG2E

    @pl.when(head < heads)
    def _():
        lower = triangle()
        blocks = q_ref.shape[0] // EDGE
        for i in range(blocks):
            rows = pl.ds(i * EDGE, EDGE)
            q = q_ref[rows, :]
            edge = jnp.where(lower, NEG, dot_t(q, k_ref[rows, :]))
            inner = range(i + 1, blocks)
            parts = [dot_t(q, k_ref[pl.ds(j * EDGE, EDGE), :]) for j in inner]
            top = jnp.max(edge, axis=1, keepdims=True)
            for part in parts:
                top = jnp.maximum(top, jnp.max(part, axis=1, keepdims=True))
            p = jnp.exp2((edge - top) * c)
            total = jnp.sum(p, axis=1, keepdims=True)
            acc = dot(p.astype(BF), v_ref[rows, :])
            for j, part in zip(inner, parts):
                p = jnp.exp2((part - top) * c)
                total += jnp.sum(p, axis=1, keepdims=True)
                acc += dot(p.astype(BF), v_ref[pl.ds(j * EDGE, EDGE), :])
            out_ref[rows, :] = (acc / total).astype(BF)
            spread_lane(top * c + jnp.log2(total), head, lse_ref, rows)

    @pl.when(head == heads)
    def _():
        lanes = lax.broadcasted_iota(jnp.int32, lse_ref.shape, 1)
        stat = jnp.where(lanes < heads, lse_ref[...], 0.0)
        high = stat.astype(BF)
        rest = stat - high.astype(F32)
        mid = rest.astype(BF)
        low = (rest - mid.astype(F32)).astype(BF)
        out_ref[...] = (
            high.astype(F32)
            + pltpu.roll(mid.astype(F32), heads, 1)
            + pltpu.roll(low.astype(F32), 2 * heads, 1)
        ).astype(BF)


def next_attention(queries, keys, values, heads, scale):
    column = pl.BlockSpec((WIN, DH), lambda h: (0, jnp.minimum(h, heads - 1)))
    tail = pl.BlockSpec((WIN, DH), lambda h: (keys.shape[0] // WIN - 1, jnp.minimum(h, heads - 1)))
    return pl.pallas_call(
        functools.partial(next_kernel, scale, heads),
        out_shape=jax.ShapeDtypeStruct((WIN, (heads + 1) * DH), BF),
        grid=(heads + 1,),
        in_specs=[column, tail, tail],
        out_specs=pl.BlockSpec((WIN, DH), lambda h: (0, h)),
        scratch_shapes=[pltpu.VMEM((WIN, DH), F32)],
        compiler_params=params(),
        cost_estimate=cost(30),
        name="next_attention",
    )(queries, keys, values)


def merge_kernel(heads, first_ref, gate_ref, own_ref, lse_ref, back_ref, stat_ref, out_ref):
    head = pl.program_id(0)
    keep = 1.0 - gate_ref[head]
    low, high = pl.ds(0, WIN), pl.ds(WIN, own_ref.shape[0] - WIN)
    lanes = lax.broadcasted_iota(jnp.int32, (WIN, DH), 1)
    lse = jnp.sum(jnp.where(lanes == head, lse_ref[...], 0.0), axis=1, keepdims=True)
    hit = (lanes == head) | (lanes == head + heads) | (lanes == head + 2 * heads)
    other = jnp.sum(jnp.where(hit, stat_ref[...].astype(F32), 0.0), axis=1, keepdims=True)
    other = jnp.where(first_ref[0] == 0, NEG, other)
    share = 1.0 / (1.0 + jnp.exp2(other - lse))
    back = back_ref[...].astype(F32)
    local = own_ref[low, :] * share + back * (1.0 - share)
    out_ref[low, :] = (local * keep).astype(BF)
    out_ref[high, :] = (own_ref[high, :] * keep).astype(BF)


def merge(first, gate, own, lse, back, heads):
    tokens = own.shape[0]
    column = pl.BlockSpec((tokens, DH), lambda h, *_: (0, h))
    return pl.pallas_call(
        functools.partial(merge_kernel, heads),
        out_shape=jax.ShapeDtypeStruct(own.shape, BF),
        grid_spec=pltpu.PrefetchScalarGridSpec(
            num_scalar_prefetch=2,
            grid=(heads,),
            in_specs=[
                column,
                pl.BlockSpec((WIN, DH), lambda h, *_: (0, 0)),
                pl.BlockSpec((WIN, DH), lambda h, *_: (0, h)),
                pl.BlockSpec((WIN, DH), lambda h, *_: (0, heads)),
            ],
            out_specs=column,
        ),
        compiler_params=params(),
        cost_estimate=cost(60),
        name="merge_local",
    )(first, gate, own, lse, back, back)


def final_kernel(scale, heads, gate_ref, q_ref, kv_ref, local_ref, out_ref):
    c = scale * LOG2E
    pieces = MB // PIECE
    for head in range(heads):
        cols = pl.ds(head * DH, DH)
        mine = pl.ds(head * TOPK, TOPK)
        keys = kv_ref[0:pieces, mine].astype(F32).reshape(TOPK * MB, DH).astype(BF)
        values = kv_ref[pieces : 2 * pieces, mine].astype(F32).reshape(TOPK * MB, DH).astype(BF)
        values = jnp.concatenate([values, jnp.ones_like(values)], axis=1)
        s = dot_t(q_ref[:, cols], keys)
        top = jnp.max(s, axis=1, keepdims=True)
        p = jnp.exp2((s - top) * c).astype(BF)
        acc = dot(p, values)
        remote = acc[:, :DH] * (gate_ref[head] / acc[:, DH:])
        out_ref[:, cols] = (remote + local_ref[:, cols].astype(F32)).astype(BF)


def final_attention(gate, queries, kv, local, heads, scale):
    tokens, width = queries.shape
    rows = 256
    per = QB // rows
    band = pl.BlockSpec((rows, width), lambda i, *_: (i, 0))
    return pl.pallas_call(
        functools.partial(final_kernel, scale, heads),
        out_shape=jax.ShapeDtypeStruct(queries.shape, BF),
        grid_spec=pltpu.PrefetchScalarGridSpec(
            num_scalar_prefetch=1,
            grid=(tokens // rows,),
            in_specs=[
                band,
                pl.BlockSpec((kv.shape[0], heads * TOPK, PIECE, DH), lambda i, *_: (0, i // per, 0, 0)),
                band,
            ],
            out_specs=band,
        ),
        compiler_params=params(),
        cost_estimate=cost(7),
        name="final_attention",
    )(gate, queries, kv, local)


def copy_kernel(in_ref, out_ref):
    out_ref[...] = in_ref[...]


def copy_rows(array, rows):
    block = pl.BlockSpec((256, array.shape[1]), lambda i: (i, 0))
    return pl.pallas_call(
        copy_kernel,
        out_shape=jax.ShapeDtypeStruct((rows, array.shape[1]), array.dtype),
        grid=(rows // 256,),
        in_specs=[block],
        out_specs=block,
        name="copy_rows",
    )(array)


def body(queries, token_keys, token_values, mem_keys, mem_values, retrieved, gate_bias):
    tokens = queries.shape[0]
    heads = gate_bias.shape[0]
    scale = DH ** (-0.5)
    devices = lax.axis_size("seq")
    blocks = mem_keys.shape[0] // MB
    q_blocks = tokens // QB
    wanted = q_blocks * heads * TOPK
    head_q = copy_rows(queries, WIN)
    next_q = lax.ppermute(head_q, "seq", [(i, i - 1) for i in range(1, devices)])
    ids = retrieved.reshape(-1)
    ids_tile = jnp.zeros((PIECE * DH,), BF).at[:wanted].set(ids.astype(BF)).reshape(PIECE, DH)
    ids_tile, _ = lax.optimization_barrier((ids_tile, head_q))
    sent = pack(mem_keys, mem_values, ids_tile, blocks, heads)
    store = lax.all_to_all(sent, "seq", split_axis=0, concat_axis=0, tiled=True)
    gate_share = 1.0 / (1.0 + jnp.exp(-gate_bias))
    first = lax.axis_index("seq").reshape(1).astype(jnp.int32)
    own, lse = own_attention(queries, token_keys, token_values, heads, scale)
    partial = next_attention(next_q, token_keys, token_values, heads, scale)
    store, own, lse, partial = lax.optimization_barrier((store, own, lse, partial))
    back = lax.ppermute(partial, "seq", [(i, i + 1) for i in range(devices - 1)])
    all_ids = store[:, blocks * heads, 0, :wanted].astype(jnp.int32)
    stride = blocks * heads + 1
    request_head = jnp.arange(wanted, dtype=jnp.int32) // TOPK % heads
    rows = (all_ids // blocks) * stride + (all_ids % blocks) * heads + request_head[None, :]
    pieces = gather(
        rows.reshape(-1), store.reshape(devices * stride, PIECE, DH), devices, wanted
    )
    kv = lax.all_to_all(pieces, "seq", split_axis=0, concat_axis=0, tiled=True)
    local = merge(first, gate_share, own, lse, back, heads)
    kv, local = lax.optimization_barrier((kv, local))
    return final_attention(gate_share, queries, kv, local, heads, scale)


def solution(mesh):
    in_specs = (
        P("seq", "head"),
        P("seq", "head"),
        P("seq", "head"),
        P("seq", "head"),
        P("seq", "head"),
        P("seq", "head", None),
        P("head"),
    )
    return jax.shard_map(
        body, mesh=mesh, in_specs=in_specs, out_specs=P("seq", "head"), check_vma=False
    )
```

```python
import functools

import jax
import jax.numpy as jnp
from jax import lax
from jax.experimental import pallas as pl
from jax.experimental.pallas import tpu as pltpu
from jax.sharding import PartitionSpec as P

QB = 512
MB = 128
TOPK = 2
WIN = 512
DH = 128
PIECE = 8
EDGE = 256
FORWARD = 5
LOG2E = 1.4426950408889634
NEG = -1e30
VMEM_LIMIT = 24 << 20
BF = jnp.bfloat16
F32 = jnp.float32
ANY = pl.BlockSpec(memory_space=pl.ANY)
WHOLE = pl.BlockSpec(memory_space=pltpu.VMEM)
SMALL = pl.BlockSpec(memory_space=pltpu.SMEM)


def params():
    return pltpu.CompilerParams(vmem_limit_bytes=VMEM_LIMIT)


def cost(micros):
    return pl.CostEstimate(flops=int(micros * 1e9), transcendentals=0, bytes_accessed=0)


def in_hbm(array):
    return pltpu.with_memory_space_constraint(array, pltpu.HBM)


def copy_all(copies):
    for copy in copies:
        copy.start()
    for copy in copies:
        copy.wait()


def edges_kernel(q_ref, k_ref, v_ref, back_ref, ahead_ref, sems):
    split = FORWARD * DH
    tail = pl.ds(k_ref.shape[0] - WIN, WIN)
    width = q_ref.shape[1] - split
    copy_all(
        [
            pltpu.make_async_copy(
                q_ref.at[pl.ds(0, WIN), pl.ds(split, width)], back_ref, sems.at[0]
            ),
            pltpu.make_async_copy(
                k_ref.at[tail, pl.ds(0, split)], ahead_ref.at[:, pl.ds(0, split)], sems.at[1]
            ),
            pltpu.make_async_copy(
                v_ref.at[tail, pl.ds(0, split)], ahead_ref.at[:, pl.ds(split, split)], sems.at[2]
            ),
        ]
    )


def edges(queries, keys, values):
    split = FORWARD * DH
    return pl.pallas_call(
        edges_kernel,
        out_shape=(
            pltpu.HBM((WIN, queries.shape[1] - split), BF),
            pltpu.HBM((WIN, 2 * split), BF),
        ),
        in_specs=[ANY] * 3,
        out_specs=(ANY, ANY),
        scratch_shapes=[pltpu.SemaphoreType.DMA((3,))],
        cost_estimate=cost(2),
        name="cut_edges",
    )(queries, keys, values)


def pack_kernel(blocks, heads, keys_ref, values_ref, ids_ref, out_ref, sems):
    pieces = MB // PIECE
    copies = []
    for half, source in enumerate((keys_ref, values_ref)):
        for block in range(blocks):
            copies.append(
                pltpu.make_async_copy(
                    source.at[pl.ds(block * pieces, pieces)],
                    out_ref.at[pl.ds(half * pieces, pieces), pl.ds(block * heads, heads)],
                    sems.at[len(copies)],
                )
            )
    copies.append(
        pltpu.make_async_copy(ids_ref, out_ref.at[:, pl.ds(blocks * heads, 1)], sems.at[len(copies)])
    )
    copy_all(copies)


def tiles(array):
    rows, width = array.shape
    return array.reshape(rows // PIECE, PIECE, width // DH, DH).transpose(0, 2, 1, 3)


def pack(mem_keys, mem_values, ids_tile, blocks, heads):
    devices = 2 * MB // PIECE
    return pl.pallas_call(
        functools.partial(pack_kernel, blocks, heads),
        out_shape=pltpu.HBM((devices, blocks * heads + 1, PIECE, DH), BF),
        in_specs=[ANY] * 3,
        out_specs=ANY,
        scratch_shapes=[pltpu.SemaphoreType.DMA((2 * blocks + 1,))],
        cost_estimate=cost(2),
        name="pack_pieces",
    )(
        in_hbm(tiles(mem_keys)),
        in_hbm(tiles(mem_values)),
        jnp.broadcast_to(ids_tile, (devices, 1, PIECE, DH)),
    )


def gather_kernel(wanted, group, rows_ref, store_ref, out_ref):
    first = pl.program_id(0) * group

    @pl.loop(0, group)
    def _(device):
        base = (first + device) * wanted
        for request in range(wanted):
            out_ref[device, request] = store_ref[rows_ref[base + request]]


def gather(rows, store, devices, wanted):
    group = 4
    return pl.pallas_call(
        functools.partial(gather_kernel, wanted, group),
        out_shape=pltpu.HBM((devices, wanted, PIECE, DH), BF),
        grid_spec=pltpu.PrefetchScalarGridSpec(
            num_scalar_prefetch=1,
            grid=(devices // group,),
            in_specs=[pl.BlockSpec(store.shape, lambda i, rows: (0, 0, 0))],
            out_specs=pl.BlockSpec((group, wanted, PIECE, DH), lambda i, rows: (i, 0, 0, 0)),
        ),
        compiler_params=params(),
        cost_estimate=cost(6),
        name="gather_pieces",
    )(rows, store)


def dot_t(a, b):
    return lax.dot_general(a, b, (((1,), (1,)), ((), ())), preferred_element_type=F32)


def dot(a, b):
    return jnp.dot(a, b, preferred_element_type=F32)


def with_ones(values):
    return jnp.concatenate([values, jnp.ones_like(values)], axis=1)


def triangle():
    row = lax.broadcasted_iota(jnp.int32, (EDGE, EDGE), 0)
    col = lax.broadcasted_iota(jnp.int32, (EDGE, EDGE), 1)
    return col <= row


def own_kernel(scale, heads, q_ref, k_ref, v_ref, low_ref, lse_ref, out_ref):
    lower = triangle()
    c = scale * LOG2E
    lanes = lax.broadcasted_iota(jnp.int32, (EDGE, DH), 1)
    for head in range(heads):
        cols = pl.ds(head * DH, DH)
        for i in range(WIN // EDGE):
            rows = pl.ds(i * EDGE, EDGE)
            seen = pl.ds(0, (i + 1) * EDGE)
            s = dot_t(q_ref[rows, cols], k_ref[seen, cols])
            diag = jnp.where(lower, s[:, i * EDGE :], NEG)
            if i:
                s = jnp.concatenate([s[:, : i * EDGE], diag], axis=1)
            else:
                s = diag
            top = jnp.max(s, axis=1, keepdims=True)
            p = jnp.exp2((s - top) * c).astype(BF)
            acc = dot(p, with_ones(v_ref[seen, cols]))
            total = acc[:, DH:]
            low_ref[rows, cols] = acc[:, :DH] / total
            lse_ref[rows, :] = jnp.where(lanes == head, top * c + jnp.log2(total), lse_ref[rows, :])
        for i in range(WIN // EDGE, q_ref.shape[0] // EDGE):
            rows = pl.ds(i * EDGE, EDGE)
            seen = pl.ds(i * EDGE - WIN, WIN + EDGE)
            s = dot_t(q_ref[rows, cols], k_ref[seen, cols])
            ends = jnp.where(lower, s[:, WIN:], s[:, :EDGE])
            mid = s[:, EDGE:WIN]
            top = jnp.maximum(
                jnp.max(ends, axis=1, keepdims=True), jnp.max(mid, axis=1, keepdims=True)
            )
            ends = jnp.exp2((ends - top) * c)
            mid = jnp.exp2((mid - top) * c).astype(BF)
            first = jnp.where(lower, 0.0, ends).astype(BF)
            last = jnp.where(lower, ends, 0.0).astype(BF)
            acc = dot(jnp.concatenate([first, mid, last], axis=1), with_ones(v_ref[seen, cols]))
            out_ref[rows, cols] = (acc[:, :DH] / acc[:, DH:]).astype(BF)


def own_attention(queries, keys, values, heads, scale):
    tokens, width = queries.shape
    return pl.pallas_call(
        functools.partial(own_kernel, scale, heads),
        out_shape=(
            jax.ShapeDtypeStruct((WIN, width), F32),
            jax.ShapeDtypeStruct((WIN, DH), F32),
            jax.ShapeDtypeStruct((tokens, width), BF),
        ),
        in_specs=[WHOLE] * 3,
        out_specs=(WHOLE,) * 3,
        compiler_params=params(),
        cost_estimate=cost(20),
        name="own_attention",
    )(queries, keys, values)


def edge_kernel(scale, q_heads, k_heads, v_heads, tail, q_ref, k_ref, v_ref, out_ref, lse_ref):
    lower = triangle()
    c = scale * LOG2E
    lanes = lax.broadcasted_iota(jnp.int32, (EDGE, DH), 1)
    count = len(q_heads)
    lse_ref[...] = jnp.zeros_like(lse_ref)
    for slot in range(count):
        q_cols = pl.ds(q_heads[slot] * DH, DH)
        k_cols = pl.ds(k_heads[slot] * DH, DH)
        v_cols = pl.ds(v_heads[slot] * DH, DH)
        for i in range(WIN // EDGE):
            rows = pl.ds(i * EDGE, EDGE)
            seen = pl.ds(tail + i * EDGE, WIN - i * EDGE)
            s = dot_t(q_ref[rows, q_cols], k_ref[seen, k_cols])
            edge = jnp.where(lower, NEG, s[:, :EDGE])
            if s.shape[1] > EDGE:
                s = jnp.concatenate([edge, s[:, EDGE:]], axis=1)
            else:
                s = edge
            top = jnp.max(s, axis=1, keepdims=True)
            p = jnp.exp2((s - top) * c).astype(BF)
            acc = dot(p, with_ones(v_ref[seen, v_cols]))
            total = acc[:, DH:]
            out_ref[rows, pl.ds(slot * DH, DH)] = (acc[:, :DH] / total).astype(BF)
            lse_ref[rows, :] = jnp.where(lanes == slot, top * c + jnp.log2(total), lse_ref[rows, :])
    stat = lse_ref[...]
    high = stat.astype(BF).astype(F32)
    mid = (stat - high).astype(BF).astype(F32)
    low = (stat - high - mid).astype(BF).astype(F32)
    packed = high + pltpu.roll(mid, count, 1) + pltpu.roll(low, 2 * count, 1)
    out_ref[:, pl.ds(count * DH, DH)] = packed.astype(BF)


def edge_attention(queries, keys, values, q_heads, k_heads, v_heads, tail, scale, micros, name):
    return pl.pallas_call(
        functools.partial(edge_kernel, scale, q_heads, k_heads, v_heads, tail),
        out_shape=jax.ShapeDtypeStruct((WIN, (len(q_heads) + 1) * DH), BF),
        in_specs=[WHOLE] * 3,
        out_specs=WHOLE,
        scratch_shapes=[pltpu.VMEM((WIN, DH), F32)],
        compiler_params=params(),
        cost_estimate=cost(micros),
        name=name,
    )(queries, keys, values)


def merge_kernel(heads, first_ref, low_ref, lse_ref, near_ref, far_ref, into_ref, out_ref):
    del into_ref
    for i in range(WIN // EDGE):
        rows = pl.ds(i * EDGE, EDGE)
        for head in range(heads):
            near = head < FORWARD
            ref, count, slot = (
                (near_ref, FORWARD, head) if near else (far_ref, heads - FORWARD, head - FORWARD)
            )
            stat = ref[rows, pl.ds(count * DH, DH)].astype(F32)
            other = (
                stat[:, slot : slot + 1]
                + stat[:, count + slot : count + slot + 1]
                + stat[:, 2 * count + slot : 2 * count + slot + 1]
            )
            other = jnp.where(first_ref[0] == 0, NEG, other)
            share = 1.0 / (1.0 + jnp.exp2(other - lse_ref[rows, head : head + 1]))
            cols = pl.ds(head * DH, DH)
            there = ref[rows, pl.ds(slot * DH, DH)].astype(F32)
            out_ref[rows, cols] = (low_ref[rows, cols] * share + there * (1.0 - share)).astype(BF)


def merge(first, low, lse, near, far, local, heads):
    width = low.shape[1]
    whole = lambda array: pl.BlockSpec(array.shape, lambda i: (0, 0))
    return pl.pallas_call(
        functools.partial(merge_kernel, heads),
        out_shape=pltpu.HBM(local.shape, BF),
        grid=(1,),
        in_specs=[SMALL, whole(low), whole(lse), whole(near), whole(far), ANY],
        out_specs=pl.BlockSpec((WIN, width), lambda i: (0, 0)),
        input_output_aliases={5: 0},
        compiler_params=params(),
        cost_estimate=cost(60),
        name="merge_local",
    )(first, low, lse, near, far, in_hbm(local))


def final_kernel(scale, heads, gate_ref, q_ref, kv_ref, local_ref, out_ref):
    c = scale * LOG2E
    pieces = MB // PIECE
    for head in range(heads):
        cols = pl.ds(head * DH, DH)
        mine = pl.ds(head * TOPK, TOPK)
        keys = kv_ref[0:pieces, mine].astype(F32).reshape(TOPK * MB, DH).astype(BF)
        values = kv_ref[pieces : 2 * pieces, mine].astype(F32).reshape(TOPK * MB, DH).astype(BF)
        s = dot_t(q_ref[:, cols], keys)
        top = jnp.max(s, axis=1, keepdims=True)
        p = jnp.exp2((s - top) * c).astype(BF)
        acc = dot(p, with_ones(values))
        gate = gate_ref[head]
        remote = acc[:, :DH] * (gate / acc[:, DH:])
        local = local_ref[:, cols].astype(F32)
        out_ref[:, cols] = (remote + (1.0 - gate) * local).astype(BF)


def final_attention(gate, queries, kv, local, heads, scale):
    tokens, width = queries.shape
    rows = 256
    per = QB // rows
    band = pl.BlockSpec((rows, width), lambda i, *_: (i, 0))
    return pl.pallas_call(
        functools.partial(final_kernel, scale, heads),
        out_shape=jax.ShapeDtypeStruct(queries.shape, BF),
        grid_spec=pltpu.PrefetchScalarGridSpec(
            num_scalar_prefetch=1,
            grid=(tokens // rows,),
            in_specs=[
                band,
                pl.BlockSpec((kv.shape[0], heads * TOPK, PIECE, DH), lambda i, *_: (0, i // per, 0, 0)),
                band,
            ],
            out_specs=band,
        ),
        compiler_params=params(),
        cost_estimate=cost(7),
        name="final_attention",
    )(gate, queries, kv, local)


def body(queries, token_keys, token_values, mem_keys, mem_values, retrieved, gate_bias):
    tokens = queries.shape[0]
    heads = gate_bias.shape[0]
    scale = DH ** (-0.5)
    devices = lax.axis_size("seq")
    blocks = mem_keys.shape[0] // MB
    q_blocks = tokens // QB
    wanted = q_blocks * heads * TOPK
    far_heads = list(range(FORWARD, heads))
    near_heads = list(range(FORWARD))
    upward = [(i, i + 1) for i in range(devices - 1)]
    downward = [(i, i - 1) for i in range(1, devices)]
    back_q, ahead_kv = edges(queries, token_keys, token_values)
    far_q = lax.ppermute(back_q, "seq", downward)
    near_kv = lax.ppermute(ahead_kv, "seq", upward)
    ids = retrieved.reshape(-1)
    ids_tile = jnp.zeros((PIECE * DH,), BF).at[:wanted].set(ids.astype(BF)).reshape(PIECE, DH)
    ids_tile, _ = lax.optimization_barrier((ids_tile, back_q))
    sent = pack(mem_keys, mem_values, ids_tile, blocks, heads)
    store = lax.all_to_all(sent, "seq", split_axis=0, concat_axis=0, tiled=True)
    gate_share = 1.0 / (1.0 + jnp.exp(-gate_bias))
    first = lax.axis_index("seq").reshape(1).astype(jnp.int32)
    low, lse, local = own_attention(queries, token_keys, token_values, heads, scale)
    far_part = edge_attention(
        far_q,
        token_keys,
        token_values,
        list(range(len(far_heads))),
        far_heads,
        far_heads,
        tokens - WIN,
        scale,
        60,
        "far_attention",
    )
    store, low, lse, local, far_part = lax.optimization_barrier((store, low, lse, local, far_part))
    far = lax.ppermute(far_part, "seq", upward)
    all_ids = store[:, blocks * heads, 0, :wanted].astype(jnp.int32)
    stride = blocks * heads + 1
    request_head = jnp.arange(wanted, dtype=jnp.int32) // TOPK % heads
    rows = (all_ids // blocks) * stride + (all_ids % blocks) * heads + request_head[None, :]
    pieces = gather(rows.reshape(-1), store.reshape(devices * stride, PIECE, DH), devices, wanted)
    pieces, late_q = lax.optimization_barrier((pieces, queries))
    kv = lax.all_to_all(pieces, "seq", split_axis=0, concat_axis=0, tiled=True)
    near = edge_attention(
        late_q,
        near_kv,
        near_kv,
        near_heads,
        near_heads,
        [FORWARD + head for head in near_heads],
        0,
        scale,
        5,
        "near_attention",
    )
    local = merge(first, low, lse, near, far, local, heads)
    kv, local = lax.optimization_barrier((kv, local))
    return final_attention(gate_share, in_hbm(queries), in_hbm(kv), in_hbm(local), heads, scale)


def solution(mesh):
    in_specs = (
        P("seq", "head"),
        P("seq", "head"),
        P("seq", "head"),
        P("seq", "head"),
        P("seq", "head"),
        P("seq", "head", None),
        P("head"),
    )
    return jax.shard_map(
        body, mesh=mesh, in_specs=in_specs, out_specs=P("seq", "head"), check_vma=False
    )
```

```python
import functools

import jax
import jax.numpy as jnp
from jax import lax
from jax.experimental import pallas as pl
from jax.experimental.pallas import tpu as pltpu
from jax.sharding import PartitionSpec as P

QB = 512
MB = 128
TOPK = 2
WIN = 512
DH = 128
PIECE = 8
EDGE = 256
FORWARD = 5
LOG2E = 1.4426950408889634
NEG = -1e30
VMEM_LIMIT = 24 << 20
BF = jnp.bfloat16
F32 = jnp.float32
ANY = pl.BlockSpec(memory_space=pl.ANY)
WHOLE = pl.BlockSpec(memory_space=pltpu.VMEM)
SMALL = pl.BlockSpec(memory_space=pltpu.SMEM)


def params():
    return pltpu.CompilerParams(vmem_limit_bytes=VMEM_LIMIT)


def cost(micros):
    return pl.CostEstimate(flops=int(micros * 1e9), transcendentals=0, bytes_accessed=0)


def in_hbm(array):
    return pltpu.with_memory_space_constraint(array, pltpu.HBM)


def copy_all(copies):
    for copy in copies:
        copy.start()
    for copy in copies:
        copy.wait()


def edges_kernel(q_ref, k_ref, v_ref, back_ref, ahead_ref, sems):
    split = FORWARD * DH
    tail = pl.ds(k_ref.shape[0] - WIN, WIN)
    width = q_ref.shape[1] - split
    copy_all(
        [
            pltpu.make_async_copy(
                q_ref.at[pl.ds(0, WIN), pl.ds(split, width)], back_ref, sems.at[0]
            ),
            pltpu.make_async_copy(
                k_ref.at[tail, pl.ds(0, split)], ahead_ref.at[:, pl.ds(0, split)], sems.at[1]
            ),
            pltpu.make_async_copy(
                v_ref.at[tail, pl.ds(0, split)], ahead_ref.at[:, pl.ds(split, split)], sems.at[2]
            ),
        ]
    )


def edges(queries, keys, values):
    split = FORWARD * DH
    return pl.pallas_call(
        edges_kernel,
        out_shape=(
            jax.ShapeDtypeStruct((WIN, queries.shape[1] - split), BF),
            jax.ShapeDtypeStruct((WIN, 2 * split), BF),
        ),
        in_specs=[ANY] * 3,
        out_specs=(WHOLE, WHOLE),
        scratch_shapes=[pltpu.SemaphoreType.DMA((3,))],
        compiler_params=params(),
        cost_estimate=cost(2),
        name="cut_edges",
    )(in_hbm(queries), in_hbm(keys), in_hbm(values))


def pack_kernel(blocks, heads, keys_ref, values_ref, ids_ref, out_ref, stage, in_sems, out_sems):
    pieces = MB // PIECE
    loads, stores = [], []
    for half, source in enumerate((keys_ref, values_ref)):
        for block in range(blocks):
            slot = len(loads)
            here = stage.at[pl.ds(slot * pieces, pieces)]
            there = out_ref.at[pl.ds(half * pieces, pieces), pl.ds(block * heads, heads)]
            rows = pl.ds(block * pieces, pieces)
            loads.append(pltpu.make_async_copy(source.at[rows], here, in_sems.at[slot]))
            stores.append(pltpu.make_async_copy(here, there, out_sems.at[slot]))
    ids_store = pltpu.make_async_copy(
        ids_ref, out_ref.at[:, pl.ds(blocks * heads, 1)], out_sems.at[2 * blocks]
    )
    for load in loads:
        load.start()
    ids_store.start()
    for load, store in zip(loads, stores):
        load.wait()
        store.start()
    for store in stores:
        store.wait()
    ids_store.wait()


def tiles(array):
    rows, width = array.shape
    return array.reshape(rows // PIECE, PIECE, width // DH, DH).transpose(0, 2, 1, 3)


def pack(mem_keys, mem_values, ids_tile, blocks, heads):
    devices = 2 * MB // PIECE
    return pl.pallas_call(
        functools.partial(pack_kernel, blocks, heads),
        out_shape=pltpu.HBM((devices, blocks * heads + 1, PIECE, DH), BF),
        in_specs=[ANY, ANY, WHOLE],
        out_specs=ANY,
        scratch_shapes=[
            pltpu.VMEM((2 * blocks * MB // PIECE, heads, PIECE, DH), BF),
            pltpu.SemaphoreType.DMA((2 * blocks,)),
            pltpu.SemaphoreType.DMA((2 * blocks + 1,)),
        ],
        compiler_params=params(),
        cost_estimate=cost(2),
        name="pack_pieces",
    )(
        in_hbm(tiles(mem_keys)),
        in_hbm(tiles(mem_values)),
        jnp.broadcast_to(ids_tile, (devices, 1, PIECE, DH)),
    )


def gather_kernel(wanted, group, rows_ref, store_ref, out_ref):
    first = pl.program_id(0) * group

    @pl.loop(0, group)
    def _(device):
        base = (first + device) * wanted
        for request in range(wanted):
            out_ref[device, request] = store_ref[rows_ref[base + request]]


def gather(rows, store, devices, wanted):
    group = 4
    return pl.pallas_call(
        functools.partial(gather_kernel, wanted, group),
        out_shape=pltpu.HBM((devices, wanted, PIECE, DH), BF),
        grid_spec=pltpu.PrefetchScalarGridSpec(
            num_scalar_prefetch=1,
            grid=(devices // group,),
            in_specs=[pl.BlockSpec(store.shape, lambda i, rows: (0, 0, 0))],
            out_specs=pl.BlockSpec((group, wanted, PIECE, DH), lambda i, rows: (i, 0, 0, 0)),
        ),
        compiler_params=params(),
        cost_estimate=cost(6),
        name="gather_pieces",
    )(rows, store)


def dot_t(a, b):
    return lax.dot_general(a, b, (((1,), (1,)), ((), ())), preferred_element_type=F32)


def dot(a, b):
    return jnp.dot(a, b, preferred_element_type=F32)


def with_ones(values):
    return jnp.concatenate([values, jnp.ones_like(values)], axis=1)


def triangle():
    row = lax.broadcasted_iota(jnp.int32, (EDGE, EDGE), 0)
    col = lax.broadcasted_iota(jnp.int32, (EDGE, EDGE), 1)
    return col <= row


def own_kernel(scale, heads, q_ref, k_ref, v_ref, low_ref, lse_ref, out_ref):
    lower = triangle()
    c = scale * LOG2E
    lanes = lax.broadcasted_iota(jnp.int32, (EDGE, DH), 1)
    for head in range(heads):
        cols = pl.ds(head * DH, DH)
        for i in range(WIN // EDGE):
            rows = pl.ds(i * EDGE, EDGE)
            seen = pl.ds(0, (i + 1) * EDGE)
            s = dot_t(q_ref[rows, cols], k_ref[seen, cols])
            diag = jnp.where(lower, s[:, i * EDGE :], NEG)
            if i:
                s = jnp.concatenate([s[:, : i * EDGE], diag], axis=1)
            else:
                s = diag
            top = jnp.max(s, axis=1, keepdims=True)
            p = jnp.exp2((s - top) * c).astype(BF)
            acc = dot(p, with_ones(v_ref[seen, cols]))
            total = acc[:, DH:]
            low_ref[rows, cols] = acc[:, :DH] / total
            lse_ref[rows, :] = jnp.where(lanes == head, top * c + jnp.log2(total), lse_ref[rows, :])
        for i in range(WIN // EDGE, q_ref.shape[0] // EDGE):
            rows = pl.ds(i * EDGE, EDGE)
            seen = pl.ds(i * EDGE - WIN, WIN + EDGE)
            s = dot_t(q_ref[rows, cols], k_ref[seen, cols])
            ends = jnp.where(lower, s[:, WIN:], s[:, :EDGE])
            mid = s[:, EDGE:WIN]
            top = jnp.maximum(
                jnp.max(ends, axis=1, keepdims=True), jnp.max(mid, axis=1, keepdims=True)
            )
            ends = jnp.exp2((ends - top) * c)
            mid = jnp.exp2((mid - top) * c).astype(BF)
            first = jnp.where(lower, 0.0, ends).astype(BF)
            last = jnp.where(lower, ends, 0.0).astype(BF)
            acc = dot(jnp.concatenate([first, mid, last], axis=1), with_ones(v_ref[seen, cols]))
            out_ref[rows, cols] = (acc[:, :DH] / acc[:, DH:]).astype(BF)


def own_attention(queries, keys, values, heads, scale):
    tokens, width = queries.shape
    return pl.pallas_call(
        functools.partial(own_kernel, scale, heads),
        out_shape=(
            jax.ShapeDtypeStruct((WIN, width), F32),
            jax.ShapeDtypeStruct((WIN, DH), F32),
            jax.ShapeDtypeStruct((tokens, width), BF),
        ),
        in_specs=[WHOLE] * 3,
        out_specs=(WHOLE,) * 3,
        compiler_params=params(),
        cost_estimate=cost(20),
        name="own_attention",
    )(queries, keys, values)


def edge_kernel(scale, q_heads, k_heads, v_heads, tail, q_ref, k_ref, v_ref, out_ref, lse_ref):
    lower = triangle()
    c = scale * LOG2E
    lanes = lax.broadcasted_iota(jnp.int32, (EDGE, DH), 1)
    count = len(q_heads)
    lse_ref[...] = jnp.zeros_like(lse_ref)
    for slot in range(count):
        q_cols = pl.ds(q_heads[slot] * DH, DH)
        k_cols = pl.ds(k_heads[slot] * DH, DH)
        v_cols = pl.ds(v_heads[slot] * DH, DH)
        for i in range(WIN // EDGE):
            rows = pl.ds(i * EDGE, EDGE)
            seen = pl.ds(tail + i * EDGE, WIN - i * EDGE)
            s = dot_t(q_ref[rows, q_cols], k_ref[seen, k_cols])
            edge = jnp.where(lower, NEG, s[:, :EDGE])
            if s.shape[1] > EDGE:
                s = jnp.concatenate([edge, s[:, EDGE:]], axis=1)
            else:
                s = edge
            top = jnp.max(s, axis=1, keepdims=True)
            p = jnp.exp2((s - top) * c).astype(BF)
            acc = dot(p, with_ones(v_ref[seen, v_cols]))
            total = acc[:, DH:]
            out_ref[rows, pl.ds(slot * DH, DH)] = (acc[:, :DH] / total).astype(BF)
            lse_ref[rows, :] = jnp.where(lanes == slot, top * c + jnp.log2(total), lse_ref[rows, :])
    stat = lse_ref[...]
    high = stat.astype(BF).astype(F32)
    mid = (stat - high).astype(BF).astype(F32)
    low = (stat - high - mid).astype(BF).astype(F32)
    packed = high + pltpu.roll(mid, count, 1) + pltpu.roll(low, 2 * count, 1)
    out_ref[:, pl.ds(count * DH, DH)] = packed.astype(BF)


def edge_attention(queries, keys, values, q_heads, k_heads, v_heads, tail, scale, micros, name):
    return pl.pallas_call(
        functools.partial(edge_kernel, scale, q_heads, k_heads, v_heads, tail),
        out_shape=jax.ShapeDtypeStruct((WIN, (len(q_heads) + 1) * DH), BF),
        in_specs=[WHOLE] * 3,
        out_specs=WHOLE,
        scratch_shapes=[pltpu.VMEM((WIN, DH), F32)],
        compiler_params=params(),
        cost_estimate=cost(micros),
        name=name,
    )(queries, keys, values)


def unpacked(stat, count):
    return stat + pltpu.roll(stat, DH - count, 1) + pltpu.roll(stat, DH - 2 * count, 1)


def merge_kernel(heads, first_ref, low_ref, lse_ref, near_ref, far_ref, into_ref, out_ref):
    del into_ref
    lanes = lax.broadcasted_iota(jnp.int32, (EDGE, DH), 1)
    behind = heads - FORWARD
    for i in range(WIN // EDGE):
        rows = pl.ds(i * EDGE, EDGE)
        near_stat = unpacked(near_ref[rows, pl.ds(FORWARD * DH, DH)].astype(F32), FORWARD)
        far_stat = unpacked(far_ref[rows, pl.ds(behind * DH, DH)].astype(F32), behind)
        other = jnp.where(lanes < FORWARD, near_stat, pltpu.roll(far_stat, FORWARD, 1))
        other = jnp.where(first_ref[0] == 0, NEG, other)
        own = jnp.where(lanes < heads, lse_ref[rows, :], 0.0)
        shares = 1.0 / (1.0 + jnp.exp2(other - own))
        for head in range(heads):
            ref, slot = (near_ref, head) if head < FORWARD else (far_ref, head - FORWARD)
            share = shares[:, head : head + 1]
            cols = pl.ds(head * DH, DH)
            mine = low_ref[rows, cols]
            there = ref[rows, pl.ds(slot * DH, DH)].astype(F32)
            out_ref[rows, cols] = (there + (mine - there) * share).astype(BF)


def merge(first, low, lse, near, far, local, heads):
    width = low.shape[1]
    whole = lambda array: pl.BlockSpec(array.shape, lambda i: (0, 0))
    return pl.pallas_call(
        functools.partial(merge_kernel, heads),
        out_shape=pltpu.HBM(local.shape, BF),
        grid=(1,),
        in_specs=[SMALL, whole(low), whole(lse), whole(near), whole(far), ANY],
        out_specs=pl.BlockSpec((WIN, width), lambda i: (0, 0)),
        input_output_aliases={5: 0},
        compiler_params=params(),
        cost_estimate=cost(60),
        name="merge_local",
    )(first, low, lse, near, far, in_hbm(local))


def final_kernel(scale, heads, gate_ref, q_ref, kv_ref, local_ref, out_ref):
    c = scale * LOG2E
    pieces = MB // PIECE
    for head in range(heads):
        cols = pl.ds(head * DH, DH)
        mine = pl.ds(head * TOPK, TOPK)
        keys = kv_ref[0:pieces, mine].astype(F32).reshape(TOPK * MB, DH).astype(BF)
        values = kv_ref[pieces : 2 * pieces, mine].astype(F32).reshape(TOPK * MB, DH).astype(BF)
        s = dot_t(q_ref[:, cols], keys)
        top = jnp.max(s, axis=1, keepdims=True)
        p = jnp.exp2((s - top) * c).astype(BF)
        acc = dot(p, with_ones(values))
        gate = gate_ref[head]
        remote = acc[:, :DH] * (gate / acc[:, DH:])
        local = local_ref[:, cols].astype(F32)
        out_ref[:, cols] = (remote + (1.0 - gate) * local).astype(BF)


def final_attention(gate, queries, kv, local, heads, scale):
    tokens, width = queries.shape
    rows = 256
    per = QB // rows
    band = pl.BlockSpec((rows, width), lambda i, *_: (i, 0))
    return pl.pallas_call(
        functools.partial(final_kernel, scale, heads),
        out_shape=jax.ShapeDtypeStruct(queries.shape, BF),
        grid_spec=pltpu.PrefetchScalarGridSpec(
            num_scalar_prefetch=1,
            grid=(tokens // rows,),
            in_specs=[
                band,
                pl.BlockSpec((kv.shape[0], heads * TOPK, PIECE, DH), lambda i, *_: (0, i // per, 0, 0)),
                band,
            ],
            out_specs=band,
        ),
        compiler_params=params(),
        cost_estimate=cost(7),
        name="final_attention",
    )(gate, queries, kv, local)


def body(queries, token_keys, token_values, mem_keys, mem_values, retrieved, gate_bias):
    tokens = queries.shape[0]
    heads = gate_bias.shape[0]
    scale = DH ** (-0.5)
    devices = lax.axis_size("seq")
    blocks = mem_keys.shape[0] // MB
    q_blocks = tokens // QB
    wanted = q_blocks * heads * TOPK
    far_heads = list(range(FORWARD, heads))
    near_heads = list(range(FORWARD))
    upward = [(i, i + 1) for i in range(devices - 1)]
    downward = [(i, i - 1) for i in range(1, devices)]
    back_q, ahead_kv = edges(queries, token_keys, token_values)
    far_q = lax.ppermute(back_q, "seq", downward)
    near_kv = lax.ppermute(ahead_kv, "seq", upward)
    ids = retrieved.reshape(-1)
    ids_tile = jnp.zeros((PIECE * DH,), BF).at[:wanted].set(ids.astype(BF)).reshape(PIECE, DH)
    ids_tile, _ = lax.optimization_barrier((ids_tile, back_q))
    sent = pack(mem_keys, mem_values, ids_tile, blocks, heads)
    store = lax.all_to_all(sent, "seq", split_axis=0, concat_axis=0, tiled=True)
    gate_share = 1.0 / (1.0 + jnp.exp(-gate_bias))
    first = lax.axis_index("seq").reshape(1).astype(jnp.int32)
    low, lse, local = own_attention(queries, token_keys, token_values, heads, scale)
    far_part = edge_attention(
        far_q,
        token_keys,
        token_values,
        list(range(len(far_heads))),
        far_heads,
        far_heads,
        tokens - WIN,
        scale,
        60,
        "far_attention",
    )
    near = edge_attention(
        queries,
        near_kv,
        near_kv,
        near_heads,
        near_heads,
        [FORWARD + head for head in near_heads],
        0,
        scale,
        60,
        "near_attention",
    )
    store, low, lse, local, far_part, near = lax.optimization_barrier(
        (store, low, lse, local, far_part, near)
    )
    far = lax.ppermute(far_part, "seq", upward)
    all_ids = store[:, blocks * heads, 0, :wanted].astype(jnp.int32)
    stride = blocks * heads + 1
    request_head = jnp.arange(wanted, dtype=jnp.int32) // TOPK % heads
    rows = (all_ids // blocks) * stride + (all_ids % blocks) * heads + request_head[None, :]
    pieces = gather(rows.reshape(-1), store.reshape(devices * stride, PIECE, DH), devices, wanted)
    kv = lax.all_to_all(pieces, "seq", split_axis=0, concat_axis=0, tiled=True)
    local = merge(first, low, lse, near, far, local, heads)
    kv, local = lax.optimization_barrier((kv, local))
    return final_attention(gate_share, in_hbm(queries), in_hbm(kv), in_hbm(local), heads, scale)


def solution(mesh):
    in_specs = (
        P("seq", "head"),
        P("seq", "head"),
        P("seq", "head"),
        P("seq", "head"),
        P("seq", "head"),
        P("seq", "head", None),
        P("head"),
    )
    return jax.shard_map(
        body, mesh=mesh, in_specs=in_specs, out_specs=P("seq", "head"), check_vma=False
    )
```

```python
import functools

import jax
import jax.numpy as jnp
from jax import lax
from jax.experimental import pallas as pl
from jax.experimental.pallas import tpu as pltpu
from jax.sharding import PartitionSpec as P

QB = 512
MB = 128
TOPK = 2
WIN = 512
DH = 128
PIECE = 8
EDGE = 256
FORWARD = 5
HALVES = 2
LOG2E = 1.4426950408889634
NEG = -1e30
VMEM_LIMIT = 40 << 20
BF = jnp.bfloat16
F32 = jnp.float32
ANY = pl.BlockSpec(memory_space=pl.ANY)
WHOLE = pl.BlockSpec(memory_space=pltpu.VMEM)
SMALL = pl.BlockSpec(memory_space=pltpu.SMEM)


def params():
    return pltpu.CompilerParams(vmem_limit_bytes=VMEM_LIMIT)


def cost(micros):
    return pl.CostEstimate(flops=int(micros * 1e9), transcendentals=0, bytes_accessed=0)


def in_hbm(array):
    return pltpu.with_memory_space_constraint(array, pltpu.HBM)


def copy_all(copies):
    for copy in copies:
        copy.start()
    for copy in copies:
        copy.wait()


def edges_kernel(q_ref, k_ref, v_ref, back_ref, ahead_ref, sems):
    split = FORWARD * DH
    tail = pl.ds(k_ref.shape[0] - WIN, WIN)
    width = q_ref.shape[1] - split
    copy_all(
        [
            pltpu.make_async_copy(
                q_ref.at[pl.ds(0, WIN), pl.ds(split, width)], back_ref, sems.at[0]
            ),
            pltpu.make_async_copy(
                k_ref.at[tail, pl.ds(0, split)], ahead_ref.at[:, pl.ds(0, split)], sems.at[1]
            ),
            pltpu.make_async_copy(
                v_ref.at[tail, pl.ds(0, split)], ahead_ref.at[:, pl.ds(split, split)], sems.at[2]
            ),
        ]
    )


def edges(queries, keys, values):
    split = FORWARD * DH
    return pl.pallas_call(
        edges_kernel,
        out_shape=(
            jax.ShapeDtypeStruct((WIN, queries.shape[1] - split), BF),
            jax.ShapeDtypeStruct((WIN, 2 * split), BF),
        ),
        in_specs=[ANY] * 3,
        out_specs=(WHOLE, WHOLE),
        scratch_shapes=[pltpu.SemaphoreType.DMA((3,))],
        compiler_params=params(),
        cost_estimate=cost(2),
        name="cut_edges",
    )(in_hbm(queries), in_hbm(keys), in_hbm(values))


def pack_kernel(blocks, heads, keys_ref, values_ref, ids_ref, out_ref, stage, in_sems, out_sems):
    pieces = MB // PIECE
    loads, stores = [], []
    for half, source in enumerate((keys_ref, values_ref)):
        for block in range(blocks):
            slot = len(loads)
            here = stage.at[pl.ds(slot * pieces, pieces)]
            there = out_ref.at[pl.ds(half * pieces, pieces), pl.ds(block * heads, heads)]
            rows = pl.ds(block * pieces, pieces)
            loads.append(pltpu.make_async_copy(source.at[rows], here, in_sems.at[slot]))
            stores.append(pltpu.make_async_copy(here, there, out_sems.at[slot]))
    ids_store = pltpu.make_async_copy(
        ids_ref, out_ref.at[:, pl.ds(blocks * heads, 1)], out_sems.at[2 * blocks]
    )
    for load in loads:
        load.start()
    ids_store.start()
    for load, store in zip(loads, stores):
        load.wait()
        store.start()
    for store in stores:
        store.wait()
    ids_store.wait()


def tiles(array):
    rows, width = array.shape
    return array.reshape(rows // PIECE, PIECE, width // DH, DH).transpose(0, 2, 1, 3)


def pack(mem_keys, mem_values, ids_tile, blocks, heads):
    devices = 2 * MB // PIECE
    return pl.pallas_call(
        functools.partial(pack_kernel, blocks, heads),
        out_shape=pltpu.HBM((devices, blocks * heads + 1, PIECE, DH), BF),
        in_specs=[ANY, ANY, WHOLE],
        out_specs=ANY,
        scratch_shapes=[
            pltpu.VMEM((2 * blocks * MB // PIECE, heads, PIECE, DH), BF),
            pltpu.SemaphoreType.DMA((2 * blocks,)),
            pltpu.SemaphoreType.DMA((2 * blocks + 1,)),
        ],
        compiler_params=params(),
        cost_estimate=cost(2),
        name="pack_pieces",
    )(
        in_hbm(tiles(mem_keys)),
        in_hbm(tiles(mem_values)),
        jnp.broadcast_to(ids_tile, (devices, 1, PIECE, DH)),
    )


def gather_kernel(
    blocks, heads, wanted, store_ref, out_ref, ids, rows_v, rows_s, store, stage, ids_sem, sems, out_sems
):
    devices, stride = store_ref.shape[:2]
    parts = sems.shape[0]
    groups = out_sems.shape[0]
    size = devices // groups
    ids_load = pltpu.make_async_copy(store_ref.at[:, stride - 1], ids, ids_sem.at[0])
    ids_load.start()
    loads, stores = [], []
    for part in range(parts):
        span = pl.ds(part * (devices // parts), devices // parts)
        loads.append(pltpu.make_async_copy(store_ref.at[span], store.at[span], sems.at[part]))
    for group in range(groups):
        span = pl.ds(group * size, size)
        stores.append(pltpu.make_async_copy(stage.at[span], out_ref.at[span], out_sems.at[group]))
    for load in loads:
        load.start()
    ids_load.wait()
    row = lax.broadcasted_iota(jnp.int32, (devices, PIECE, DH), 1)
    block = jnp.sum(jnp.where(row == 0, ids[...].astype(F32), 0.0), axis=1).astype(jnp.int32)
    lane = lax.broadcasted_iota(jnp.int32, (devices, DH), 1)
    head = lane // TOPK % heads
    rows_v[...] = block // blocks * stride + block % blocks * heads + head
    rows_copy = pltpu.make_async_copy(rows_v, rows_s, ids_sem.at[1])
    rows_copy.start()
    rows_copy.wait()
    for load in loads:
        load.wait()
    flat = store.reshape(devices * stride, PIECE, DH)
    for group in range(groups):

        @pl.loop(group * size, (group + 1) * size)
        def _(device):
            for request in range(wanted):
                stage[device, request] = flat[rows_s[device, request]]

        stores[group].start()
    for store_copy in stores:
        store_copy.wait()


def gather(store, blocks, heads, wanted):
    devices = store.shape[0]
    return pl.pallas_call(
        functools.partial(gather_kernel, blocks, heads, wanted),
        out_shape=pltpu.HBM((devices, wanted, PIECE, DH), BF),
        in_specs=[ANY],
        out_specs=ANY,
        scratch_shapes=[
            pltpu.VMEM((devices, PIECE, DH), BF),
            pltpu.VMEM((devices, DH), jnp.int32),
            pltpu.SMEM((devices, DH), jnp.int32),
            pltpu.VMEM(store.shape, BF),
            pltpu.VMEM((devices, wanted, PIECE, DH), BF),
            pltpu.SemaphoreType.DMA((2,)),
            pltpu.SemaphoreType.DMA((4,)),
            pltpu.SemaphoreType.DMA((8,)),
        ],
        compiler_params=params(),
        cost_estimate=cost(6),
        name="gather_pieces",
    )(in_hbm(store))


def dot_t(a, b):
    return lax.dot_general(a, b, (((1,), (1,)), ((), ())), preferred_element_type=F32)


def dot(a, b):
    return jnp.dot(a, b, preferred_element_type=F32)


def with_ones(values):
    return jnp.concatenate([values, jnp.ones_like(values)], axis=1)


def triangle():
    row = lax.broadcasted_iota(jnp.int32, (EDGE, EDGE), 0)
    col = lax.broadcasted_iota(jnp.int32, (EDGE, EDGE), 1)
    return col <= row


def own_kernel(scale, heads, q_ref, k_ref, v_ref, low_ref, lse_ref, out_ref):
    lower = triangle()
    c = scale * LOG2E
    lanes = lax.broadcasted_iota(jnp.int32, (EDGE, DH), 1)
    for head in range(heads):
        cols = pl.ds(head * DH, DH)
        for i in range(WIN // EDGE):
            rows = pl.ds(i * EDGE, EDGE)
            seen = pl.ds(0, (i + 1) * EDGE)
            s = dot_t(q_ref[rows, cols], k_ref[seen, cols])
            diag = jnp.where(lower, s[:, i * EDGE :], NEG)
            if i:
                s = jnp.concatenate([s[:, : i * EDGE], diag], axis=1)
            else:
                s = diag
            top = jnp.max(s, axis=1, keepdims=True)
            p = jnp.exp2((s - top) * c).astype(BF)
            acc = dot(p, with_ones(v_ref[seen, cols]))
            total = acc[:, DH:]
            low_ref[rows, cols] = acc[:, :DH] / total
            lse_ref[rows, :] = jnp.where(lanes == head, top * c + jnp.log2(total), lse_ref[rows, :])
        for i in range(WIN // EDGE, q_ref.shape[0] // EDGE):
            rows = pl.ds(i * EDGE, EDGE)
            seen = pl.ds(i * EDGE - WIN, WIN + EDGE)
            s = dot_t(q_ref[rows, cols], k_ref[seen, cols])
            ends = jnp.where(lower, s[:, WIN:], s[:, :EDGE])
            mid = s[:, EDGE:WIN]
            top = jnp.maximum(
                jnp.max(ends, axis=1, keepdims=True), jnp.max(mid, axis=1, keepdims=True)
            )
            ends = jnp.exp2((ends - top) * c)
            mid = jnp.exp2((mid - top) * c).astype(BF)
            first = jnp.where(lower, 0.0, ends).astype(BF)
            last = jnp.where(lower, ends, 0.0).astype(BF)
            acc = dot(jnp.concatenate([first, mid, last], axis=1), with_ones(v_ref[seen, cols]))
            out_ref[rows, cols] = (acc[:, :DH] / acc[:, DH:]).astype(BF)


def own_attention(queries, keys, values, heads, scale):
    tokens, width = queries.shape
    return pl.pallas_call(
        functools.partial(own_kernel, scale, heads),
        out_shape=(
            jax.ShapeDtypeStruct((WIN, width), F32),
            jax.ShapeDtypeStruct((WIN, DH), F32),
            jax.ShapeDtypeStruct((tokens, width), BF),
        ),
        in_specs=[WHOLE] * 3,
        out_specs=(WHOLE,) * 3,
        compiler_params=params(),
        cost_estimate=cost(1),
        name="own_attention",
    )(queries, keys, values)


def edge_part(scale, slots, tail, q_ref, k_ref, v_ref, out_ref, lse_ref):
    lower = triangle()
    c = scale * LOG2E
    lanes = lax.broadcasted_iota(jnp.int32, (EDGE, DH), 1)
    count = len(slots)
    lse_ref[...] = jnp.zeros_like(lse_ref)
    for slot, (q_head, k_head, v_head) in enumerate(slots):
        q_cols = pl.ds(q_head * DH, DH)
        k_cols = pl.ds(k_head * DH, DH)
        v_cols = pl.ds(v_head * DH, DH)
        for i in range(WIN // EDGE):
            rows = pl.ds(i * EDGE, EDGE)
            seen = pl.ds(tail + i * EDGE, WIN - i * EDGE)
            s = dot_t(q_ref[rows, q_cols], k_ref[seen, k_cols])
            edge = jnp.where(lower, NEG, s[:, :EDGE])
            if s.shape[1] > EDGE:
                s = jnp.concatenate([edge, s[:, EDGE:]], axis=1)
            else:
                s = edge
            top = jnp.max(s, axis=1, keepdims=True)
            p = jnp.exp2((s - top) * c).astype(BF)
            acc = dot(p, with_ones(v_ref[seen, v_cols]))
            total = acc[:, DH:]
            out_ref[rows, pl.ds(slot * DH, DH)] = (acc[:, :DH] / total).astype(BF)
            lse_ref[rows, :] = jnp.where(lanes == slot, top * c + jnp.log2(total), lse_ref[rows, :])
    stat = lse_ref[...]
    high = stat.astype(BF).astype(F32)
    mid = (stat - high).astype(BF).astype(F32)
    low = (stat - high - mid).astype(BF).astype(F32)
    packed = high + pltpu.roll(mid, count, 1) + pltpu.roll(low, 2 * count, 1)
    out_ref[:, pl.ds(count * DH, DH)] = packed.astype(BF)


def edge_kernel(
    scale, heads, far_q_ref, near_kv_ref, q_ref, k_ref, v_ref, far_ref, near_ref, lse_ref
):
    far = [(head - FORWARD, head, head) for head in range(FORWARD, heads)]
    near = [(head, head, FORWARD + head) for head in range(FORWARD)]
    tail = k_ref.shape[0] - WIN
    edge_part(scale, far, tail, far_q_ref, k_ref, v_ref, far_ref, lse_ref)
    edge_part(scale, near, 0, q_ref, near_kv_ref, near_kv_ref, near_ref, lse_ref)


def edge_attention(far_q, near_kv, queries, keys, values, heads, scale):
    return pl.pallas_call(
        functools.partial(edge_kernel, scale, heads),
        out_shape=(
            jax.ShapeDtypeStruct((WIN, (heads - FORWARD + 1) * DH), BF),
            jax.ShapeDtypeStruct((WIN, (FORWARD + 1) * DH), BF),
        ),
        in_specs=[WHOLE] * 5,
        out_specs=(WHOLE,) * 2,
        scratch_shapes=[pltpu.VMEM((WIN, DH), F32)],
        compiler_params=params(),
        cost_estimate=cost(60),
        name="edge_attention",
    )(far_q, near_kv, queries, keys, values)


def unpacked(stat, count):
    return stat + pltpu.roll(stat, DH - count, 1) + pltpu.roll(stat, DH - 2 * count, 1)


def merge_kernel(heads, first_ref, low_ref, lse_ref, near_ref, far_ref, into_ref, out_ref):
    del into_ref
    lanes = lax.broadcasted_iota(jnp.int32, (EDGE, DH), 1)
    behind = heads - FORWARD
    for i in range(WIN // EDGE):
        rows = pl.ds(i * EDGE, EDGE)
        near_stat = unpacked(near_ref[rows, pl.ds(FORWARD * DH, DH)].astype(F32), FORWARD)
        far_stat = unpacked(far_ref[rows, pl.ds(behind * DH, DH)].astype(F32), behind)
        other = jnp.where(lanes < FORWARD, near_stat, pltpu.roll(far_stat, FORWARD, 1))
        other = jnp.where(first_ref[0] == 0, NEG, other)
        own = jnp.where(lanes < heads, lse_ref[rows, :], 0.0)
        shares = 1.0 / (1.0 + jnp.exp2(other - own))
        for head in range(heads):
            ref, slot = (near_ref, head) if head < FORWARD else (far_ref, head - FORWARD)
            share = shares[:, head : head + 1]
            cols = pl.ds(head * DH, DH)
            mine = low_ref[rows, cols]
            there = ref[rows, pl.ds(slot * DH, DH)].astype(F32)
            out_ref[rows, cols] = (there + (mine - there) * share).astype(BF)


def merge(first, low, lse, near, far, local, heads):
    width = low.shape[1]
    whole = lambda array: pl.BlockSpec(array.shape, lambda i: (0, 0))
    return pl.pallas_call(
        functools.partial(merge_kernel, heads),
        out_shape=pltpu.HBM(local.shape, BF),
        grid=(1,),
        in_specs=[SMALL, whole(low), whole(lse), whole(near), whole(far), ANY],
        out_specs=pl.BlockSpec((WIN, width), lambda i: (0, 0)),
        input_output_aliases={5: 0},
        compiler_params=params(),
        cost_estimate=cost(60),
        name="merge_local",
    )(first, low, lse, near, far, in_hbm(local))


def final_kernel(
    scale, heads, gate_ref, q_hbm, kv_hbm, local_hbm, out_hbm, q_ref, kv_ref, local_ref, out_ref, sems, out_sems
):
    c = scale * LOG2E
    pieces = MB // PIECE
    blocks = q_hbm.shape[0] // QB
    step = heads // HALVES
    chunks = [(block, half) for block in range(blocks) for half in range(HALVES)]
    loads, stores = [], []
    for index, (block, half) in enumerate(chunks):
        area = (pl.ds(block * QB, QB), pl.ds(half * step * DH, step * DH))
        mine = (slice(None), pl.ds((block * heads + half * step) * TOPK, step * TOPK))
        loads.append(
            [
                pltpu.make_async_copy(source.at[where], target.at[where], sems.at[index, kind])
                for kind, (source, target, where) in enumerate(
                    ((kv_hbm, kv_ref, mine), (q_hbm, q_ref, area), (local_hbm, local_ref, area))
                )
            ]
        )
        stores.append(pltpu.make_async_copy(out_ref.at[area], out_hbm.at[area], out_sems.at[index]))
    for index in range(2):
        for load in loads[index]:
            load.start()
    for index, (block, half) in enumerate(chunks):
        for load in loads[index]:
            load.wait()
        if index + 2 < len(chunks):
            for load in loads[index + 2]:
                load.start()
        rows = pl.ds(block * QB, QB)
        for head in range(half * step, (half + 1) * step):
            cols = pl.ds(head * DH, DH)
            mine = pl.ds((block * heads + head) * TOPK, TOPK)
            keys = kv_ref[0:pieces, mine].astype(F32).reshape(TOPK * MB, DH).astype(BF)
            values = kv_ref[pieces : 2 * pieces, mine].astype(F32).reshape(TOPK * MB, DH).astype(BF)
            s = dot_t(q_ref[rows, cols], keys)
            top = jnp.max(s, axis=1, keepdims=True)
            p = jnp.exp2((s - top) * c).astype(BF)
            acc = dot(p, with_ones(values))
            gate = gate_ref[head]
            remote = acc[:, :DH] * (gate / acc[:, DH:])
            local = local_ref[rows, cols].astype(F32)
            out_ref[rows, cols] = (remote + (1.0 - gate) * local).astype(BF)
        stores[index].start()
    for store in stores:
        store.wait()


def final_attention(gate, queries, kv, local, heads, scale):
    chunks = queries.shape[0] // QB * HALVES
    return pl.pallas_call(
        functools.partial(final_kernel, scale, heads),
        out_shape=pltpu.HBM(queries.shape, BF),
        in_specs=[SMALL, ANY, ANY, ANY],
        out_specs=ANY,
        scratch_shapes=[
            pltpu.VMEM(queries.shape, BF),
            pltpu.VMEM(kv.shape, BF),
            pltpu.VMEM(queries.shape, BF),
            pltpu.VMEM(queries.shape, BF),
            pltpu.SemaphoreType.DMA((chunks, 3)),
            pltpu.SemaphoreType.DMA((chunks,)),
        ],
        compiler_params=params(),
        cost_estimate=cost(7),
        name="final_attention",
    )(gate, in_hbm(queries), in_hbm(kv), in_hbm(local))


def body(queries, token_keys, token_values, mem_keys, mem_values, retrieved, gate_bias):
    tokens = queries.shape[0]
    heads = gate_bias.shape[0]
    scale = DH ** (-0.5)
    devices = lax.axis_size("seq")
    blocks = mem_keys.shape[0] // MB
    q_blocks = tokens // QB
    wanted = q_blocks * heads * TOPK
    upward = [(i, i + 1) for i in range(devices - 1)]
    downward = [(i, i - 1) for i in range(1, devices)]
    back_q, ahead_kv = edges(queries, token_keys, token_values)
    far_q = lax.ppermute(back_q, "seq", downward)
    near_kv = lax.ppermute(ahead_kv, "seq", upward)
    ids = retrieved.reshape(-1)
    ids_tile = jnp.zeros((PIECE * DH,), BF).at[:wanted].set(ids.astype(BF)).reshape(PIECE, DH)
    ids_tile, _ = lax.optimization_barrier((ids_tile, back_q))
    sent = pack(mem_keys, mem_values, ids_tile, blocks, heads)
    store = lax.all_to_all(sent, "seq", split_axis=0, concat_axis=0, tiled=True)
    gate_share = 1.0 / (1.0 + jnp.exp(-gate_bias))
    first = lax.axis_index("seq").reshape(1).astype(jnp.int32)
    low, lse, local = own_attention(queries, token_keys, token_values, heads, scale)
    far_part, near = edge_attention(
        far_q, near_kv, queries, token_keys, token_values, heads, scale
    )
    store, low, lse, local, far_part, near = lax.optimization_barrier(
        (store, low, lse, local, far_part, near)
    )
    far = lax.ppermute(far_part, "seq", upward)
    pieces = gather(store, blocks, heads, wanted)
    kv = lax.all_to_all(pieces, "seq", split_axis=0, concat_axis=0, tiled=True)
    local = merge(first, low, lse, near, far, local, heads)
    kv, local = lax.optimization_barrier((kv, local))
    return final_attention(gate_share, queries, kv, local, heads, scale)


def solution(mesh):
    in_specs = (
        P("seq", "head"),
        P("seq", "head"),
        P("seq", "head"),
        P("seq", "head"),
        P("seq", "head"),
        P("seq", "head", None),
        P("head"),
    )
    return jax.shard_map(
        body, mesh=mesh, in_specs=in_specs, out_specs=P("seq", "head"), check_vma=False
    )
```

```python
import functools

import jax
import jax.numpy as jnp
from jax import lax
from jax.experimental import pallas as pl
from jax.experimental.pallas import tpu as pltpu
from jax.sharding import PartitionSpec as P

QB = 512
MB = 128
TOPK = 2
WIN = 512
DH = 128
PIECE = 8
EDGE = 256
FORWARD = 5
HALVES = 2
LOG2E = 1.4426950408889634
NEG = -1e30
BF = jnp.bfloat16
F32 = jnp.float32
ANY = pl.BlockSpec(memory_space=pl.ANY)
WHOLE = pl.BlockSpec(memory_space=pltpu.VMEM)
SMALL = pl.BlockSpec(memory_space=pltpu.SMEM)


def params(mebibytes):
    return pltpu.CompilerParams(vmem_limit_bytes=mebibytes << 20)


def cost(micros):
    return pl.CostEstimate(flops=int(micros * 1e9), transcendentals=0, bytes_accessed=0)


def in_hbm(array):
    return pltpu.with_memory_space_constraint(array, pltpu.HBM)


def tiles(array):
    rows, width = array.shape
    return array.reshape(rows // PIECE, PIECE, width // DH, DH).transpose(0, 2, 1, 3)


def prepare_kernel(
    blocks,
    heads,
    keys_ref,
    values_ref,
    ids_ref,
    q_ref,
    k_ref,
    v_ref,
    sent_ref,
    back_ref,
    ahead_ref,
    stage,
    in_sems,
    out_sems,
    cut_sems,
):
    pieces = MB // PIECE
    loads, stores = [], []
    for half, source in enumerate((keys_ref, values_ref)):
        for block in range(blocks):
            slot = len(loads)
            here = stage.at[pl.ds(slot * pieces, pieces)]
            there = sent_ref.at[pl.ds(half * pieces, pieces), pl.ds(block * heads, heads)]
            rows = pl.ds(block * pieces, pieces)
            loads.append(pltpu.make_async_copy(source.at[rows], here, in_sems.at[slot]))
            stores.append(pltpu.make_async_copy(here, there, out_sems.at[slot]))
    ids_store = pltpu.make_async_copy(
        ids_ref, sent_ref.at[:, pl.ds(blocks * heads, 1)], out_sems.at[2 * blocks]
    )
    split = FORWARD * DH
    tail = pl.ds(k_ref.shape[0] - WIN, WIN)
    cuts = [
        pltpu.make_async_copy(
            k_ref.at[tail, pl.ds(0, split)], ahead_ref.at[:, pl.ds(0, split)], cut_sems.at[0]
        ),
        pltpu.make_async_copy(
            v_ref.at[tail, pl.ds(0, split)], ahead_ref.at[:, pl.ds(split, split)], cut_sems.at[1]
        ),
        pltpu.make_async_copy(
            q_ref.at[pl.ds(0, WIN), pl.ds(split, q_ref.shape[1] - split)], back_ref, cut_sems.at[2]
        ),
    ]
    for load in loads:
        load.start()
    for cut in cuts:
        cut.start()
    ids_store.start()
    for load, store in zip(loads, stores):
        load.wait()
        store.start()
    for cut in cuts:
        cut.wait()
    for store in stores:
        store.wait()
    ids_store.wait()


def prepare(mem_keys, mem_values, ids_tile, queries, keys, values, blocks, heads):
    devices = 2 * MB // PIECE
    split = FORWARD * DH
    return pl.pallas_call(
        functools.partial(prepare_kernel, blocks, heads),
        out_shape=(
            pltpu.HBM((devices, blocks * heads + 1, PIECE, DH), BF),
            jax.ShapeDtypeStruct((WIN, queries.shape[1] - split), BF),
            jax.ShapeDtypeStruct((WIN, 2 * split), BF),
        ),
        in_specs=[ANY, ANY, WHOLE, ANY, ANY, ANY],
        out_specs=(ANY, WHOLE, WHOLE),
        scratch_shapes=[
            pltpu.VMEM((2 * blocks * MB // PIECE, heads, PIECE, DH), BF),
            pltpu.SemaphoreType.DMA((2 * blocks,)),
            pltpu.SemaphoreType.DMA((2 * blocks + 1,)),
            pltpu.SemaphoreType.DMA((3,)),
        ],
        compiler_params=params(8),
        cost_estimate=cost(2),
        name="prepare",
    )(
        in_hbm(tiles(mem_keys)),
        in_hbm(tiles(mem_values)),
        jnp.broadcast_to(ids_tile, (devices, 1, PIECE, DH)),
        in_hbm(queries),
        in_hbm(keys),
        in_hbm(values),
    )


def gather_kernel(
    blocks, heads, wanted, store_ref, out_ref, ids, rows_v, rows_s, store, stage, ids_sem, sems, out_sems
):
    devices, stride = store_ref.shape[:2]
    parts = sems.shape[0]
    groups = out_sems.shape[0]
    size = devices // groups
    ids_load = pltpu.make_async_copy(store_ref.at[:, stride - 1], ids, ids_sem.at[0])
    ids_load.start()
    loads, stores = [], []
    for part in range(parts):
        span = pl.ds(part * (devices // parts), devices // parts)
        loads.append(pltpu.make_async_copy(store_ref.at[span], store.at[span], sems.at[part]))
    for group in range(groups):
        span = pl.ds(group * size, size)
        stores.append(pltpu.make_async_copy(stage.at[span], out_ref.at[span], out_sems.at[group]))
    for load in loads:
        load.start()
    ids_load.wait()
    row = lax.broadcasted_iota(jnp.int32, (devices, PIECE, DH), 1)
    block = jnp.sum(jnp.where(row == 0, ids[...].astype(F32), 0.0), axis=1).astype(jnp.int32)
    lane = lax.broadcasted_iota(jnp.int32, (devices, DH), 1)
    head = lane // TOPK % heads
    rows_v[...] = block // blocks * stride + block % blocks * heads + head
    rows_copy = pltpu.make_async_copy(rows_v, rows_s, ids_sem.at[1])
    rows_copy.start()
    rows_copy.wait()
    for load in loads:
        load.wait()
    flat = store.reshape(devices * stride, PIECE, DH)
    for group in range(groups):

        @pl.loop(group * size, (group + 1) * size)
        def _(device):
            for request in range(wanted):
                stage[device, request] = flat[rows_s[device, request]]

        stores[group].start()
    for store_copy in stores:
        store_copy.wait()


def gather(store, blocks, heads, wanted):
    devices = store.shape[0]
    return pl.pallas_call(
        functools.partial(gather_kernel, blocks, heads, wanted),
        out_shape=pltpu.HBM((devices, wanted, PIECE, DH), BF),
        in_specs=[ANY],
        out_specs=ANY,
        scratch_shapes=[
            pltpu.VMEM((devices, PIECE, DH), BF),
            pltpu.VMEM((devices, DH), jnp.int32),
            pltpu.SMEM((devices, DH), jnp.int32),
            pltpu.VMEM(store.shape, BF),
            pltpu.VMEM((devices, wanted, PIECE, DH), BF),
            pltpu.SemaphoreType.DMA((2,)),
            pltpu.SemaphoreType.DMA((4,)),
            pltpu.SemaphoreType.DMA((8,)),
        ],
        compiler_params=params(16),
        cost_estimate=cost(6),
        name="gather_pieces",
    )(in_hbm(store))


def dot_t(a, b):
    return lax.dot_general(a, b, (((1,), (1,)), ((), ())), preferred_element_type=F32)


def dot(a, b):
    return jnp.dot(a, b, preferred_element_type=F32)


def with_ones(values):
    return jnp.concatenate([values, jnp.ones_like(values)], axis=1)


def triangle():
    row = lax.broadcasted_iota(jnp.int32, (EDGE, EDGE), 0)
    col = lax.broadcasted_iota(jnp.int32, (EDGE, EDGE), 1)
    return col <= row


def own_kernel(scale, heads, q_ref, k_ref, v_ref, low_ref, lse_ref, out_ref):
    lower = triangle()
    c = scale * LOG2E
    lanes = lax.broadcasted_iota(jnp.int32, (EDGE, DH), 1)
    for head in range(heads):
        cols = pl.ds(head * DH, DH)
        for i in range(WIN // EDGE):
            rows = pl.ds(i * EDGE, EDGE)
            seen = pl.ds(0, (i + 1) * EDGE)
            s = dot_t(q_ref[rows, cols], k_ref[seen, cols])
            diag = jnp.where(lower, s[:, i * EDGE :], NEG)
            if i:
                s = jnp.concatenate([s[:, : i * EDGE], diag], axis=1)
            else:
                s = diag
            top = jnp.max(s, axis=1, keepdims=True)
            p = jnp.exp2((s - top) * c).astype(BF)
            acc = dot(p, with_ones(v_ref[seen, cols]))
            total = acc[:, DH:]
            low_ref[rows, cols] = acc[:, :DH] / total
            lse_ref[rows, :] = jnp.where(lanes == head, top * c + jnp.log2(total), lse_ref[rows, :])
        for i in range(WIN // EDGE, q_ref.shape[0] // EDGE):
            rows = pl.ds(i * EDGE, EDGE)
            seen = pl.ds(i * EDGE - WIN, WIN + EDGE)
            s = dot_t(q_ref[rows, cols], k_ref[seen, cols])
            ends = jnp.where(lower, s[:, WIN:], s[:, :EDGE])
            mid = s[:, EDGE:WIN]
            top = jnp.maximum(
                jnp.max(ends, axis=1, keepdims=True), jnp.max(mid, axis=1, keepdims=True)
            )
            ends = jnp.exp2((ends - top) * c)
            mid = jnp.exp2((mid - top) * c).astype(BF)
            first = jnp.where(lower, 0.0, ends).astype(BF)
            last = jnp.where(lower, ends, 0.0).astype(BF)
            acc = dot(jnp.concatenate([first, mid, last], axis=1), with_ones(v_ref[seen, cols]))
            out_ref[rows, cols] = (acc[:, :DH] / acc[:, DH:]).astype(BF)


def own_attention(queries, keys, values, heads, scale):
    tokens, width = queries.shape
    return pl.pallas_call(
        functools.partial(own_kernel, scale, heads),
        out_shape=(
            jax.ShapeDtypeStruct((WIN, width), F32),
            jax.ShapeDtypeStruct((WIN, DH), F32),
            jax.ShapeDtypeStruct((tokens, width), BF),
        ),
        in_specs=[WHOLE] * 3,
        out_specs=(WHOLE,) * 3,
        compiler_params=params(30),
        cost_estimate=cost(1),
        name="own_attention",
    )(queries, keys, values)


def edge_part(scale, slots, tail, q_ref, k_ref, v_ref, out_ref, lse_ref):
    lower = triangle()
    c = scale * LOG2E
    lanes = lax.broadcasted_iota(jnp.int32, (EDGE, DH), 1)
    count = len(slots)
    lse_ref[...] = jnp.zeros_like(lse_ref)
    for slot, (q_head, k_head, v_head) in enumerate(slots):
        q_cols = pl.ds(q_head * DH, DH)
        k_cols = pl.ds(k_head * DH, DH)
        v_cols = pl.ds(v_head * DH, DH)
        for i in range(WIN // EDGE):
            rows = pl.ds(i * EDGE, EDGE)
            seen = pl.ds(tail + i * EDGE, WIN - i * EDGE)
            s = dot_t(q_ref[rows, q_cols], k_ref[seen, k_cols])
            edge = jnp.where(lower, NEG, s[:, :EDGE])
            if s.shape[1] > EDGE:
                s = jnp.concatenate([edge, s[:, EDGE:]], axis=1)
            else:
                s = edge
            top = jnp.max(s, axis=1, keepdims=True)
            p = jnp.exp2((s - top) * c).astype(BF)
            acc = dot(p, with_ones(v_ref[seen, v_cols]))
            total = acc[:, DH:]
            out_ref[rows, pl.ds(slot * DH, DH)] = (acc[:, :DH] / total).astype(BF)
            lse_ref[rows, :] = jnp.where(lanes == slot, top * c + jnp.log2(total), lse_ref[rows, :])
    stat = lse_ref[...]
    high = stat.astype(BF).astype(F32)
    mid = (stat - high).astype(BF).astype(F32)
    low = (stat - high - mid).astype(BF).astype(F32)
    packed = high + pltpu.roll(mid, count, 1) + pltpu.roll(low, 2 * count, 1)
    out_ref[:, pl.ds(count * DH, DH)] = packed.astype(BF)


def edge_kernel(
    scale, heads, far_q_ref, near_kv_ref, q_ref, k_ref, v_ref, far_ref, near_ref, lse_ref
):
    far = [(head - FORWARD, head, head) for head in range(FORWARD, heads)]
    near = [(head, head, FORWARD + head) for head in range(FORWARD)]
    tail = k_ref.shape[0] - WIN
    edge_part(scale, far, tail, far_q_ref, k_ref, v_ref, far_ref, lse_ref)
    edge_part(scale, near, 0, q_ref, near_kv_ref, near_kv_ref, near_ref, lse_ref)


def edge_attention(far_q, near_kv, queries, keys, values, heads, scale):
    return pl.pallas_call(
        functools.partial(edge_kernel, scale, heads),
        out_shape=(
            jax.ShapeDtypeStruct((WIN, (heads - FORWARD + 1) * DH), BF),
            jax.ShapeDtypeStruct((WIN, (FORWARD + 1) * DH), BF),
        ),
        in_specs=[WHOLE] * 5,
        out_specs=(WHOLE,) * 2,
        scratch_shapes=[pltpu.VMEM((WIN, DH), F32)],
        compiler_params=params(24),
        cost_estimate=cost(60),
        name="edge_attention",
    )(far_q, near_kv, queries, keys, values)


def unpacked(stat, count):
    return stat + pltpu.roll(stat, DH - count, 1) + pltpu.roll(stat, DH - 2 * count, 1)


def merge_kernel(heads, first_ref, low_ref, lse_ref, near_ref, far_ref, into_ref, out_ref):
    del into_ref
    lanes = lax.broadcasted_iota(jnp.int32, (EDGE, DH), 1)
    behind = heads - FORWARD
    for i in range(WIN // EDGE):
        rows = pl.ds(i * EDGE, EDGE)
        near_stat = unpacked(near_ref[rows, pl.ds(FORWARD * DH, DH)].astype(F32), FORWARD)
        far_stat = unpacked(far_ref[rows, pl.ds(behind * DH, DH)].astype(F32), behind)
        other = jnp.where(lanes < FORWARD, near_stat, pltpu.roll(far_stat, FORWARD, 1))
        other = jnp.where(first_ref[0] == 0, NEG, other)
        own = jnp.where(lanes < heads, lse_ref[rows, :], 0.0)
        shares = 1.0 / (1.0 + jnp.exp2(other - own))
        for head in range(heads):
            ref, slot = (near_ref, head) if head < FORWARD else (far_ref, head - FORWARD)
            share = shares[:, head : head + 1]
            cols = pl.ds(head * DH, DH)
            mine = low_ref[rows, cols]
            there = ref[rows, pl.ds(slot * DH, DH)].astype(F32)
            out_ref[rows, cols] = (there + (mine - there) * share).astype(BF)


def merge(first, low, lse, near, far, local, heads):
    width = low.shape[1]
    whole = lambda array: pl.BlockSpec(array.shape, lambda i: (0, 0))
    return pl.pallas_call(
        functools.partial(merge_kernel, heads),
        out_shape=pltpu.HBM(local.shape, BF),
        grid=(1,),
        in_specs=[SMALL, whole(low), whole(lse), whole(near), whole(far), ANY],
        out_specs=pl.BlockSpec((WIN, width), lambda i: (0, 0)),
        input_output_aliases={5: 0},
        compiler_params=params(16),
        cost_estimate=cost(60),
        name="merge_local",
    )(first, low, lse, near, far, in_hbm(local))


def final_kernel(
    scale, heads, gate_ref, q_hbm, kv_hbm, local_hbm, out_hbm, q_ref, kv_ref, local_ref, out_ref, sems, out_sems
):
    c = scale * LOG2E
    pieces = MB // PIECE
    blocks = q_hbm.shape[0] // QB
    step = heads // HALVES
    chunks = [(block, half) for block in range(blocks) for half in range(HALVES)]
    loads, stores = [], []
    for index, (block, half) in enumerate(chunks):
        area = (pl.ds(block * QB, QB), pl.ds(half * step * DH, step * DH))
        mine = (slice(None), pl.ds((block * heads + half * step) * TOPK, step * TOPK))
        loads.append(
            [
                pltpu.make_async_copy(source.at[where], target.at[where], sems.at[index, kind])
                for kind, (source, target, where) in enumerate(
                    ((kv_hbm, kv_ref, mine), (q_hbm, q_ref, area), (local_hbm, local_ref, area))
                )
            ]
        )
        stores.append(pltpu.make_async_copy(out_ref.at[area], out_hbm.at[area], out_sems.at[index]))
    for index in range(2):
        for load in loads[index]:
            load.start()
    for index, (block, half) in enumerate(chunks):
        for load in loads[index]:
            load.wait()
        if index + 2 < len(chunks):
            for load in loads[index + 2]:
                load.start()
        rows = pl.ds(block * QB, QB)
        for head in range(half * step, (half + 1) * step):
            cols = pl.ds(head * DH, DH)
            mine = pl.ds((block * heads + head) * TOPK, TOPK)
            keys = kv_ref[0:pieces, mine].astype(F32).reshape(TOPK * MB, DH).astype(BF)
            values = kv_ref[pieces : 2 * pieces, mine].astype(F32).reshape(TOPK * MB, DH).astype(BF)
            s = dot_t(q_ref[rows, cols], keys)
            top = jnp.max(s, axis=1, keepdims=True)
            p = jnp.exp2((s - top) * c).astype(BF)
            acc = dot(p, with_ones(values))
            gate = gate_ref[head]
            remote = acc[:, :DH] * (gate / acc[:, DH:])
            local = local_ref[rows, cols].astype(F32)
            out_ref[rows, cols] = (remote + (1.0 - gate) * local).astype(BF)
        stores[index].start()
    for store in stores:
        store.wait()


def final_attention(gate, queries, kv, local, heads, scale):
    chunks = queries.shape[0] // QB * HALVES
    return pl.pallas_call(
        functools.partial(final_kernel, scale, heads),
        out_shape=pltpu.HBM(queries.shape, BF),
        in_specs=[SMALL, ANY, ANY, ANY],
        out_specs=ANY,
        scratch_shapes=[
            pltpu.VMEM(queries.shape, BF),
            pltpu.VMEM(kv.shape, BF),
            pltpu.VMEM(queries.shape, BF),
            pltpu.VMEM(queries.shape, BF),
            pltpu.SemaphoreType.DMA((chunks, 3)),
            pltpu.SemaphoreType.DMA((chunks,)),
        ],
        compiler_params=params(24),
        cost_estimate=cost(7),
        name="final_attention",
    )(gate, in_hbm(queries), in_hbm(kv), in_hbm(local))


def body(queries, token_keys, token_values, mem_keys, mem_values, retrieved, gate_bias):
    tokens = queries.shape[0]
    heads = gate_bias.shape[0]
    scale = DH ** (-0.5)
    devices = lax.axis_size("seq")
    blocks = mem_keys.shape[0] // MB
    q_blocks = tokens // QB
    wanted = q_blocks * heads * TOPK
    upward = [(i, i + 1) for i in range(devices - 1)]
    downward = [(i, i - 1) for i in range(1, devices)]
    ids = retrieved.reshape(-1)
    ids_tile = jnp.zeros((PIECE * DH,), BF).at[:wanted].set(ids.astype(BF)).reshape(PIECE, DH)
    sent, back_q, ahead_kv = prepare(
        mem_keys, mem_values, ids_tile, queries, token_keys, token_values, blocks, heads
    )
    far_q = lax.ppermute(back_q, "seq", downward)
    near_kv = lax.ppermute(ahead_kv, "seq", upward)
    store = lax.all_to_all(sent, "seq", split_axis=0, concat_axis=0, tiled=True)
    gate_share = 1.0 / (1.0 + jnp.exp(-gate_bias))
    first = lax.axis_index("seq").reshape(1).astype(jnp.int32)
    low, lse, local = own_attention(queries, token_keys, token_values, heads, scale)
    far_part, near = edge_attention(
        far_q, near_kv, queries, token_keys, token_values, heads, scale
    )
    store, low, lse, local, far_part, near = lax.optimization_barrier(
        (store, low, lse, local, far_part, near)
    )
    far = lax.ppermute(far_part, "seq", upward)
    pieces = gather(store, blocks, heads, wanted)
    kv = lax.all_to_all(pieces, "seq", split_axis=0, concat_axis=0, tiled=True)
    local = merge(first, low, lse, near, far, local, heads)
    kv, local = lax.optimization_barrier((kv, local))
    return final_attention(gate_share, queries, kv, local, heads, scale)


def solution(mesh):
    in_specs = (
        P("seq", "head"),
        P("seq", "head"),
        P("seq", "head"),
        P("seq", "head"),
        P("seq", "head"),
        P("seq", "head", None),
        P("head"),
    )
    return jax.shard_map(
        body, mesh=mesh, in_specs=in_specs, out_specs=P("seq", "head"), check_vma=False
    )
```

```python
import functools

import jax
import jax.numpy as jnp
from jax import lax
from jax.experimental import pallas as pl
from jax.experimental.pallas import tpu as pltpu
from jax.sharding import PartitionSpec as P

QB = 512
MB = 128
TOPK = 2
WIN = 512
DH = 128
PIECE = 8
EDGE = 256
FORWARD = 5
HALVES = 2
LOG2E = 1.4426950408889634
NEG = -1e30
BF = jnp.bfloat16
F32 = jnp.float32
ANY = pl.BlockSpec(memory_space=pl.ANY)
WHOLE = pl.BlockSpec(memory_space=pltpu.VMEM)
SMALL = pl.BlockSpec(memory_space=pltpu.SMEM)


def params(mebibytes):
    return pltpu.CompilerParams(vmem_limit_bytes=mebibytes << 20)


def cost(micros):
    return pl.CostEstimate(flops=int(micros * 1e9), transcendentals=0, bytes_accessed=0)


def in_hbm(array):
    return pltpu.with_memory_space_constraint(array, pltpu.HBM)


def copy_all(copies):
    for copy in copies:
        copy.start()
    for copy in copies:
        copy.wait()


def cut_kernel(areas, *refs):
    out_ref, sems = refs[-2:]
    width = out_ref.shape[1] // len(areas)
    copies = [
        pltpu.make_async_copy(
            ref.at[pl.ds(row, WIN), pl.ds(col, width)],
            out_ref.at[:, pl.ds(index * width, width)],
            sems.at[index],
        )
        for index, (ref, (row, col)) in enumerate(zip(refs, areas))
    ]
    copy_all(copies)


def cut(arrays, areas, width, name):
    return pl.pallas_call(
        functools.partial(cut_kernel, areas),
        out_shape=jax.ShapeDtypeStruct((WIN, width), BF),
        in_specs=[ANY] * len(arrays),
        out_specs=WHOLE,
        scratch_shapes=[pltpu.SemaphoreType.DMA((len(arrays),))],
        compiler_params=params(4),
        cost_estimate=cost(2),
        name=name,
    )(*map(in_hbm, arrays))


def pack_kernel(blocks, heads, keys_ref, values_ref, ids_ref, out_ref, stage, in_sems, out_sems):
    pieces = MB // PIECE
    loads, stores = [], []
    for half, source in enumerate((keys_ref, values_ref)):
        for block in range(blocks):
            slot = len(loads)
            here = stage.at[pl.ds(slot * pieces, pieces)]
            there = out_ref.at[pl.ds(half * pieces, pieces), pl.ds(block * heads, heads)]
            rows = pl.ds(block * pieces, pieces)
            loads.append(pltpu.make_async_copy(source.at[rows], here, in_sems.at[slot]))
            stores.append(pltpu.make_async_copy(here, there, out_sems.at[slot]))
    ids_store = pltpu.make_async_copy(
        ids_ref, out_ref.at[:, pl.ds(blocks * heads, 1)], out_sems.at[2 * blocks]
    )
    for load in loads:
        load.start()
    ids_store.start()
    for load, store in zip(loads, stores):
        load.wait()
        store.start()
    for store in stores:
        store.wait()
    ids_store.wait()


def tiles(array):
    rows, width = array.shape
    return array.reshape(rows // PIECE, PIECE, width // DH, DH).transpose(0, 2, 1, 3)


def pack(mem_keys, mem_values, ids_tile, blocks, heads):
    devices = 2 * MB // PIECE
    return pl.pallas_call(
        functools.partial(pack_kernel, blocks, heads),
        out_shape=pltpu.HBM((devices, blocks * heads + 1, PIECE, DH), BF),
        in_specs=[ANY, ANY, WHOLE],
        out_specs=ANY,
        scratch_shapes=[
            pltpu.VMEM((2 * blocks * MB // PIECE, heads, PIECE, DH), BF),
            pltpu.SemaphoreType.DMA((2 * blocks,)),
            pltpu.SemaphoreType.DMA((2 * blocks + 1,)),
        ],
        compiler_params=params(8),
        cost_estimate=cost(2),
        name="pack_pieces",
    )(
        in_hbm(tiles(mem_keys)),
        in_hbm(tiles(mem_values)),
        jnp.broadcast_to(ids_tile, (devices, 1, PIECE, DH)),
    )


def gather_kernel(
    blocks, heads, wanted, store_ref, out_ref, ids, rows_v, rows_s, store, stage, ids_sem, sems, out_sems
):
    devices, stride = store_ref.shape[:2]
    parts = sems.shape[0]
    groups = out_sems.shape[0]
    size = devices // groups
    ids_load = pltpu.make_async_copy(store_ref.at[:, stride - 1], ids, ids_sem.at[0])
    ids_load.start()
    loads, stores = [], []
    for part in range(parts):
        span = pl.ds(part * (devices // parts), devices // parts)
        loads.append(pltpu.make_async_copy(store_ref.at[span], store.at[span], sems.at[part]))
    for group in range(groups):
        span = pl.ds(group * size, size)
        stores.append(pltpu.make_async_copy(stage.at[span], out_ref.at[span], out_sems.at[group]))
    for load in loads:
        load.start()
    ids_load.wait()
    row = lax.broadcasted_iota(jnp.int32, (devices, PIECE, DH), 1)
    block = jnp.sum(jnp.where(row == 0, ids[...].astype(F32), 0.0), axis=1).astype(jnp.int32)
    lane = lax.broadcasted_iota(jnp.int32, (devices, DH), 1)
    head = lane // TOPK % heads
    rows_v[...] = block // blocks * stride + block % blocks * heads + head
    rows_copy = pltpu.make_async_copy(rows_v, rows_s, ids_sem.at[1])
    rows_copy.start()
    rows_copy.wait()
    for load in loads:
        load.wait()
    flat = store.reshape(devices * stride, PIECE, DH)
    for group in range(groups):

        @pl.loop(group * size, (group + 1) * size)
        def _(device):
            for request in range(wanted):
                stage[device, request] = flat[rows_s[device, request]]

        stores[group].start()
    for store_copy in stores:
        store_copy.wait()


def gather(store, blocks, heads, wanted):
    devices = store.shape[0]
    return pl.pallas_call(
        functools.partial(gather_kernel, blocks, heads, wanted),
        out_shape=pltpu.HBM((devices, wanted, PIECE, DH), BF),
        in_specs=[ANY],
        out_specs=ANY,
        scratch_shapes=[
            pltpu.VMEM((devices, PIECE, DH), BF),
            pltpu.VMEM((devices, DH), jnp.int32),
            pltpu.SMEM((devices, DH), jnp.int32),
            pltpu.VMEM(store.shape, BF),
            pltpu.VMEM((devices, wanted, PIECE, DH), BF),
            pltpu.SemaphoreType.DMA((2,)),
            pltpu.SemaphoreType.DMA((4,)),
            pltpu.SemaphoreType.DMA((8,)),
        ],
        compiler_params=params(16),
        cost_estimate=cost(6),
        name="gather_pieces",
    )(in_hbm(store))


def dot_t(a, b):
    return lax.dot_general(a, b, (((1,), (1,)), ((), ())), preferred_element_type=F32)


def dot(a, b):
    return jnp.dot(a, b, preferred_element_type=F32)


def with_ones(values):
    return jnp.concatenate([values, jnp.ones_like(values)], axis=1)


def triangle():
    row = lax.broadcasted_iota(jnp.int32, (EDGE, EDGE), 0)
    col = lax.broadcasted_iota(jnp.int32, (EDGE, EDGE), 1)
    return col <= row


def own_kernel(scale, heads, q_ref, k_ref, v_ref, low_ref, lse_ref, out_ref):
    lower = triangle()
    c = scale * LOG2E
    lanes = lax.broadcasted_iota(jnp.int32, (EDGE, DH), 1)
    for head in range(heads):
        cols = pl.ds(head * DH, DH)
        for i in range(WIN // EDGE):
            rows = pl.ds(i * EDGE, EDGE)
            seen = pl.ds(0, (i + 1) * EDGE)
            s = dot_t(q_ref[rows, cols], k_ref[seen, cols])
            diag = jnp.where(lower, s[:, i * EDGE :], NEG)
            if i:
                s = jnp.concatenate([s[:, : i * EDGE], diag], axis=1)
            else:
                s = diag
            top = jnp.max(s, axis=1, keepdims=True)
            p = jnp.exp2((s - top) * c).astype(BF)
            acc = dot(p, with_ones(v_ref[seen, cols]))
            total = acc[:, DH:]
            low_ref[rows, cols] = acc[:, :DH] / total
            lse_ref[rows, :] = jnp.where(lanes == head, top * c + jnp.log2(total), lse_ref[rows, :])
        for i in range(WIN // EDGE, q_ref.shape[0] // EDGE):
            rows = pl.ds(i * EDGE, EDGE)
            seen = pl.ds(i * EDGE - WIN, WIN + EDGE)
            s = dot_t(q_ref[rows, cols], k_ref[seen, cols])
            ends = jnp.where(lower, s[:, WIN:], s[:, :EDGE])
            mid = s[:, EDGE:WIN]
            top = jnp.maximum(
                jnp.max(ends, axis=1, keepdims=True), jnp.max(mid, axis=1, keepdims=True)
            )
            ends = jnp.exp2((ends - top) * c)
            mid = jnp.exp2((mid - top) * c).astype(BF)
            first = jnp.where(lower, 0.0, ends).astype(BF)
            last = jnp.where(lower, ends, 0.0).astype(BF)
            acc = dot(jnp.concatenate([first, mid, last], axis=1), with_ones(v_ref[seen, cols]))
            out_ref[rows, cols] = (acc[:, :DH] / acc[:, DH:]).astype(BF)


def own_attention(queries, keys, values, heads, scale):
    tokens, width = queries.shape
    return pl.pallas_call(
        functools.partial(own_kernel, scale, heads),
        out_shape=(
            jax.ShapeDtypeStruct((WIN, width), F32),
            jax.ShapeDtypeStruct((WIN, DH), F32),
            jax.ShapeDtypeStruct((tokens, width), BF),
        ),
        in_specs=[WHOLE] * 3,
        out_specs=(WHOLE,) * 3,
        compiler_params=params(30),
        cost_estimate=cost(20),
        name="own_attention",
    )(queries, keys, values)


def edge_part(scale, slots, tail, q_ref, k_ref, v_ref, out_ref, lse_ref):
    lower = triangle()
    c = scale * LOG2E
    lanes = lax.broadcasted_iota(jnp.int32, (EDGE, DH), 1)
    count = len(slots)
    lse_ref[...] = jnp.zeros_like(lse_ref)
    for slot, (q_head, k_head, v_head) in enumerate(slots):
        q_cols = pl.ds(q_head * DH, DH)
        k_cols = pl.ds(k_head * DH, DH)
        v_cols = pl.ds(v_head * DH, DH)
        for i in range(WIN // EDGE):
            rows = pl.ds(i * EDGE, EDGE)
            seen = pl.ds(tail + i * EDGE, WIN - i * EDGE)
            s = dot_t(q_ref[rows, q_cols], k_ref[seen, k_cols])
            edge = jnp.where(lower, NEG, s[:, :EDGE])
            if s.shape[1] > EDGE:
                s = jnp.concatenate([edge, s[:, EDGE:]], axis=1)
            else:
                s = edge
            top = jnp.max(s, axis=1, keepdims=True)
            p = jnp.exp2((s - top) * c).astype(BF)
            acc = dot(p, with_ones(v_ref[seen, v_cols]))
            total = acc[:, DH:]
            out_ref[rows, pl.ds(slot * DH, DH)] = (acc[:, :DH] / total).astype(BF)
            lse_ref[rows, :] = jnp.where(lanes == slot, top * c + jnp.log2(total), lse_ref[rows, :])
    stat = lse_ref[...]
    high = stat.astype(BF).astype(F32)
    mid = (stat - high).astype(BF).astype(F32)
    low = (stat - high - mid).astype(BF).astype(F32)
    packed = high + pltpu.roll(mid, count, 1) + pltpu.roll(low, 2 * count, 1)
    out_ref[:, pl.ds(count * DH, DH)] = packed.astype(BF)


def far_kernel(scale, heads, q_ref, k_ref, v_ref, out_ref, lse_ref):
    slots = [(head - FORWARD, head, head) for head in range(FORWARD, heads)]
    edge_part(scale, slots, k_ref.shape[0] - WIN, q_ref, k_ref, v_ref, out_ref, lse_ref)


def near_kernel(scale, q_ref, kv_ref, out_ref, lse_ref):
    slots = [(head, head, FORWARD + head) for head in range(FORWARD)]
    edge_part(scale, slots, 0, q_ref, kv_ref, kv_ref, out_ref, lse_ref)


def edge_attention(kernel, arrays, count, micros, name):
    return pl.pallas_call(
        kernel,
        out_shape=jax.ShapeDtypeStruct((WIN, (count + 1) * DH), BF),
        in_specs=[WHOLE] * len(arrays),
        out_specs=WHOLE,
        scratch_shapes=[pltpu.VMEM((WIN, DH), F32)],
        compiler_params=params(24),
        cost_estimate=cost(micros),
        name=name,
    )(*arrays)


def unpacked(stat, count):
    return stat + pltpu.roll(stat, DH - count, 1) + pltpu.roll(stat, DH - 2 * count, 1)


def merge_kernel(heads, first_ref, low_ref, lse_ref, near_ref, far_ref, into_ref, out_ref):
    del into_ref
    lanes = lax.broadcasted_iota(jnp.int32, (EDGE, DH), 1)
    behind = heads - FORWARD
    for i in range(WIN // EDGE):
        rows = pl.ds(i * EDGE, EDGE)
        near_stat = unpacked(near_ref[rows, pl.ds(FORWARD * DH, DH)].astype(F32), FORWARD)
        far_stat = unpacked(far_ref[rows, pl.ds(behind * DH, DH)].astype(F32), behind)
        other = jnp.where(lanes < FORWARD, near_stat, pltpu.roll(far_stat, FORWARD, 1))
        other = jnp.where(first_ref[0] == 0, NEG, other)
        own = jnp.where(lanes < heads, lse_ref[rows, :], 0.0)
        shares = 1.0 / (1.0 + jnp.exp2(other - own))
        for head in range(heads):
            ref, slot = (near_ref, head) if head < FORWARD else (far_ref, head - FORWARD)
            share = shares[:, head : head + 1]
            cols = pl.ds(head * DH, DH)
            mine = low_ref[rows, cols]
            there = ref[rows, pl.ds(slot * DH, DH)].astype(F32)
            out_ref[rows, cols] = (there + (mine - there) * share).astype(BF)


def merge(first, low, lse, near, far, local, heads):
    width = low.shape[1]
    whole = lambda array: pl.BlockSpec(array.shape, lambda i: (0, 0))
    return pl.pallas_call(
        functools.partial(merge_kernel, heads),
        out_shape=pltpu.HBM(local.shape, BF),
        grid=(1,),
        in_specs=[SMALL, whole(low), whole(lse), whole(near), whole(far), ANY],
        out_specs=pl.BlockSpec((WIN, width), lambda i: (0, 0)),
        input_output_aliases={5: 0},
        compiler_params=params(16),
        cost_estimate=cost(60),
        name="merge_local",
    )(first, low, lse, near, far, in_hbm(local))


def final_kernel(
    scale, heads, gate_ref, q_hbm, kv_hbm, local_hbm, out_hbm, q_ref, kv_ref, local_ref, out_ref, sems, out_sems
):
    c = scale * LOG2E
    pieces = MB // PIECE
    blocks = q_hbm.shape[0] // QB
    step = heads // HALVES
    chunks = [(block, half) for block in range(blocks) for half in range(HALVES)]
    loads, stores = [], []
    for index, (block, half) in enumerate(chunks):
        area = (pl.ds(block * QB, QB), pl.ds(half * step * DH, step * DH))
        mine = (slice(None), pl.ds((block * heads + half * step) * TOPK, step * TOPK))
        loads.append(
            [
                pltpu.make_async_copy(source.at[where], target.at[where], sems.at[index, kind])
                for kind, (source, target, where) in enumerate(
                    ((kv_hbm, kv_ref, mine), (q_hbm, q_ref, area), (local_hbm, local_ref, area))
                )
            ]
        )
        stores.append(pltpu.make_async_copy(out_ref.at[area], out_hbm.at[area], out_sems.at[index]))
    for index in range(2):
        for load in loads[index]:
            load.start()
    for index, (block, half) in enumerate(chunks):
        for load in loads[index]:
            load.wait()
        if index + 2 < len(chunks):
            for load in loads[index + 2]:
                load.start()
        rows = pl.ds(block * QB, QB)
        for head in range(half * step, (half + 1) * step):
            cols = pl.ds(head * DH, DH)
            mine = pl.ds((block * heads + head) * TOPK, TOPK)
            keys = kv_ref[0:pieces, mine].astype(F32).reshape(TOPK * MB, DH).astype(BF)
            values = kv_ref[pieces : 2 * pieces, mine].astype(F32).reshape(TOPK * MB, DH).astype(BF)
            s = dot_t(q_ref[rows, cols], keys)
            top = jnp.max(s, axis=1, keepdims=True)
            p = jnp.exp2((s - top) * c).astype(BF)
            acc = dot(p, with_ones(values))
            gate = gate_ref[head]
            remote = acc[:, :DH] * (gate / acc[:, DH:])
            local = local_ref[rows, cols].astype(F32)
            out_ref[rows, cols] = (remote + (1.0 - gate) * local).astype(BF)
        stores[index].start()
    for store in stores:
        store.wait()


def final_attention(gate, queries, kv, local, heads, scale):
    chunks = queries.shape[0] // QB * HALVES
    return pl.pallas_call(
        functools.partial(final_kernel, scale, heads),
        out_shape=pltpu.HBM(queries.shape, BF),
        in_specs=[SMALL, ANY, ANY, ANY],
        out_specs=ANY,
        scratch_shapes=[
            pltpu.VMEM(queries.shape, BF),
            pltpu.VMEM(kv.shape, BF),
            pltpu.VMEM(queries.shape, BF),
            pltpu.VMEM(queries.shape, BF),
            pltpu.SemaphoreType.DMA((chunks, 3)),
            pltpu.SemaphoreType.DMA((chunks,)),
        ],
        compiler_params=params(24),
        cost_estimate=cost(7),
        name="final_attention",
    )(gate, in_hbm(queries), in_hbm(kv), in_hbm(local))


def body(queries, token_keys, token_values, mem_keys, mem_values, retrieved, gate_bias):
    tokens = queries.shape[0]
    heads = gate_bias.shape[0]
    scale = DH ** (-0.5)
    devices = lax.axis_size("seq")
    blocks = mem_keys.shape[0] // MB
    q_blocks = tokens // QB
    wanted = q_blocks * heads * TOPK
    upward = [(i, i + 1) for i in range(devices - 1)]
    downward = [(i, i - 1) for i in range(1, devices)]
    split = FORWARD * DH
    back_q = cut([queries], [(0, split)], heads * DH - split, "cut_queries")
    far_q = lax.ppermute(back_q, "seq", downward)
    ids = retrieved.reshape(-1)
    ids_tile = jnp.zeros((PIECE * DH,), BF).at[:wanted].set(ids.astype(BF)).reshape(PIECE, DH)
    ids_tile, _ = lax.optimization_barrier((ids_tile, back_q))
    sent = pack(mem_keys, mem_values, ids_tile, blocks, heads)
    sent, late_keys, late_values = lax.optimization_barrier((sent, token_keys, token_values))
    tail = tokens - WIN
    ahead_kv = cut([late_keys, late_values], [(tail, 0)] * 2, 2 * split, "cut_tails")
    near_kv = lax.ppermute(ahead_kv, "seq", upward)
    store = lax.all_to_all(sent, "seq", split_axis=0, concat_axis=0, tiled=True)
    gate_share = 1.0 / (1.0 + jnp.exp(-gate_bias))
    first = lax.axis_index("seq").reshape(1).astype(jnp.int32)
    low, lse, local = own_attention(queries, token_keys, token_values, heads, scale)
    far_part = edge_attention(
        functools.partial(far_kernel, scale, heads),
        (far_q, token_keys, token_values),
        heads - FORWARD,
        60,
        "far_attention",
    )
    store, low, lse, local, far_part = lax.optimization_barrier((store, low, lse, local, far_part))
    far = lax.ppermute(far_part, "seq", upward)
    pieces = gather(store, blocks, heads, wanted)
    pieces, late_q = lax.optimization_barrier((pieces, queries))
    kv = lax.all_to_all(pieces, "seq", split_axis=0, concat_axis=0, tiled=True)
    near = edge_attention(
        functools.partial(near_kernel, scale), (late_q, near_kv), FORWARD, 5, "near_attention"
    )
    local = merge(first, low, lse, near, far, local, heads)
    kv, local = lax.optimization_barrier((kv, local))
    return final_attention(gate_share, queries, kv, local, heads, scale)


def solution(mesh):
    in_specs = (
        P("seq", "head"),
        P("seq", "head"),
        P("seq", "head"),
        P("seq", "head"),
        P("seq", "head"),
        P("seq", "head", None),
        P("head"),
    )
    return jax.shard_map(
        body, mesh=mesh, in_specs=in_specs, out_specs=P("seq", "head"), check_vma=False
    )
```

```python
import functools

import jax
import jax.numpy as jnp
from jax import lax
from jax.experimental import pallas as pl
from jax.experimental.pallas import tpu as pltpu
from jax.sharding import PartitionSpec as P

QB = 512
MB = 128
TOPK = 2
WIN = 512
DH = 128
PIECE = 8
EDGE = 256
FORWARD = 5
HALVES = 2
LOG2E = 1.4426950408889634
NEG = -1e30
BF = jnp.bfloat16
F32 = jnp.float32
ANY = pl.BlockSpec(memory_space=pl.ANY)
WHOLE = pl.BlockSpec(memory_space=pltpu.VMEM)
SMALL = pl.BlockSpec(memory_space=pltpu.SMEM)


def params(mebibytes):
    return pltpu.CompilerParams(vmem_limit_bytes=mebibytes << 20)


def cost(micros):
    return pl.CostEstimate(flops=int(micros * 1e9), transcendentals=0, bytes_accessed=0)


def in_hbm(array):
    return pltpu.with_memory_space_constraint(array, pltpu.HBM)


def copy_all(copies):
    for copy in copies:
        copy.start()
    for copy in copies:
        copy.wait()


def cut_kernel(areas, *refs):
    out_ref, sems = refs[-2:]
    width = out_ref.shape[1] // len(areas)
    copies = [
        pltpu.make_async_copy(
            ref.at[pl.ds(row, WIN), pl.ds(col, width)],
            out_ref.at[:, pl.ds(index * width, width)],
            sems.at[index],
        )
        for index, (ref, (row, col)) in enumerate(zip(refs, areas))
    ]
    copy_all(copies)


def cut(arrays, areas, width, name):
    return pl.pallas_call(
        functools.partial(cut_kernel, areas),
        out_shape=jax.ShapeDtypeStruct((WIN, width), BF),
        in_specs=[ANY] * len(arrays),
        out_specs=WHOLE,
        scratch_shapes=[pltpu.SemaphoreType.DMA((len(arrays),))],
        compiler_params=params(4),
        cost_estimate=cost(2),
        name=name,
    )(*map(in_hbm, arrays))


def pack_kernel(blocks, heads, keys_ref, values_ref, ids_ref, out_ref, stage, in_sems, out_sems):
    pieces = MB // PIECE
    loads, stores = [], []
    for half, source in enumerate((keys_ref, values_ref)):
        for block in range(blocks):
            slot = len(loads)
            here = stage.at[pl.ds(slot * pieces, pieces)]
            there = out_ref.at[pl.ds(half * pieces, pieces), pl.ds(block * heads, heads)]
            rows = pl.ds(block * pieces, pieces)
            loads.append(pltpu.make_async_copy(source.at[rows], here, in_sems.at[slot]))
            stores.append(pltpu.make_async_copy(here, there, out_sems.at[slot]))
    ids_store = pltpu.make_async_copy(
        ids_ref, out_ref.at[:, pl.ds(blocks * heads, 1)], out_sems.at[2 * blocks]
    )
    for load in loads:
        load.start()
    ids_store.start()
    for load, store in zip(loads, stores):
        load.wait()
        store.start()
    for store in stores:
        store.wait()
    ids_store.wait()


def tiles(array):
    rows, width = array.shape
    return array.reshape(rows // PIECE, PIECE, width // DH, DH).transpose(0, 2, 1, 3)


def pack(mem_keys, mem_values, ids_tile, blocks, heads):
    devices = 2 * MB // PIECE
    return pl.pallas_call(
        functools.partial(pack_kernel, blocks, heads),
        out_shape=pltpu.HBM((devices, blocks * heads + 1, PIECE, DH), BF),
        in_specs=[ANY, ANY, WHOLE],
        out_specs=ANY,
        scratch_shapes=[
            pltpu.VMEM((2 * blocks * MB // PIECE, heads, PIECE, DH), BF),
            pltpu.SemaphoreType.DMA((2 * blocks,)),
            pltpu.SemaphoreType.DMA((2 * blocks + 1,)),
        ],
        compiler_params=params(8),
        cost_estimate=cost(2),
        name="pack_pieces",
    )(
        in_hbm(tiles(mem_keys)),
        in_hbm(tiles(mem_values)),
        jnp.broadcast_to(ids_tile, (devices, 1, PIECE, DH)),
    )


def gather_kernel(
    blocks, heads, wanted, store_ref, out_ref, ids, rows_v, rows_s, store, stage, ids_sem, sems, out_sems
):
    devices, stride = store_ref.shape[:2]
    parts = sems.shape[0]
    groups = out_sems.shape[0]
    size = devices // groups
    ids_load = pltpu.make_async_copy(store_ref.at[:, stride - 1], ids, ids_sem.at[0])
    ids_load.start()
    loads, stores = [], []
    for part in range(parts):
        span = pl.ds(part * (devices // parts), devices // parts)
        loads.append(pltpu.make_async_copy(store_ref.at[span], store.at[span], sems.at[part]))
    for group in range(groups):
        span = pl.ds(group * size, size)
        stores.append(pltpu.make_async_copy(stage.at[span], out_ref.at[span], out_sems.at[group]))
    for load in loads:
        load.start()
    ids_load.wait()
    row = lax.broadcasted_iota(jnp.int32, (devices, PIECE, DH), 1)
    block = jnp.sum(jnp.where(row == 0, ids[...].astype(F32), 0.0), axis=1).astype(jnp.int32)
    lane = lax.broadcasted_iota(jnp.int32, (devices, DH), 1)
    head = lane // TOPK % heads
    rows_v[...] = block // blocks * stride + block % blocks * heads + head
    rows_copy = pltpu.make_async_copy(rows_v, rows_s, ids_sem.at[1])
    rows_copy.start()
    rows_copy.wait()
    for load in loads:
        load.wait()
    flat = store.reshape(devices * stride, PIECE, DH)
    for group in range(groups):

        @pl.loop(group * size, (group + 1) * size)
        def _(device):
            for request in range(wanted):
                stage[device, request] = flat[rows_s[device, request]]

        stores[group].start()
    for store_copy in stores:
        store_copy.wait()


def gather(store, blocks, heads, wanted):
    devices = store.shape[0]
    return pl.pallas_call(
        functools.partial(gather_kernel, blocks, heads, wanted),
        out_shape=pltpu.HBM((devices, wanted, PIECE, DH), BF),
        in_specs=[ANY],
        out_specs=ANY,
        scratch_shapes=[
            pltpu.VMEM((devices, PIECE, DH), BF),
            pltpu.VMEM((devices, DH), jnp.int32),
            pltpu.SMEM((devices, DH), jnp.int32),
            pltpu.VMEM(store.shape, BF),
            pltpu.VMEM((devices, wanted, PIECE, DH), BF),
            pltpu.SemaphoreType.DMA((2,)),
            pltpu.SemaphoreType.DMA((4,)),
            pltpu.SemaphoreType.DMA((8,)),
        ],
        compiler_params=params(16),
        cost_estimate=cost(6),
        name="gather_pieces",
    )(in_hbm(store))


def dot_t(a, b):
    return lax.dot_general(a, b, (((1,), (1,)), ((), ())), preferred_element_type=F32)


def dot(a, b):
    return jnp.dot(a, b, preferred_element_type=F32)


def with_ones(values):
    return jnp.concatenate([values, jnp.ones_like(values)], axis=1)


def triangle():
    row = lax.broadcasted_iota(jnp.int32, (EDGE, EDGE), 0)
    col = lax.broadcasted_iota(jnp.int32, (EDGE, EDGE), 1)
    return col <= row


def own_kernel(scale, heads, q_ref, k_ref, v_ref, low_ref, lse_ref, out_ref):
    lower = triangle()
    c = scale * LOG2E
    lanes = lax.broadcasted_iota(jnp.int32, (EDGE, DH), 1)
    for head in range(heads):
        cols = pl.ds(head * DH, DH)
        for i in range(WIN // EDGE):
            rows = pl.ds(i * EDGE, EDGE)
            seen = pl.ds(0, (i + 1) * EDGE)
            s = dot_t(q_ref[rows, cols], k_ref[seen, cols])
            diag = jnp.where(lower, s[:, i * EDGE :], NEG)
            if i:
                s = jnp.concatenate([s[:, : i * EDGE], diag], axis=1)
            else:
                s = diag
            top = jnp.max(s, axis=1, keepdims=True)
            p = jnp.exp2((s - top) * c).astype(BF)
            acc = dot(p, with_ones(v_ref[seen, cols]))
            total = acc[:, DH:]
            low_ref[rows, cols] = acc[:, :DH] / total
            lse_ref[rows, :] = jnp.where(lanes == head, top * c + jnp.log2(total), lse_ref[rows, :])
        for i in range(WIN // EDGE, q_ref.shape[0] // EDGE):
            rows = pl.ds(i * EDGE, EDGE)
            seen = pl.ds(i * EDGE - WIN, WIN + EDGE)
            s = dot_t(q_ref[rows, cols], k_ref[seen, cols])
            ends = jnp.where(lower, s[:, WIN:], s[:, :EDGE])
            mid = s[:, EDGE:WIN]
            top = jnp.maximum(
                jnp.max(ends, axis=1, keepdims=True), jnp.max(mid, axis=1, keepdims=True)
            )
            ends = jnp.exp2((ends - top) * c)
            mid = jnp.exp2((mid - top) * c).astype(BF)
            first = jnp.where(lower, 0.0, ends).astype(BF)
            last = jnp.where(lower, ends, 0.0).astype(BF)
            acc = dot(jnp.concatenate([first, mid, last], axis=1), with_ones(v_ref[seen, cols]))
            out_ref[rows, cols] = (acc[:, :DH] / acc[:, DH:]).astype(BF)


def own_attention(queries, keys, values, heads, scale):
    tokens, width = queries.shape
    return pl.pallas_call(
        functools.partial(own_kernel, scale, heads),
        out_shape=(
            jax.ShapeDtypeStruct((WIN, width), F32),
            jax.ShapeDtypeStruct((WIN, DH), F32),
            jax.ShapeDtypeStruct((tokens, width), BF),
        ),
        in_specs=[WHOLE] * 3,
        out_specs=(WHOLE,) * 3,
        compiler_params=params(30),
        cost_estimate=cost(20),
        name="own_attention",
    )(queries, keys, values)


def edge_part(scale, slots, tail, q_ref, k_ref, v_ref, out_ref, lse_ref):
    lower = triangle()
    c = scale * LOG2E
    lanes = lax.broadcasted_iota(jnp.int32, (EDGE, DH), 1)
    count = len(slots)
    lse_ref[...] = jnp.zeros_like(lse_ref)
    for slot, (q_head, k_head, v_head) in enumerate(slots):
        q_cols = pl.ds(q_head * DH, DH)
        k_cols = pl.ds(k_head * DH, DH)
        v_cols = pl.ds(v_head * DH, DH)
        for i in range(WIN // EDGE):
            rows = pl.ds(i * EDGE, EDGE)
            seen = pl.ds(tail + i * EDGE, WIN - i * EDGE)
            s = dot_t(q_ref[rows, q_cols], k_ref[seen, k_cols])
            edge = jnp.where(lower, NEG, s[:, :EDGE])
            if s.shape[1] > EDGE:
                s = jnp.concatenate([edge, s[:, EDGE:]], axis=1)
            else:
                s = edge
            top = jnp.max(s, axis=1, keepdims=True)
            p = jnp.exp2((s - top) * c).astype(BF)
            acc = dot(p, with_ones(v_ref[seen, v_cols]))
            total = acc[:, DH:]
            out_ref[rows, pl.ds(slot * DH, DH)] = (acc[:, :DH] / total).astype(BF)
            lse_ref[rows, :] = jnp.where(lanes == slot, top * c + jnp.log2(total), lse_ref[rows, :])
    stat = lse_ref[...]
    high = stat.astype(BF).astype(F32)
    mid = (stat - high).astype(BF).astype(F32)
    low = (stat - high - mid).astype(BF).astype(F32)
    packed = high + pltpu.roll(mid, count, 1) + pltpu.roll(low, 2 * count, 1)
    out_ref[:, pl.ds(count * DH, DH)] = packed.astype(BF)


def far_kernel(scale, heads, q_ref, k_ref, v_ref, out_ref, lse_ref):
    slots = [(head - FORWARD, head, head) for head in range(FORWARD, heads)]
    edge_part(scale, slots, k_ref.shape[0] - WIN, q_ref, k_ref, v_ref, out_ref, lse_ref)


def near_kernel(scale, q_ref, kv_ref, out_ref, lse_ref):
    slots = [(head, head, FORWARD + head) for head in range(FORWARD)]
    edge_part(scale, slots, 0, q_ref, kv_ref, kv_ref, out_ref, lse_ref)


def edge_attention(kernel, arrays, count, micros, name):
    return pl.pallas_call(
        kernel,
        out_shape=jax.ShapeDtypeStruct((WIN, (count + 1) * DH), BF),
        in_specs=[WHOLE] * len(arrays),
        out_specs=WHOLE,
        scratch_shapes=[pltpu.VMEM((WIN, DH), F32)],
        compiler_params=params(24),
        cost_estimate=cost(micros),
        name=name,
    )(*arrays)


def unpacked(stat, count):
    return stat + pltpu.roll(stat, DH - count, 1) + pltpu.roll(stat, DH - 2 * count, 1)


def merge_kernel(heads, first_ref, low_ref, lse_ref, near_ref, far_ref, into_ref, out_ref):
    del into_ref
    lanes = lax.broadcasted_iota(jnp.int32, (EDGE, DH), 1)
    behind = heads - FORWARD
    for i in range(WIN // EDGE):
        rows = pl.ds(i * EDGE, EDGE)
        near_stat = unpacked(near_ref[rows, pl.ds(FORWARD * DH, DH)].astype(F32), FORWARD)
        far_stat = unpacked(far_ref[rows, pl.ds(behind * DH, DH)].astype(F32), behind)
        other = jnp.where(lanes < FORWARD, near_stat, pltpu.roll(far_stat, FORWARD, 1))
        other = jnp.where(first_ref[0] == 0, NEG, other)
        own = jnp.where(lanes < heads, lse_ref[rows, :], 0.0)
        shares = 1.0 / (1.0 + jnp.exp2(other - own))
        for head in range(heads):
            ref, slot = (near_ref, head) if head < FORWARD else (far_ref, head - FORWARD)
            share = shares[:, head : head + 1]
            cols = pl.ds(head * DH, DH)
            mine = low_ref[rows, cols]
            there = ref[rows, pl.ds(slot * DH, DH)].astype(F32)
            out_ref[rows, cols] = (there + (mine - there) * share).astype(BF)


def merge(first, low, lse, near, far, local, heads):
    width = low.shape[1]
    whole = lambda array: pl.BlockSpec(array.shape, lambda i: (0, 0))
    return pl.pallas_call(
        functools.partial(merge_kernel, heads),
        out_shape=pltpu.HBM(local.shape, BF),
        grid=(1,),
        in_specs=[SMALL, whole(low), whole(lse), whole(near), whole(far), ANY],
        out_specs=pl.BlockSpec((WIN, width), lambda i: (0, 0)),
        input_output_aliases={5: 0},
        compiler_params=params(16),
        cost_estimate=cost(60),
        name="merge_local",
    )(first, low, lse, near, far, in_hbm(local))


def final_kernel(
    scale, heads, gate_ref, q_hbm, kv_hbm, local_hbm, out_hbm, q_ref, kv_ref, local_ref, out_ref, sems, out_sems
):
    c = scale * LOG2E
    pieces = MB // PIECE
    blocks = q_hbm.shape[0] // QB
    step = heads // HALVES
    chunks = [(block, half) for block in range(blocks) for half in range(HALVES)]
    loads, stores = [], []
    for index, (block, half) in enumerate(chunks):
        area = (pl.ds(block * QB, QB), pl.ds(half * step * DH, step * DH))
        mine = (slice(None), pl.ds((block * heads + half * step) * TOPK, step * TOPK))
        loads.append(
            [
                pltpu.make_async_copy(source.at[where], target.at[where], sems.at[index, kind])
                for kind, (source, target, where) in enumerate(
                    ((kv_hbm, kv_ref, mine), (q_hbm, q_ref, area), (local_hbm, local_ref, area))
                )
            ]
        )
        stores.append(pltpu.make_async_copy(out_ref.at[area], out_hbm.at[area], out_sems.at[index]))
    for index in range(2):
        for load in loads[index]:
            load.start()
    for index, (block, half) in enumerate(chunks):
        for load in loads[index]:
            load.wait()
        if index + 2 < len(chunks):
            for load in loads[index + 2]:
                load.start()
        rows = pl.ds(block * QB, QB)
        for head in range(half * step, (half + 1) * step):
            cols = pl.ds(head * DH, DH)
            mine = pl.ds((block * heads + head) * TOPK, TOPK)
            keys = kv_ref[0:pieces, mine].astype(F32).reshape(TOPK * MB, DH).astype(BF)
            values = kv_ref[pieces : 2 * pieces, mine].astype(F32).reshape(TOPK * MB, DH).astype(BF)
            s = dot_t(q_ref[rows, cols], keys)
            top = jnp.max(s, axis=1, keepdims=True)
            p = jnp.exp2((s - top) * c).astype(BF)
            acc = dot(p, with_ones(values))
            gate = gate_ref[head]
            remote = acc[:, :DH] * (gate / acc[:, DH:])
            local = local_ref[rows, cols].astype(F32)
            out_ref[rows, cols] = (remote + (1.0 - gate) * local).astype(BF)
        stores[index].start()
    for store in stores:
        store.wait()


def final_attention(gate, queries, kv, local, heads, scale):
    chunks = queries.shape[0] // QB * HALVES
    return pl.pallas_call(
        functools.partial(final_kernel, scale, heads),
        out_shape=pltpu.HBM(queries.shape, BF),
        in_specs=[SMALL, ANY, ANY, ANY],
        out_specs=ANY,
        scratch_shapes=[
            pltpu.VMEM(queries.shape, BF),
            pltpu.VMEM(kv.shape, BF),
            pltpu.VMEM(queries.shape, BF),
            pltpu.VMEM(queries.shape, BF),
            pltpu.SemaphoreType.DMA((chunks, 3)),
            pltpu.SemaphoreType.DMA((chunks,)),
        ],
        compiler_params=params(24),
        cost_estimate=cost(7),
        name="final_attention",
    )(gate, in_hbm(queries), in_hbm(kv), in_hbm(local))


def body(queries, token_keys, token_values, mem_keys, mem_values, retrieved, gate_bias):
    tokens = queries.shape[0]
    heads = gate_bias.shape[0]
    scale = DH ** (-0.5)
    devices = lax.axis_size("seq")
    blocks = mem_keys.shape[0] // MB
    q_blocks = tokens // QB
    wanted = q_blocks * heads * TOPK
    upward = [(i, i + 1) for i in range(devices - 1)]
    downward = [(i, i - 1) for i in range(1, devices)]
    split = FORWARD * DH
    back_q = cut([queries], [(0, split)], heads * DH - split, "cut_queries")
    far_q = lax.ppermute(back_q, "seq", downward)
    ids = retrieved.reshape(-1)
    ids_tile = jnp.zeros((PIECE * DH,), BF).at[:wanted].set(ids.astype(BF)).reshape(PIECE, DH)
    ids_tile, _ = lax.optimization_barrier((ids_tile, back_q))
    sent = pack(mem_keys, mem_values, ids_tile, blocks, heads)
    sent, late_keys, late_values = lax.optimization_barrier((sent, token_keys, token_values))
    tail = tokens - WIN
    ahead_kv = cut([late_keys, late_values], [(tail, 0)] * 2, 2 * split, "cut_tails")
    near_kv = lax.ppermute(ahead_kv, "seq", upward)
    store = lax.all_to_all(sent, "seq", split_axis=0, concat_axis=0, tiled=True)
    gate_share = 1.0 / (1.0 + jnp.exp(-gate_bias))
    first = lax.axis_index("seq").reshape(1).astype(jnp.int32)
    low, lse, local = own_attention(queries, token_keys, token_values, heads, scale)
    low, far_keys, far_values = lax.optimization_barrier((low, token_keys, token_values))
    far_part = edge_attention(
        functools.partial(far_kernel, scale, heads),
        (far_q, far_keys, far_values),
        heads - FORWARD,
        60,
        "far_attention",
    )
    far = lax.ppermute(far_part, "seq", upward)
    store, low, lse, local, _ = lax.optimization_barrier((store, low, lse, local, far_part))
    pieces = gather(store, blocks, heads, wanted)
    pieces, late_q = lax.optimization_barrier((pieces, queries))
    kv = lax.all_to_all(pieces, "seq", split_axis=0, concat_axis=0, tiled=True)
    near = edge_attention(
        functools.partial(near_kernel, scale), (late_q, near_kv), FORWARD, 5, "near_attention"
    )
    local = merge(first, low, lse, near, far, local, heads)
    kv, local = lax.optimization_barrier((kv, local))
    return final_attention(gate_share, queries, kv, local, heads, scale)


def solution(mesh):
    in_specs = (
        P("seq", "head"),
        P("seq", "head"),
        P("seq", "head"),
        P("seq", "head"),
        P("seq", "head"),
        P("seq", "head", None),
        P("head"),
    )
    return jax.shard_map(
        body, mesh=mesh, in_specs=in_specs, out_specs=P("seq", "head"), check_vma=False
    )
```

```python
import functools

import jax
import jax.numpy as jnp
from jax import lax
from jax.experimental import pallas as pl
from jax.experimental.pallas import tpu as pltpu
from jax.sharding import PartitionSpec as P

QB = 512
MB = 128
TOPK = 2
WIN = 512
DH = 128
PIECE = 8
EDGE = 256
FORWARD = 3
HALVES = 2
LOG2E = 1.4426950408889634
NEG = -1e30
BF = jnp.bfloat16
F32 = jnp.float32
ANY = pl.BlockSpec(memory_space=pl.ANY)
WHOLE = pl.BlockSpec(memory_space=pltpu.VMEM)
SMALL = pl.BlockSpec(memory_space=pltpu.SMEM)


def params(mebibytes):
    return pltpu.CompilerParams(vmem_limit_bytes=mebibytes << 20)


def cost(micros):
    return pl.CostEstimate(flops=int(micros * 1e9), transcendentals=0, bytes_accessed=0)


def in_hbm(array):
    return pltpu.with_memory_space_constraint(array, pltpu.HBM)


def copy_all(copies):
    for copy in copies:
        copy.start()
    for copy in copies:
        copy.wait()


def cut_kernel(areas, *refs):
    out_ref, sems = refs[-2:]
    width = out_ref.shape[1] // len(areas)
    copies = [
        pltpu.make_async_copy(
            ref.at[pl.ds(row, WIN), pl.ds(col, width)],
            out_ref.at[:, pl.ds(index * width, width)],
            sems.at[index],
        )
        for index, (ref, (row, col)) in enumerate(zip(refs, areas))
    ]
    copy_all(copies)


def cut(arrays, areas, width, name):
    return pl.pallas_call(
        functools.partial(cut_kernel, areas),
        out_shape=jax.ShapeDtypeStruct((WIN, width), BF),
        in_specs=[ANY] * len(arrays),
        out_specs=WHOLE,
        scratch_shapes=[pltpu.SemaphoreType.DMA((len(arrays),))],
        compiler_params=params(4),
        cost_estimate=cost(2),
        name=name,
    )(*map(in_hbm, arrays))


def pack_kernel(blocks, heads, keys_ref, values_ref, ids_ref, out_ref, stage, in_sems, out_sems):
    pieces = MB // PIECE
    loads, stores = [], []
    for half, source in enumerate((keys_ref, values_ref)):
        for block in range(blocks):
            slot = len(loads)
            here = stage.at[pl.ds(slot * pieces, pieces)]
            there = out_ref.at[pl.ds(half * pieces, pieces), pl.ds(block * heads, heads)]
            rows = pl.ds(block * pieces, pieces)
            loads.append(pltpu.make_async_copy(source.at[rows], here, in_sems.at[slot]))
            stores.append(pltpu.make_async_copy(here, there, out_sems.at[slot]))
    ids_store = pltpu.make_async_copy(
        ids_ref, out_ref.at[:, pl.ds(blocks * heads, 1)], out_sems.at[2 * blocks]
    )
    for load in loads:
        load.start()
    ids_store.start()
    for load, store in zip(loads, stores):
        load.wait()
        store.start()
    for store in stores:
        store.wait()
    ids_store.wait()


def tiles(array):
    rows, width = array.shape
    return array.reshape(rows // PIECE, PIECE, width // DH, DH).transpose(0, 2, 1, 3)


def pack(mem_keys, mem_values, ids_tile, blocks, heads):
    devices = 2 * MB // PIECE
    return pl.pallas_call(
        functools.partial(pack_kernel, blocks, heads),
        out_shape=pltpu.HBM((devices, blocks * heads + 1, PIECE, DH), BF),
        in_specs=[ANY, ANY, WHOLE],
        out_specs=ANY,
        scratch_shapes=[
            pltpu.VMEM((2 * blocks * MB // PIECE, heads, PIECE, DH), BF),
            pltpu.SemaphoreType.DMA((2 * blocks,)),
            pltpu.SemaphoreType.DMA((2 * blocks + 1,)),
        ],
        compiler_params=params(8),
        cost_estimate=cost(2),
        name="pack_pieces",
    )(
        in_hbm(tiles(mem_keys)),
        in_hbm(tiles(mem_values)),
        jnp.broadcast_to(ids_tile, (devices, 1, PIECE, DH)),
    )


def gather_kernel(
    blocks, heads, wanted, store_ref, out_ref, ids, rows_v, rows_s, store, stage, ids_sem, sems, out_sems
):
    devices, stride = store_ref.shape[:2]
    parts = sems.shape[0]
    groups = out_sems.shape[0]
    size = devices // groups
    ids_load = pltpu.make_async_copy(store_ref.at[:, stride - 1], ids, ids_sem.at[0])
    ids_load.start()
    loads, stores = [], []
    for part in range(parts):
        span = pl.ds(part * (devices // parts), devices // parts)
        loads.append(pltpu.make_async_copy(store_ref.at[span], store.at[span], sems.at[part]))
    for group in range(groups):
        span = pl.ds(group * size, size)
        stores.append(pltpu.make_async_copy(stage.at[span], out_ref.at[span], out_sems.at[group]))
    for load in loads:
        load.start()
    ids_load.wait()
    row = lax.broadcasted_iota(jnp.int32, (devices, PIECE, DH), 1)
    block = jnp.sum(jnp.where(row == 0, ids[...].astype(F32), 0.0), axis=1).astype(jnp.int32)
    lane = lax.broadcasted_iota(jnp.int32, (devices, DH), 1)
    head = lane // TOPK % heads
    rows_v[...] = block // blocks * stride + block % blocks * heads + head
    rows_copy = pltpu.make_async_copy(rows_v, rows_s, ids_sem.at[1])
    rows_copy.start()
    rows_copy.wait()
    for load in loads:
        load.wait()
    flat = store.reshape(devices * stride, PIECE, DH)
    for group in range(groups):

        @pl.loop(group * size, (group + 1) * size)
        def _(device):
            for request in range(wanted):
                stage[device, request] = flat[rows_s[device, request]]

        stores[group].start()
    for store_copy in stores:
        store_copy.wait()


def gather(store, blocks, heads, wanted):
    devices = store.shape[0]
    return pl.pallas_call(
        functools.partial(gather_kernel, blocks, heads, wanted),
        out_shape=pltpu.HBM((devices, wanted, PIECE, DH), BF),
        in_specs=[ANY],
        out_specs=ANY,
        scratch_shapes=[
            pltpu.VMEM((devices, PIECE, DH), BF),
            pltpu.VMEM((devices, DH), jnp.int32),
            pltpu.SMEM((devices, DH), jnp.int32),
            pltpu.VMEM(store.shape, BF),
            pltpu.VMEM((devices, wanted, PIECE, DH), BF),
            pltpu.SemaphoreType.DMA((2,)),
            pltpu.SemaphoreType.DMA((4,)),
            pltpu.SemaphoreType.DMA((8,)),
        ],
        compiler_params=params(16),
        cost_estimate=cost(6),
        name="gather_pieces",
    )(in_hbm(store))


def dot_t(a, b):
    return lax.dot_general(a, b, (((1,), (1,)), ((), ())), preferred_element_type=F32)


def dot(a, b):
    return jnp.dot(a, b, preferred_element_type=F32)


def with_ones(values):
    return jnp.concatenate([values, jnp.ones_like(values)], axis=1)


def triangle():
    row = lax.broadcasted_iota(jnp.int32, (EDGE, EDGE), 0)
    col = lax.broadcasted_iota(jnp.int32, (EDGE, EDGE), 1)
    return col <= row


def own_kernel(scale, heads, q_ref, k_ref, v_ref, low_ref, lse_ref, out_ref):
    lower = triangle()
    c = scale * LOG2E
    lanes = lax.broadcasted_iota(jnp.int32, (EDGE, DH), 1)
    for head in range(heads):
        cols = pl.ds(head * DH, DH)
        for i in range(WIN // EDGE):
            rows = pl.ds(i * EDGE, EDGE)
            seen = pl.ds(0, (i + 1) * EDGE)
            s = dot_t(q_ref[rows, cols], k_ref[seen, cols])
            diag = jnp.where(lower, s[:, i * EDGE :], NEG)
            if i:
                s = jnp.concatenate([s[:, : i * EDGE], diag], axis=1)
            else:
                s = diag
            top = jnp.max(s, axis=1, keepdims=True)
            p = jnp.exp2((s - top) * c).astype(BF)
            acc = dot(p, with_ones(v_ref[seen, cols]))
            total = acc[:, DH:]
            low_ref[rows, cols] = acc[:, :DH] / total
            lse_ref[rows, :] = jnp.where(lanes == head, top * c + jnp.log2(total), lse_ref[rows, :])
        for i in range(WIN // EDGE, q_ref.shape[0] // EDGE):
            rows = pl.ds(i * EDGE, EDGE)
            seen = pl.ds(i * EDGE - WIN, WIN + EDGE)
            s = dot_t(q_ref[rows, cols], k_ref[seen, cols])
            ends = jnp.where(lower, s[:, WIN:], s[:, :EDGE])
            mid = s[:, EDGE:WIN]
            top = jnp.maximum(
                jnp.max(ends, axis=1, keepdims=True), jnp.max(mid, axis=1, keepdims=True)
            )
            ends = jnp.exp2((ends - top) * c)
            mid = jnp.exp2((mid - top) * c).astype(BF)
            first = jnp.where(lower, 0.0, ends).astype(BF)
            last = jnp.where(lower, ends, 0.0).astype(BF)
            acc = dot(jnp.concatenate([first, mid, last], axis=1), with_ones(v_ref[seen, cols]))
            out_ref[rows, cols] = (acc[:, :DH] / acc[:, DH:]).astype(BF)


def own_attention(queries, keys, values, heads, scale):
    tokens, width = queries.shape
    return pl.pallas_call(
        functools.partial(own_kernel, scale, heads),
        out_shape=(
            jax.ShapeDtypeStruct((WIN, width), F32),
            jax.ShapeDtypeStruct((WIN, DH), F32),
            jax.ShapeDtypeStruct((tokens, width), BF),
        ),
        in_specs=[WHOLE] * 3,
        out_specs=(WHOLE,) * 3,
        compiler_params=params(30),
        cost_estimate=cost(20),
        name="own_attention",
    )(queries, keys, values)


def edge_part(scale, slots, tail, q_ref, k_ref, v_ref, out_ref, lse_ref):
    lower = triangle()
    c = scale * LOG2E
    lanes = lax.broadcasted_iota(jnp.int32, (EDGE, DH), 1)
    count = len(slots)
    lse_ref[...] = jnp.zeros_like(lse_ref)
    for slot, (q_head, k_head, v_head) in enumerate(slots):
        q_cols = pl.ds(q_head * DH, DH)
        k_cols = pl.ds(k_head * DH, DH)
        v_cols = pl.ds(v_head * DH, DH)
        for i in range(WIN // EDGE):
            rows = pl.ds(i * EDGE, EDGE)
            seen = pl.ds(tail + i * EDGE, WIN - i * EDGE)
            s = dot_t(q_ref[rows, q_cols], k_ref[seen, k_cols])
            edge = jnp.where(lower, NEG, s[:, :EDGE])
            if s.shape[1] > EDGE:
                s = jnp.concatenate([edge, s[:, EDGE:]], axis=1)
            else:
                s = edge
            top = jnp.max(s, axis=1, keepdims=True)
            p = jnp.exp2((s - top) * c).astype(BF)
            acc = dot(p, with_ones(v_ref[seen, v_cols]))
            total = acc[:, DH:]
            out_ref[rows, pl.ds(slot * DH, DH)] = (acc[:, :DH] / total).astype(BF)
            lse_ref[rows, :] = jnp.where(lanes == slot, top * c + jnp.log2(total), lse_ref[rows, :])
    stat = lse_ref[...]
    high = stat.astype(BF).astype(F32)
    mid = (stat - high).astype(BF).astype(F32)
    low = (stat - high - mid).astype(BF).astype(F32)
    packed = high + pltpu.roll(mid, count, 1) + pltpu.roll(low, 2 * count, 1)
    out_ref[:, pl.ds(count * DH, DH)] = packed.astype(BF)


def far_kernel(scale, heads, q_ref, k_ref, v_ref, out_ref, lse_ref):
    slots = [(head - FORWARD, head, head) for head in range(FORWARD, heads)]
    edge_part(scale, slots, k_ref.shape[0] - WIN, q_ref, k_ref, v_ref, out_ref, lse_ref)


def near_kernel(scale, q_ref, kv_ref, out_ref, lse_ref):
    slots = [(head, head, FORWARD + head) for head in range(FORWARD)]
    edge_part(scale, slots, 0, q_ref, kv_ref, kv_ref, out_ref, lse_ref)


def edge_attention(kernel, arrays, count, micros, name):
    return pl.pallas_call(
        kernel,
        out_shape=jax.ShapeDtypeStruct((WIN, (count + 1) * DH), BF),
        in_specs=[WHOLE] * len(arrays),
        out_specs=WHOLE,
        scratch_shapes=[pltpu.VMEM((WIN, DH), F32)],
        compiler_params=params(24),
        cost_estimate=cost(micros),
        name=name,
    )(*arrays)


def unpacked(stat, count):
    return stat + pltpu.roll(stat, DH - count, 1) + pltpu.roll(stat, DH - 2 * count, 1)


def merge_kernel(heads, first_ref, low_ref, lse_ref, near_ref, far_ref, into_ref, out_ref):
    del into_ref
    lanes = lax.broadcasted_iota(jnp.int32, (EDGE, DH), 1)
    behind = heads - FORWARD
    for i in range(WIN // EDGE):
        rows = pl.ds(i * EDGE, EDGE)
        near_stat = unpacked(near_ref[rows, pl.ds(FORWARD * DH, DH)].astype(F32), FORWARD)
        far_stat = unpacked(far_ref[rows, pl.ds(behind * DH, DH)].astype(F32), behind)
        other = jnp.where(lanes < FORWARD, near_stat, pltpu.roll(far_stat, FORWARD, 1))
        other = jnp.where(first_ref[0] == 0, NEG, other)
        own = jnp.where(lanes < heads, lse_ref[rows, :], 0.0)
        shares = 1.0 / (1.0 + jnp.exp2(other - own))
        for head in range(heads):
            ref, slot = (near_ref, head) if head < FORWARD else (far_ref, head - FORWARD)
            share = shares[:, head : head + 1]
            cols = pl.ds(head * DH, DH)
            mine = low_ref[rows, cols]
            there = ref[rows, pl.ds(slot * DH, DH)].astype(F32)
            out_ref[rows, cols] = (there + (mine - there) * share).astype(BF)


def merge(first, low, lse, near, far, local, heads):
    width = low.shape[1]
    whole = lambda array: pl.BlockSpec(array.shape, lambda i: (0, 0))
    return pl.pallas_call(
        functools.partial(merge_kernel, heads),
        out_shape=pltpu.HBM(local.shape, BF),
        grid=(1,),
        in_specs=[SMALL, whole(low), whole(lse), whole(near), whole(far), ANY],
        out_specs=pl.BlockSpec((WIN, width), lambda i: (0, 0)),
        input_output_aliases={5: 0},
        compiler_params=params(16),
        cost_estimate=cost(60),
        name="merge_local",
    )(first, low, lse, near, far, in_hbm(local))


def final_kernel(
    scale, heads, gate_ref, q_hbm, kv_hbm, local_hbm, out_hbm, q_ref, kv_ref, local_ref, out_ref, sems, out_sems
):
    c = scale * LOG2E
    pieces = MB // PIECE
    blocks = q_hbm.shape[0] // QB
    step = heads // HALVES
    chunks = [(block, half) for block in range(blocks) for half in range(HALVES)]
    loads, stores = [], []
    for index, (block, half) in enumerate(chunks):
        area = (pl.ds(block * QB, QB), pl.ds(half * step * DH, step * DH))
        mine = (slice(None), pl.ds((block * heads + half * step) * TOPK, step * TOPK))
        loads.append(
            [
                pltpu.make_async_copy(source.at[where], target.at[where], sems.at[index, kind])
                for kind, (source, target, where) in enumerate(
                    ((kv_hbm, kv_ref, mine), (q_hbm, q_ref, area), (local_hbm, local_ref, area))
                )
            ]
        )
        stores.append(pltpu.make_async_copy(out_ref.at[area], out_hbm.at[area], out_sems.at[index]))
    for index in range(2):
        for load in loads[index]:
            load.start()
    for index, (block, half) in enumerate(chunks):
        for load in loads[index]:
            load.wait()
        if index + 2 < len(chunks):
            for load in loads[index + 2]:
                load.start()
        rows = pl.ds(block * QB, QB)
        for head in range(half * step, (half + 1) * step):
            cols = pl.ds(head * DH, DH)
            mine = pl.ds((block * heads + head) * TOPK, TOPK)
            keys = kv_ref[0:pieces, mine].astype(F32).reshape(TOPK * MB, DH).astype(BF)
            values = kv_ref[pieces : 2 * pieces, mine].astype(F32).reshape(TOPK * MB, DH).astype(BF)
            s = dot_t(q_ref[rows, cols], keys)
            top = jnp.max(s, axis=1, keepdims=True)
            p = jnp.exp2((s - top) * c).astype(BF)
            acc = dot(p, with_ones(values))
            gate = gate_ref[head]
            remote = acc[:, :DH] * (gate / acc[:, DH:])
            local = local_ref[rows, cols].astype(F32)
            out_ref[rows, cols] = (remote + (1.0 - gate) * local).astype(BF)
        stores[index].start()
    for store in stores:
        store.wait()


def final_attention(gate, queries, kv, local, heads, scale):
    chunks = queries.shape[0] // QB * HALVES
    return pl.pallas_call(
        functools.partial(final_kernel, scale, heads),
        out_shape=pltpu.HBM(queries.shape, BF),
        in_specs=[SMALL, ANY, ANY, ANY],
        out_specs=ANY,
        scratch_shapes=[
            pltpu.VMEM(queries.shape, BF),
            pltpu.VMEM(kv.shape, BF),
            pltpu.VMEM(queries.shape, BF),
            pltpu.VMEM(queries.shape, BF),
            pltpu.SemaphoreType.DMA((chunks, 3)),
            pltpu.SemaphoreType.DMA((chunks,)),
        ],
        compiler_params=params(24),
        cost_estimate=cost(7),
        name="final_attention",
    )(gate, in_hbm(queries), in_hbm(kv), in_hbm(local))


def body(queries, token_keys, token_values, mem_keys, mem_values, retrieved, gate_bias):
    tokens = queries.shape[0]
    heads = gate_bias.shape[0]
    scale = DH ** (-0.5)
    devices = lax.axis_size("seq")
    blocks = mem_keys.shape[0] // MB
    q_blocks = tokens // QB
    wanted = q_blocks * heads * TOPK
    upward = [(i, i + 1) for i in range(devices - 1)]
    downward = [(i, i - 1) for i in range(1, devices)]
    split = FORWARD * DH
    back_q = cut([queries], [(0, split)], heads * DH - split, "cut_queries")
    far_q = lax.ppermute(back_q, "seq", downward)
    ids = retrieved.reshape(-1)
    ids_tile = jnp.zeros((PIECE * DH,), BF).at[:wanted].set(ids.astype(BF)).reshape(PIECE, DH)
    ids_tile, _ = lax.optimization_barrier((ids_tile, back_q))
    sent = pack(mem_keys, mem_values, ids_tile, blocks, heads)
    sent, late_keys, late_values = lax.optimization_barrier((sent, token_keys, token_values))
    tail = tokens - WIN
    ahead_kv = cut([late_keys, late_values], [(tail, 0)] * 2, 2 * split, "cut_tails")
    near_kv = lax.ppermute(ahead_kv, "seq", upward)
    store = lax.all_to_all(sent, "seq", split_axis=0, concat_axis=0, tiled=True)
    gate_share = 1.0 / (1.0 + jnp.exp(-gate_bias))
    first = lax.axis_index("seq").reshape(1).astype(jnp.int32)
    low, lse, local = own_attention(queries, token_keys, token_values, heads, scale)
    low, far_keys, far_values = lax.optimization_barrier((low, token_keys, token_values))
    far_part = edge_attention(
        functools.partial(far_kernel, scale, heads),
        (far_q, far_keys, far_values),
        heads - FORWARD,
        60,
        "far_attention",
    )
    far = lax.ppermute(far_part, "seq", upward)
    store, low, lse, local, _ = lax.optimization_barrier((store, low, lse, local, far_part))
    pieces = gather(store, blocks, heads, wanted)
    pieces, late_q = lax.optimization_barrier((pieces, queries))
    kv = lax.all_to_all(pieces, "seq", split_axis=0, concat_axis=0, tiled=True)
    near = edge_attention(
        functools.partial(near_kernel, scale), (late_q, near_kv), FORWARD, 5, "near_attention"
    )
    local = merge(first, low, lse, near, far, local, heads)
    kv, local = lax.optimization_barrier((kv, local))
    return final_attention(gate_share, queries, kv, local, heads, scale)


def solution(mesh):
    in_specs = (
        P("seq", "head"),
        P("seq", "head"),
        P("seq", "head"),
        P("seq", "head"),
        P("seq", "head"),
        P("seq", "head", None),
        P("head"),
    )
    return jax.shard_map(
        body, mesh=mesh, in_specs=in_specs, out_specs=P("seq", "head"), check_vma=False
    )
```

```python
import functools

import jax
import jax.numpy as jnp
from jax import lax
from jax.experimental import pallas as pl
from jax.experimental.pallas import tpu as pltpu
from jax.sharding import PartitionSpec as P

QB = 512
MB = 128
TOPK = 2
WIN = 512
DH = 128
PIECE = 8
EDGE = 256
FORWARD = 5
HALVES = 2
DEPTH = 2
LOG2E = 1.4426950408889634
NEG = -1e30
BF = jnp.bfloat16
F32 = jnp.float32
ANY = pl.BlockSpec(memory_space=pl.ANY)
WHOLE = pl.BlockSpec(memory_space=pltpu.VMEM)
SMALL = pl.BlockSpec(memory_space=pltpu.SMEM)


def params(mebibytes):
    return pltpu.CompilerParams(vmem_limit_bytes=mebibytes << 20)


def cost(micros):
    return pl.CostEstimate(flops=int(micros * 1e9), transcendentals=0, bytes_accessed=0)


def in_hbm(array):
    return pltpu.with_memory_space_constraint(array, pltpu.HBM)


def copy_all(copies):
    for copy in copies:
        copy.start()
    for copy in copies:
        copy.wait()


def edges_kernel(q_ref, k_ref, v_ref, back_ref, ahead_ref, sems):
    split = FORWARD * DH
    tail = pl.ds(k_ref.shape[0] - WIN, WIN)
    width = q_ref.shape[1] - split
    copy_all(
        [
            pltpu.make_async_copy(
                q_ref.at[pl.ds(0, WIN), pl.ds(split, width)], back_ref, sems.at[0]
            ),
            pltpu.make_async_copy(
                k_ref.at[tail, pl.ds(0, split)], ahead_ref.at[:, pl.ds(0, split)], sems.at[1]
            ),
            pltpu.make_async_copy(
                v_ref.at[tail, pl.ds(0, split)], ahead_ref.at[:, pl.ds(split, split)], sems.at[2]
            ),
        ]
    )


def edges(queries, keys, values):
    split = FORWARD * DH
    return pl.pallas_call(
        edges_kernel,
        out_shape=(
            jax.ShapeDtypeStruct((WIN, queries.shape[1] - split), BF),
            jax.ShapeDtypeStruct((WIN, 2 * split), BF),
        ),
        in_specs=[ANY] * 3,
        out_specs=(WHOLE, WHOLE),
        scratch_shapes=[pltpu.SemaphoreType.DMA((3,))],
        compiler_params=params(8),
        cost_estimate=cost(2),
        name="cut_edges",
    )(in_hbm(queries), in_hbm(keys), in_hbm(values))


def pack_kernel(blocks, heads, keys_ref, values_ref, ids_ref, out_ref, stage, in_sems, out_sems):
    pieces = MB // PIECE
    loads, stores = [], []
    for half, source in enumerate((keys_ref, values_ref)):
        for block in range(blocks):
            slot = len(loads)
            here = stage.at[pl.ds(slot * pieces, pieces)]
            there = out_ref.at[pl.ds(half * pieces, pieces), pl.ds(block * heads, heads)]
            rows = pl.ds(block * pieces, pieces)
            loads.append(pltpu.make_async_copy(source.at[rows], here, in_sems.at[slot]))
            stores.append(pltpu.make_async_copy(here, there, out_sems.at[slot]))
    ids_store = pltpu.make_async_copy(
        ids_ref, out_ref.at[:, pl.ds(blocks * heads, 1)], out_sems.at[2 * blocks]
    )
    for load in loads:
        load.start()
    ids_store.start()
    for load, store in zip(loads, stores):
        load.wait()
        store.start()
    for store in stores:
        store.wait()
    ids_store.wait()


def tiles(array):
    rows, width = array.shape
    return array.reshape(rows // PIECE, PIECE, width // DH, DH).transpose(0, 2, 1, 3)


def pack(mem_keys, mem_values, ids_tile, blocks, heads):
    devices = 2 * MB // PIECE
    return pl.pallas_call(
        functools.partial(pack_kernel, blocks, heads),
        out_shape=pltpu.HBM((devices, blocks * heads + 1, PIECE, DH), BF),
        in_specs=[ANY, ANY, WHOLE],
        out_specs=ANY,
        scratch_shapes=[
            pltpu.VMEM((2 * blocks * MB // PIECE, heads, PIECE, DH), BF),
            pltpu.SemaphoreType.DMA((2 * blocks,)),
            pltpu.SemaphoreType.DMA((2 * blocks + 1,)),
        ],
        compiler_params=params(8),
        cost_estimate=cost(2),
        name="pack_pieces",
    )(
        in_hbm(tiles(mem_keys)),
        in_hbm(tiles(mem_values)),
        jnp.broadcast_to(ids_tile, (devices, 1, PIECE, DH)),
    )


def gather_kernel(
    blocks, heads, wanted, store_ref, out_ref, ids, rows_v, rows_s, store, stage, ids_sem, sems, out_sems
):
    devices, stride = store_ref.shape[:2]
    parts = sems.shape[0]
    groups = out_sems.shape[0]
    size = devices // groups
    ids_load = pltpu.make_async_copy(store_ref.at[:, stride - 1], ids, ids_sem.at[0])
    ids_load.start()
    loads, stores = [], []
    for part in range(parts):
        span = pl.ds(part * (devices // parts), devices // parts)
        loads.append(pltpu.make_async_copy(store_ref.at[span], store.at[span], sems.at[part]))
    for group in range(groups):
        span = pl.ds(group * size, size)
        stores.append(pltpu.make_async_copy(stage.at[span], out_ref.at[span], out_sems.at[group]))
    for load in loads:
        load.start()
    ids_load.wait()
    row = lax.broadcasted_iota(jnp.int32, (devices, PIECE, DH), 1)
    block = jnp.sum(jnp.where(row == 0, ids[...].astype(F32), 0.0), axis=1).astype(jnp.int32)
    lane = lax.broadcasted_iota(jnp.int32, (devices, DH), 1)
    head = lane // TOPK % heads
    rows_v[...] = block // blocks * stride + block % blocks * heads + head
    rows_copy = pltpu.make_async_copy(rows_v, rows_s, ids_sem.at[1])
    rows_copy.start()
    rows_copy.wait()
    for load in loads:
        load.wait()
    flat = store.reshape(devices * stride, PIECE, DH)
    for group in range(groups):

        @pl.loop(group * size, (group + 1) * size)
        def _(device):
            for request in range(wanted):
                stage[device, request] = flat[rows_s[device, request]]

        stores[group].start()
    for store_copy in stores:
        store_copy.wait()


def gather(store, blocks, heads, wanted):
    devices = store.shape[0]
    return pl.pallas_call(
        functools.partial(gather_kernel, blocks, heads, wanted),
        out_shape=pltpu.HBM((devices, wanted, PIECE, DH), BF),
        in_specs=[ANY],
        out_specs=ANY,
        scratch_shapes=[
            pltpu.VMEM((devices, PIECE, DH), BF),
            pltpu.VMEM((devices, DH), jnp.int32),
            pltpu.SMEM((devices, DH), jnp.int32),
            pltpu.VMEM(store.shape, BF),
            pltpu.VMEM((devices, wanted, PIECE, DH), BF),
            pltpu.SemaphoreType.DMA((2,)),
            pltpu.SemaphoreType.DMA((4,)),
            pltpu.SemaphoreType.DMA((8,)),
        ],
        compiler_params=params(16),
        cost_estimate=cost(6),
        name="gather_pieces",
    )(in_hbm(store))


def dot_t(a, b):
    return lax.dot_general(a, b, (((1,), (1,)), ((), ())), preferred_element_type=F32)


def dot(a, b):
    return jnp.dot(a, b, preferred_element_type=F32)


def with_ones(values):
    return jnp.concatenate([values, jnp.ones_like(values)], axis=1)


def triangle():
    row = lax.broadcasted_iota(jnp.int32, (EDGE, EDGE), 0)
    col = lax.broadcasted_iota(jnp.int32, (EDGE, EDGE), 1)
    return col <= row


def own_kernel(scale, heads, q_ref, k_ref, v_ref, low_ref, lse_ref, out_ref):
    lower = triangle()
    c = scale * LOG2E
    lanes = lax.broadcasted_iota(jnp.int32, (EDGE, DH), 1)
    for head in range(heads):
        cols = pl.ds(head * DH, DH)
        for i in range(WIN // EDGE):
            rows = pl.ds(i * EDGE, EDGE)
            seen = pl.ds(0, (i + 1) * EDGE)
            s = dot_t(q_ref[rows, cols], k_ref[seen, cols])
            diag = jnp.where(lower, s[:, i * EDGE :], NEG)
            if i:
                s = jnp.concatenate([s[:, : i * EDGE], diag], axis=1)
            else:
                s = diag
            top = jnp.max(s, axis=1, keepdims=True)
            p = jnp.exp2((s - top) * c).astype(BF)
            acc = dot(p, with_ones(v_ref[seen, cols]))
            total = acc[:, DH:]
            low_ref[rows, cols] = acc[:, :DH] / total
            lse_ref[rows, :] = jnp.where(lanes == head, top * c + jnp.log2(total), lse_ref[rows, :])
        for i in range(WIN // EDGE, q_ref.shape[0] // EDGE):
            rows = pl.ds(i * EDGE, EDGE)
            seen = pl.ds(i * EDGE - WIN, WIN + EDGE)
            s = dot_t(q_ref[rows, cols], k_ref[seen, cols])
            ends = jnp.where(lower, s[:, WIN:], s[:, :EDGE])
            mid = s[:, EDGE:WIN]
            top = jnp.maximum(
                jnp.max(ends, axis=1, keepdims=True), jnp.max(mid, axis=1, keepdims=True)
            )
            ends = jnp.exp2((ends - top) * c)
            mid = jnp.exp2((mid - top) * c).astype(BF)
            first = jnp.where(lower, 0.0, ends).astype(BF)
            last = jnp.where(lower, ends, 0.0).astype(BF)
            acc = dot(jnp.concatenate([first, mid, last], axis=1), with_ones(v_ref[seen, cols]))
            out_ref[rows, cols] = (acc[:, :DH] / acc[:, DH:]).astype(BF)


def own_attention(queries, keys, values, heads, scale):
    tokens, width = queries.shape
    return pl.pallas_call(
        functools.partial(own_kernel, scale, heads),
        out_shape=(
            jax.ShapeDtypeStruct((WIN, width), F32),
            jax.ShapeDtypeStruct((WIN, DH), F32),
            jax.ShapeDtypeStruct((tokens, width), BF),
        ),
        in_specs=[WHOLE] * 3,
        out_specs=(WHOLE,) * 3,
        compiler_params=params(30),
        cost_estimate=cost(1),
        name="own_attention",
    )(queries, keys, values)


def edge_part(scale, slots, tail, q_ref, k_ref, v_ref, out_ref, lse_ref):
    lower = triangle()
    c = scale * LOG2E
    lanes = lax.broadcasted_iota(jnp.int32, (EDGE, DH), 1)
    count = len(slots)
    lse_ref[...] = jnp.zeros_like(lse_ref)
    for slot, (q_head, k_head, v_head) in enumerate(slots):
        q_cols = pl.ds(q_head * DH, DH)
        k_cols = pl.ds(k_head * DH, DH)
        v_cols = pl.ds(v_head * DH, DH)
        for i in range(WIN // EDGE):
            rows = pl.ds(i * EDGE, EDGE)
            seen = pl.ds(tail + i * EDGE, WIN - i * EDGE)
            s = dot_t(q_ref[rows, q_cols], k_ref[seen, k_cols])
            edge = jnp.where(lower, NEG, s[:, :EDGE])
            if s.shape[1] > EDGE:
                s = jnp.concatenate([edge, s[:, EDGE:]], axis=1)
            else:
                s = edge
            top = jnp.max(s, axis=1, keepdims=True)
            p = jnp.exp2((s - top) * c).astype(BF)
            acc = dot(p, with_ones(v_ref[seen, v_cols]))
            total = acc[:, DH:]
            out_ref[rows, pl.ds(slot * DH, DH)] = (acc[:, :DH] / total).astype(BF)
            lse_ref[rows, :] = jnp.where(lanes == slot, top * c + jnp.log2(total), lse_ref[rows, :])
    stat = lse_ref[...]
    high = stat.astype(BF).astype(F32)
    mid = (stat - high).astype(BF).astype(F32)
    low = (stat - high - mid).astype(BF).astype(F32)
    packed = high + pltpu.roll(mid, count, 1) + pltpu.roll(low, 2 * count, 1)
    out_ref[:, pl.ds(count * DH, DH)] = packed.astype(BF)


def edge_kernel(
    scale, heads, far_q_ref, near_kv_ref, q_ref, k_ref, v_ref, far_ref, near_ref, lse_ref
):
    far = [(head - FORWARD, head, head) for head in range(FORWARD, heads)]
    near = [(head, head, FORWARD + head) for head in range(FORWARD)]
    tail = k_ref.shape[0] - WIN
    edge_part(scale, far, tail, far_q_ref, k_ref, v_ref, far_ref, lse_ref)
    edge_part(scale, near, 0, q_ref, near_kv_ref, near_kv_ref, near_ref, lse_ref)


def edge_attention(far_q, near_kv, queries, keys, values, heads, scale):
    return pl.pallas_call(
        functools.partial(edge_kernel, scale, heads),
        out_shape=(
            jax.ShapeDtypeStruct((WIN, (heads - FORWARD + 1) * DH), BF),
            jax.ShapeDtypeStruct((WIN, (FORWARD + 1) * DH), BF),
        ),
        in_specs=[WHOLE] * 5,
        out_specs=(WHOLE,) * 2,
        scratch_shapes=[pltpu.VMEM((WIN, DH), F32)],
        compiler_params=params(24),
        cost_estimate=cost(60),
        name="edge_attention",
    )(far_q, near_kv, queries, keys, values)


def unpacked(stat, count):
    return stat + pltpu.roll(stat, DH - count, 1) + pltpu.roll(stat, DH - 2 * count, 1)


def merge_kernel(heads, first_ref, low_ref, lse_ref, near_ref, far_ref, into_ref, out_ref):
    del into_ref
    lanes = lax.broadcasted_iota(jnp.int32, (EDGE, DH), 1)
    behind = heads - FORWARD
    for i in range(WIN // EDGE):
        rows = pl.ds(i * EDGE, EDGE)
        near_stat = unpacked(near_ref[rows, pl.ds(FORWARD * DH, DH)].astype(F32), FORWARD)
        far_stat = unpacked(far_ref[rows, pl.ds(behind * DH, DH)].astype(F32), behind)
        other = jnp.where(lanes < FORWARD, near_stat, pltpu.roll(far_stat, FORWARD, 1))
        other = jnp.where(first_ref[0] == 0, NEG, other)
        own = jnp.where(lanes < heads, lse_ref[rows, :], 0.0)
        shares = 1.0 / (1.0 + jnp.exp2(other - own))
        for head in range(heads):
            ref, slot = (near_ref, head) if head < FORWARD else (far_ref, head - FORWARD)
            share = shares[:, head : head + 1]
            cols = pl.ds(head * DH, DH)
            mine = low_ref[rows, cols]
            there = ref[rows, pl.ds(slot * DH, DH)].astype(F32)
            out_ref[rows, cols] = (there + (mine - there) * share).astype(BF)


def merge(first, low, lse, near, far, local, heads):
    width = low.shape[1]
    whole = lambda array: pl.BlockSpec(array.shape, lambda i: (0, 0))
    return pl.pallas_call(
        functools.partial(merge_kernel, heads),
        out_shape=pltpu.HBM(local.shape, BF),
        grid=(1,),
        in_specs=[SMALL, whole(low), whole(lse), whole(near), whole(far), ANY],
        out_specs=pl.BlockSpec((WIN, width), lambda i: (0, 0)),
        input_output_aliases={5: 0},
        compiler_params=params(16),
        cost_estimate=cost(60),
        name="merge_local",
    )(first, low, lse, near, far, in_hbm(local))


def final_kernel(
    scale, heads, gate_ref, q_hbm, kv_hbm, local_hbm, out_hbm, q_ref, kv_ref, local_ref, out_ref, sems, out_sems
):
    c = scale * LOG2E
    pieces = MB // PIECE
    blocks = q_hbm.shape[0] // QB
    step = heads // HALVES
    chunks = [(block, half) for block in range(blocks) for half in range(HALVES)]
    loads, stores = [], []
    for index, (block, half) in enumerate(chunks):
        area = (pl.ds(block * QB, QB), pl.ds(half * step * DH, step * DH))
        mine = (slice(None), pl.ds((block * heads + half * step) * TOPK, step * TOPK))
        loads.append(
            [
                pltpu.make_async_copy(source.at[where], target.at[where], sems.at[index, kind])
                for kind, (source, target, where) in enumerate(
                    ((kv_hbm, kv_ref, mine), (q_hbm, q_ref, area), (local_hbm, local_ref, area))
                )
            ]
        )
        stores.append(pltpu.make_async_copy(out_ref.at[area], out_hbm.at[area], out_sems.at[index]))
    for index in range(DEPTH):
        for load in loads[index]:
            load.start()
    for index, (block, half) in enumerate(chunks):
        for load in loads[index]:
            load.wait()
        if index + DEPTH < len(chunks):
            for load in loads[index + DEPTH]:
                load.start()
        rows = pl.ds(block * QB, QB)
        for head in range(half * step, (half + 1) * step):
            cols = pl.ds(head * DH, DH)
            mine = pl.ds((block * heads + head) * TOPK, TOPK)
            keys = kv_ref[0:pieces, mine].astype(F32).reshape(TOPK * MB, DH).astype(BF)
            values = kv_ref[pieces : 2 * pieces, mine].astype(F32).reshape(TOPK * MB, DH).astype(BF)
            s = dot_t(q_ref[rows, cols], keys)
            top = jnp.max(s, axis=1, keepdims=True)
            p = jnp.exp2((s - top) * c).astype(BF)
            acc = dot(p, with_ones(values))
            gate = gate_ref[head]
            remote = acc[:, :DH] * (gate / acc[:, DH:])
            local = local_ref[rows, cols].astype(F32)
            out_ref[rows, cols] = (remote + (1.0 - gate) * local).astype(BF)
        stores[index].start()
    for store in stores:
        store.wait()


def final_attention(gate, queries, kv, local, heads, scale):
    chunks = queries.shape[0] // QB * HALVES
    return pl.pallas_call(
        functools.partial(final_kernel, scale, heads),
        out_shape=pltpu.HBM(queries.shape, BF),
        in_specs=[SMALL, ANY, ANY, ANY],
        out_specs=ANY,
        scratch_shapes=[
            pltpu.VMEM(queries.shape, BF),
            pltpu.VMEM(kv.shape, BF),
            pltpu.VMEM(queries.shape, BF),
            pltpu.VMEM(queries.shape, BF),
            pltpu.SemaphoreType.DMA((chunks, 3)),
            pltpu.SemaphoreType.DMA((chunks,)),
        ],
        compiler_params=params(24),
        cost_estimate=cost(7),
        name="final_attention",
    )(gate, in_hbm(queries), in_hbm(kv), in_hbm(local))


def body(queries, token_keys, token_values, mem_keys, mem_values, retrieved, gate_bias):
    tokens = queries.shape[0]
    heads = gate_bias.shape[0]
    scale = DH ** (-0.5)
    devices = lax.axis_size("seq")
    blocks = mem_keys.shape[0] // MB
    q_blocks = tokens // QB
    wanted = q_blocks * heads * TOPK
    upward = [(i, i + 1) for i in range(devices - 1)]
    downward = [(i, i - 1) for i in range(1, devices)]
    back_q, ahead_kv = edges(queries, token_keys, token_values)
    far_q = lax.ppermute(back_q, "seq", downward)
    near_kv = lax.ppermute(ahead_kv, "seq", upward)
    ids = retrieved.reshape(-1)
    ids_tile = jnp.zeros((PIECE * DH,), BF).at[:wanted].set(ids.astype(BF)).reshape(PIECE, DH)
    ids_tile, _ = lax.optimization_barrier((ids_tile, back_q))
    sent = pack(mem_keys, mem_values, ids_tile, blocks, heads)
    store = lax.all_to_all(sent, "seq", split_axis=0, concat_axis=0, tiled=True)
    gate_share = 1.0 / (1.0 + jnp.exp(-gate_bias))
    first = lax.axis_index("seq").reshape(1).astype(jnp.int32)
    low, lse, local = own_attention(queries, token_keys, token_values, heads, scale)
    low, edge_q, edge_k, edge_v = lax.optimization_barrier(
        (low, queries, token_keys, token_values)
    )
    far_part, near = edge_attention(far_q, near_kv, edge_q, edge_k, edge_v, heads, scale)
    far = lax.ppermute(far_part, "seq", upward)
    store, low, lse, local, near, _ = lax.optimization_barrier(
        (store, low, lse, local, near, far_part)
    )
    pieces = gather(store, blocks, heads, wanted)
    kv = lax.all_to_all(pieces, "seq", split_axis=0, concat_axis=0, tiled=True)
    local = merge(first, low, lse, near, far, local, heads)
    kv, local = lax.optimization_barrier((kv, local))
    return final_attention(gate_share, queries, kv, local, heads, scale)


def solution(mesh):
    in_specs = (
        P("seq", "head"),
        P("seq", "head"),
        P("seq", "head"),
        P("seq", "head"),
        P("seq", "head"),
        P("seq", "head", None),
        P("head"),
    )
    return jax.shard_map(
        body, mesh=mesh, in_specs=in_specs, out_specs=P("seq", "head"), check_vma=False
    )
```

```python
import functools

import jax
import jax.numpy as jnp
from jax import lax
from jax.experimental import pallas as pl
from jax.experimental.pallas import tpu as pltpu
from jax.sharding import PartitionSpec as P

QB = 512
MB = 128
TOPK = 2
WIN = 512
DH = 128
PIECE = 8
EDGE = 256
FORWARD = 4
HALVES = 2
DEPTH = 2
LOG2E = 1.4426950408889634
NEG = -1e30
BF = jnp.bfloat16
F32 = jnp.float32
ANY = pl.BlockSpec(memory_space=pl.ANY)
WHOLE = pl.BlockSpec(memory_space=pltpu.VMEM)
SMALL = pl.BlockSpec(memory_space=pltpu.SMEM)


def params(mebibytes):
    return pltpu.CompilerParams(vmem_limit_bytes=mebibytes << 20)


def cost(micros):
    return pl.CostEstimate(flops=int(micros * 1e9), transcendentals=0, bytes_accessed=0)


def in_hbm(array):
    return pltpu.with_memory_space_constraint(array, pltpu.HBM)


def copy_all(copies):
    for copy in copies:
        copy.start()
    for copy in copies:
        copy.wait()


def cut_kernel(areas, *refs):
    out_ref, sems = refs[-2:]
    width = out_ref.shape[1] // len(areas)
    copies = [
        pltpu.make_async_copy(
            ref.at[pl.ds(row, WIN), pl.ds(col, width)],
            out_ref.at[:, pl.ds(index * width, width)],
            sems.at[index],
        )
        for index, (ref, (row, col)) in enumerate(zip(refs, areas))
    ]
    copy_all(copies)


def cut(arrays, areas, width, name):
    return pl.pallas_call(
        functools.partial(cut_kernel, areas),
        out_shape=jax.ShapeDtypeStruct((WIN, width), BF),
        in_specs=[ANY] * len(arrays),
        out_specs=WHOLE,
        scratch_shapes=[pltpu.SemaphoreType.DMA((len(arrays),))],
        compiler_params=params(4),
        cost_estimate=cost(2),
        name=name,
    )(*map(in_hbm, arrays))


def pack_kernel(blocks, heads, keys_ref, values_ref, ids_ref, out_ref, stage, in_sems, out_sems):
    pieces = MB // PIECE
    loads, stores = [], []
    for half, source in enumerate((keys_ref, values_ref)):
        for block in range(blocks):
            slot = len(loads)
            here = stage.at[pl.ds(slot * pieces, pieces)]
            there = out_ref.at[pl.ds(half * pieces, pieces), pl.ds(block * heads, heads)]
            rows = pl.ds(block * pieces, pieces)
            loads.append(pltpu.make_async_copy(source.at[rows], here, in_sems.at[slot]))
            stores.append(pltpu.make_async_copy(here, there, out_sems.at[slot]))
    ids_store = pltpu.make_async_copy(
        ids_ref, out_ref.at[:, pl.ds(blocks * heads, 1)], out_sems.at[2 * blocks]
    )
    for load in loads:
        load.start()
    ids_store.start()
    for load, store in zip(loads, stores):
        load.wait()
        store.start()
    for store in stores:
        store.wait()
    ids_store.wait()


def tiles(array):
    rows, width = array.shape
    return array.reshape(rows // PIECE, PIECE, width // DH, DH).transpose(0, 2, 1, 3)


def pack(mem_keys, mem_values, ids_tile, blocks, heads):
    devices = 2 * MB // PIECE
    return pl.pallas_call(
        functools.partial(pack_kernel, blocks, heads),
        out_shape=pltpu.HBM((devices, blocks * heads + 1, PIECE, DH), BF),
        in_specs=[ANY, ANY, WHOLE],
        out_specs=ANY,
        scratch_shapes=[
            pltpu.VMEM((2 * blocks * MB // PIECE, heads, PIECE, DH), BF),
            pltpu.SemaphoreType.DMA((2 * blocks,)),
            pltpu.SemaphoreType.DMA((2 * blocks + 1,)),
        ],
        compiler_params=params(8),
        cost_estimate=cost(2),
        name="pack_pieces",
    )(
        in_hbm(tiles(mem_keys)),
        in_hbm(tiles(mem_values)),
        jnp.broadcast_to(ids_tile, (devices, 1, PIECE, DH)),
    )


def gather_kernel(
    blocks, heads, wanted, store_ref, out_ref, ids, rows_v, rows_s, store, stage, ids_sem, sems, out_sems
):
    devices, stride = store_ref.shape[:2]
    parts = sems.shape[0]
    groups = out_sems.shape[0]
    size = devices // groups
    ids_load = pltpu.make_async_copy(store_ref.at[:, stride - 1], ids, ids_sem.at[0])
    ids_load.start()
    loads, stores = [], []
    for part in range(parts):
        span = pl.ds(part * (devices // parts), devices // parts)
        loads.append(pltpu.make_async_copy(store_ref.at[span], store.at[span], sems.at[part]))
    for group in range(groups):
        span = pl.ds(group * size, size)
        stores.append(pltpu.make_async_copy(stage.at[span], out_ref.at[span], out_sems.at[group]))
    for load in loads:
        load.start()
    ids_load.wait()
    row = lax.broadcasted_iota(jnp.int32, (devices, PIECE, DH), 1)
    block = jnp.sum(jnp.where(row == 0, ids[...].astype(F32), 0.0), axis=1).astype(jnp.int32)
    lane = lax.broadcasted_iota(jnp.int32, (devices, DH), 1)
    head = lane // TOPK % heads
    rows_v[...] = block // blocks * stride + block % blocks * heads + head
    rows_copy = pltpu.make_async_copy(rows_v, rows_s, ids_sem.at[1])
    rows_copy.start()
    rows_copy.wait()
    for load in loads:
        load.wait()
    flat = store.reshape(devices * stride, PIECE, DH)
    for group in range(groups):

        @pl.loop(group * size, (group + 1) * size)
        def _(device):
            for request in range(wanted):
                stage[device, request] = flat[rows_s[device, request]]

        stores[group].start()
    for store_copy in stores:
        store_copy.wait()


def gather(store, blocks, heads, wanted):
    devices = store.shape[0]
    return pl.pallas_call(
        functools.partial(gather_kernel, blocks, heads, wanted),
        out_shape=pltpu.HBM((devices, wanted, PIECE, DH), BF),
        in_specs=[ANY],
        out_specs=ANY,
        scratch_shapes=[
            pltpu.VMEM((devices, PIECE, DH), BF),
            pltpu.VMEM((devices, DH), jnp.int32),
            pltpu.SMEM((devices, DH), jnp.int32),
            pltpu.VMEM(store.shape, BF),
            pltpu.VMEM((devices, wanted, PIECE, DH), BF),
            pltpu.SemaphoreType.DMA((2,)),
            pltpu.SemaphoreType.DMA((4,)),
            pltpu.SemaphoreType.DMA((8,)),
        ],
        compiler_params=params(16),
        cost_estimate=cost(6),
        name="gather_pieces",
    )(in_hbm(store))


def dot_t(a, b):
    return lax.dot_general(a, b, (((1,), (1,)), ((), ())), preferred_element_type=F32)


def dot(a, b):
    return jnp.dot(a, b, preferred_element_type=F32)


def with_ones(values):
    return jnp.concatenate([values, jnp.ones_like(values)], axis=1)


def triangle():
    row = lax.broadcasted_iota(jnp.int32, (EDGE, EDGE), 0)
    col = lax.broadcasted_iota(jnp.int32, (EDGE, EDGE), 1)
    return col <= row


def own_kernel(scale, heads, q_ref, k_ref, v_ref, low_ref, lse_ref, out_ref):
    lower = triangle()
    c = scale * LOG2E
    lanes = lax.broadcasted_iota(jnp.int32, (EDGE, DH), 1)
    for head in range(heads):
        cols = pl.ds(head * DH, DH)
        for i in range(WIN // EDGE):
            rows = pl.ds(i * EDGE, EDGE)
            seen = pl.ds(0, (i + 1) * EDGE)
            s = dot_t(q_ref[rows, cols], k_ref[seen, cols])
            diag = jnp.where(lower, s[:, i * EDGE :], NEG)
            if i:
                s = jnp.concatenate([s[:, : i * EDGE], diag], axis=1)
            else:
                s = diag
            top = jnp.max(s, axis=1, keepdims=True)
            p = jnp.exp2((s - top) * c).astype(BF)
            acc = dot(p, with_ones(v_ref[seen, cols]))
            total = acc[:, DH:]
            low_ref[rows, cols] = acc[:, :DH] / total
            lse_ref[rows, :] = jnp.where(lanes == head, top * c + jnp.log2(total), lse_ref[rows, :])
        for i in range(WIN // EDGE, q_ref.shape[0] // EDGE):
            rows = pl.ds(i * EDGE, EDGE)
            seen = pl.ds(i * EDGE - WIN, WIN + EDGE)
            s = dot_t(q_ref[rows, cols], k_ref[seen, cols])
            ends = jnp.where(lower, s[:, WIN:], s[:, :EDGE])
            mid = s[:, EDGE:WIN]
            top = jnp.maximum(
                jnp.max(ends, axis=1, keepdims=True), jnp.max(mid, axis=1, keepdims=True)
            )
            ends = jnp.exp2((ends - top) * c)
            mid = jnp.exp2((mid - top) * c).astype(BF)
            first = jnp.where(lower, 0.0, ends).astype(BF)
            last = jnp.where(lower, ends, 0.0).astype(BF)
            acc = dot(jnp.concatenate([first, mid, last], axis=1), with_ones(v_ref[seen, cols]))
            out_ref[rows, cols] = (acc[:, :DH] / acc[:, DH:]).astype(BF)


def own_attention(queries, keys, values, heads, scale):
    tokens, width = queries.shape
    return pl.pallas_call(
        functools.partial(own_kernel, scale, heads),
        out_shape=(
            jax.ShapeDtypeStruct((WIN, width), F32),
            jax.ShapeDtypeStruct((WIN, DH), F32),
            jax.ShapeDtypeStruct((tokens, width), BF),
        ),
        in_specs=[WHOLE] * 3,
        out_specs=(WHOLE,) * 3,
        compiler_params=params(30),
        cost_estimate=cost(1),
        name="own_attention",
    )(queries, keys, values)


def edge_part(scale, slots, tail, q_ref, k_ref, v_ref, out_ref, lse_ref):
    lower = triangle()
    c = scale * LOG2E
    lanes = lax.broadcasted_iota(jnp.int32, (EDGE, DH), 1)
    count = len(slots)
    lse_ref[...] = jnp.zeros_like(lse_ref)
    for slot, (q_head, k_head, v_head) in enumerate(slots):
        q_cols = pl.ds(q_head * DH, DH)
        k_cols = pl.ds(k_head * DH, DH)
        v_cols = pl.ds(v_head * DH, DH)
        for i in range(WIN // EDGE):
            rows = pl.ds(i * EDGE, EDGE)
            seen = pl.ds(tail + i * EDGE, WIN - i * EDGE)
            s = dot_t(q_ref[rows, q_cols], k_ref[seen, k_cols])
            edge = jnp.where(lower, NEG, s[:, :EDGE])
            if s.shape[1] > EDGE:
                s = jnp.concatenate([edge, s[:, EDGE:]], axis=1)
            else:
                s = edge
            top = jnp.max(s, axis=1, keepdims=True)
            p = jnp.exp2((s - top) * c).astype(BF)
            acc = dot(p, with_ones(v_ref[seen, v_cols]))
            total = acc[:, DH:]
            out_ref[rows, pl.ds(slot * DH, DH)] = (acc[:, :DH] / total).astype(BF)
            lse_ref[rows, :] = jnp.where(lanes == slot, top * c + jnp.log2(total), lse_ref[rows, :])
    stat = lse_ref[...]
    high = stat.astype(BF).astype(F32)
    mid = (stat - high).astype(BF).astype(F32)
    low = (stat - high - mid).astype(BF).astype(F32)
    packed = high + pltpu.roll(mid, count, 1) + pltpu.roll(low, 2 * count, 1)
    out_ref[:, pl.ds(count * DH, DH)] = packed.astype(BF)


def edge_kernel(
    scale, heads, far_q_ref, near_kv_ref, q_ref, k_ref, v_ref, far_ref, near_ref, lse_ref
):
    far = [(head - FORWARD, head, head) for head in range(FORWARD, heads)]
    near = [(head, head, FORWARD + head) for head in range(FORWARD)]
    tail = k_ref.shape[0] - WIN
    edge_part(scale, far, tail, far_q_ref, k_ref, v_ref, far_ref, lse_ref)
    edge_part(scale, near, 0, q_ref, near_kv_ref, near_kv_ref, near_ref, lse_ref)


def edge_attention(far_q, near_kv, queries, keys, values, heads, scale):
    return pl.pallas_call(
        functools.partial(edge_kernel, scale, heads),
        out_shape=(
            jax.ShapeDtypeStruct((WIN, (heads - FORWARD + 1) * DH), BF),
            jax.ShapeDtypeStruct((WIN, (FORWARD + 1) * DH), BF),
        ),
        in_specs=[WHOLE] * 5,
        out_specs=(WHOLE,) * 2,
        scratch_shapes=[pltpu.VMEM((WIN, DH), F32)],
        compiler_params=params(24),
        cost_estimate=cost(60),
        name="edge_attention",
    )(far_q, near_kv, queries, keys, values)


def unpacked(stat, count):
    return stat + pltpu.roll(stat, DH - count, 1) + pltpu.roll(stat, DH - 2 * count, 1)


def merge_kernel(heads, first_ref, low_ref, lse_ref, near_ref, far_ref, into_ref, out_ref):
    del into_ref
    lanes = lax.broadcasted_iota(jnp.int32, (EDGE, DH), 1)
    behind = heads - FORWARD
    for i in range(WIN // EDGE):
        rows = pl.ds(i * EDGE, EDGE)
        near_stat = unpacked(near_ref[rows, pl.ds(FORWARD * DH, DH)].astype(F32), FORWARD)
        far_stat = unpacked(far_ref[rows, pl.ds(behind * DH, DH)].astype(F32), behind)
        other = jnp.where(lanes < FORWARD, near_stat, pltpu.roll(far_stat, FORWARD, 1))
        other = jnp.where(first_ref[0] == 0, NEG, other)
        own = jnp.where(lanes < heads, lse_ref[rows, :], 0.0)
        shares = 1.0 / (1.0 + jnp.exp2(other - own))
        for head in range(heads):
            ref, slot = (near_ref, head) if head < FORWARD else (far_ref, head - FORWARD)
            share = shares[:, head : head + 1]
            cols = pl.ds(head * DH, DH)
            mine = low_ref[rows, cols]
            there = ref[rows, pl.ds(slot * DH, DH)].astype(F32)
            out_ref[rows, cols] = (there + (mine - there) * share).astype(BF)


def merge(first, low, lse, near, far, local, heads):
    width = low.shape[1]
    whole = lambda array: pl.BlockSpec(array.shape, lambda i: (0, 0))
    return pl.pallas_call(
        functools.partial(merge_kernel, heads),
        out_shape=pltpu.HBM(local.shape, BF),
        grid=(1,),
        in_specs=[SMALL, whole(low), whole(lse), whole(near), whole(far), ANY],
        out_specs=pl.BlockSpec((WIN, width), lambda i: (0, 0)),
        input_output_aliases={5: 0},
        compiler_params=params(16),
        cost_estimate=cost(60),
        name="merge_local",
    )(first, low, lse, near, far, in_hbm(local))


def final_kernel(
    scale, heads, gate_ref, q_hbm, kv_hbm, local_hbm, out_hbm, q_ref, kv_ref, local_ref, out_ref, sems, out_sems
):
    c = scale * LOG2E
    pieces = MB // PIECE
    blocks = q_hbm.shape[0] // QB
    step = heads // HALVES
    chunks = [(block, half) for block in range(blocks) for half in range(HALVES)]
    loads, stores = [], []
    for index, (block, half) in enumerate(chunks):
        area = (pl.ds(block * QB, QB), pl.ds(half * step * DH, step * DH))
        mine = (slice(None), pl.ds((block * heads + half * step) * TOPK, step * TOPK))
        loads.append(
            [
                pltpu.make_async_copy(source.at[where], target.at[where], sems.at[index, kind])
                for kind, (source, target, where) in enumerate(
                    ((kv_hbm, kv_ref, mine), (q_hbm, q_ref, area), (local_hbm, local_ref, area))
                )
            ]
        )
        stores.append(pltpu.make_async_copy(out_ref.at[area], out_hbm.at[area], out_sems.at[index]))
    for index in range(DEPTH):
        for load in loads[index]:
            load.start()
    for index, (block, half) in enumerate(chunks):
        for load in loads[index]:
            load.wait()
        if index + DEPTH < len(chunks):
            for load in loads[index + DEPTH]:
                load.start()
        rows = pl.ds(block * QB, QB)
        for head in range(half * step, (half + 1) * step):
            cols = pl.ds(head * DH, DH)
            mine = pl.ds((block * heads + head) * TOPK, TOPK)
            keys = kv_ref[0:pieces, mine].astype(F32).reshape(TOPK * MB, DH).astype(BF)
            values = kv_ref[pieces : 2 * pieces, mine].astype(F32).reshape(TOPK * MB, DH).astype(BF)
            s = dot_t(q_ref[rows, cols], keys)
            top = jnp.max(s, axis=1, keepdims=True)
            p = jnp.exp2((s - top) * c).astype(BF)
            acc = dot(p, with_ones(values))
            gate = gate_ref[head]
            remote = acc[:, :DH] * (gate / acc[:, DH:])
            local = local_ref[rows, cols].astype(F32)
            out_ref[rows, cols] = (remote + (1.0 - gate) * local).astype(BF)
        stores[index].start()
    for store in stores:
        store.wait()


def final_attention(gate, queries, kv, local, heads, scale):
    chunks = queries.shape[0] // QB * HALVES
    return pl.pallas_call(
        functools.partial(final_kernel, scale, heads),
        out_shape=pltpu.HBM(queries.shape, BF),
        in_specs=[SMALL, ANY, ANY, ANY],
        out_specs=ANY,
        scratch_shapes=[
            pltpu.VMEM(queries.shape, BF),
            pltpu.VMEM(kv.shape, BF),
            pltpu.VMEM(queries.shape, BF),
            pltpu.VMEM(queries.shape, BF),
            pltpu.SemaphoreType.DMA((chunks, 3)),
            pltpu.SemaphoreType.DMA((chunks,)),
        ],
        compiler_params=params(24),
        cost_estimate=cost(7),
        name="final_attention",
    )(gate, in_hbm(queries), in_hbm(kv), in_hbm(local))


def body(queries, token_keys, token_values, mem_keys, mem_values, retrieved, gate_bias):
    tokens = queries.shape[0]
    heads = gate_bias.shape[0]
    scale = DH ** (-0.5)
    devices = lax.axis_size("seq")
    blocks = mem_keys.shape[0] // MB
    q_blocks = tokens // QB
    wanted = q_blocks * heads * TOPK
    upward = [(i, i + 1) for i in range(devices - 1)]
    downward = [(i, i - 1) for i in range(1, devices)]
    split = FORWARD * DH
    tail = tokens - WIN
    back_q = cut([queries], [(0, split)], heads * DH - split, "cut_queries")
    far_q = lax.ppermute(back_q, "seq", downward)
    ahead_kv = cut([token_keys, token_values], [(tail, 0)] * 2, 2 * split, "cut_tails")
    near_kv = lax.ppermute(ahead_kv, "seq", upward)
    ids = retrieved.reshape(-1)
    ids_tile = jnp.zeros((PIECE * DH,), BF).at[:wanted].set(ids.astype(BF)).reshape(PIECE, DH)
    ids_tile, _, _ = lax.optimization_barrier((ids_tile, back_q, ahead_kv))
    sent = pack(mem_keys, mem_values, ids_tile, blocks, heads)
    store = lax.all_to_all(sent, "seq", split_axis=0, concat_axis=0, tiled=True)
    gate_share = 1.0 / (1.0 + jnp.exp(-gate_bias))
    first = lax.axis_index("seq").reshape(1).astype(jnp.int32)
    low, lse, local = own_attention(queries, token_keys, token_values, heads, scale)
    low, edge_q, edge_k, edge_v = lax.optimization_barrier(
        (low, queries, token_keys, token_values)
    )
    far_part, near = edge_attention(far_q, near_kv, edge_q, edge_k, edge_v, heads, scale)
    far = lax.ppermute(far_part, "seq", upward)
    store, low, lse, local, near, _ = lax.optimization_barrier(
        (store, low, lse, local, near, far_part)
    )
    pieces = gather(store, blocks, heads, wanted)
    kv = lax.all_to_all(pieces, "seq", split_axis=0, concat_axis=0, tiled=True)
    local = merge(first, low, lse, near, far, local, heads)
    kv, local = lax.optimization_barrier((kv, local))
    return final_attention(gate_share, queries, kv, local, heads, scale)


def solution(mesh):
    in_specs = (
        P("seq", "head"),
        P("seq", "head"),
        P("seq", "head"),
        P("seq", "head"),
        P("seq", "head"),
        P("seq", "head", None),
        P("head"),
    )
    return jax.shard_map(
        body, mesh=mesh, in_specs=in_specs, out_specs=P("seq", "head"), check_vma=False
    )
```

```python
import functools

import jax
import jax.numpy as jnp
from jax import lax
from jax.experimental import pallas as pl
from jax.experimental.pallas import tpu as pltpu
from jax.sharding import PartitionSpec as P

QB = 512
MB = 128
TOPK = 2
WIN = 512
DH = 128
PIECE = 8
EDGE = 256
FORWARD = 4
HALVES = 2
DEPTH = 2
LOG2E = 1.4426950408889634
NEG = -1e30
BF = jnp.bfloat16
F32 = jnp.float32
ANY = pl.BlockSpec(memory_space=pl.ANY)
WHOLE = pl.BlockSpec(memory_space=pltpu.VMEM)
SMALL = pl.BlockSpec(memory_space=pltpu.SMEM)


def params(mebibytes):
    return pltpu.CompilerParams(vmem_limit_bytes=mebibytes << 20)


def cost(micros):
    return pl.CostEstimate(flops=int(micros * 1e9), transcendentals=0, bytes_accessed=0)


def in_hbm(array):
    return pltpu.with_memory_space_constraint(array, pltpu.HBM)


def copy_all(copies):
    for copy in copies:
        copy.start()
    for copy in copies:
        copy.wait()


def cut_kernel(areas, *refs):
    out_ref, sems = refs[-2:]
    width = out_ref.shape[1] // len(areas)
    copies = [
        pltpu.make_async_copy(
            ref.at[pl.ds(row, WIN), pl.ds(col, width)],
            out_ref.at[:, pl.ds(index * width, width)],
            sems.at[index],
        )
        for index, (ref, (row, col)) in enumerate(zip(refs, areas))
    ]
    copy_all(copies)


def cut(arrays, areas, width, name):
    return pl.pallas_call(
        functools.partial(cut_kernel, areas),
        out_shape=jax.ShapeDtypeStruct((WIN, width), BF),
        in_specs=[ANY] * len(arrays),
        out_specs=WHOLE,
        scratch_shapes=[pltpu.SemaphoreType.DMA((len(arrays),))],
        compiler_params=params(4),
        cost_estimate=cost(2),
        name=name,
    )(*map(in_hbm, arrays))


def pack_kernel(blocks, heads, keys_ref, values_ref, ids_ref, out_ref, stage, in_sems, out_sems):
    pieces = MB // PIECE
    loads, stores = [], []
    for half, source in enumerate((keys_ref, values_ref)):
        for block in range(blocks):
            slot = len(loads)
            here = stage.at[pl.ds(slot * pieces, pieces)]
            there = out_ref.at[pl.ds(half * pieces, pieces), pl.ds(block * heads, heads)]
            rows = pl.ds(block * pieces, pieces)
            loads.append(pltpu.make_async_copy(source.at[rows], here, in_sems.at[slot]))
            stores.append(pltpu.make_async_copy(here, there, out_sems.at[slot]))
    ids_store = pltpu.make_async_copy(
        ids_ref, out_ref.at[:, pl.ds(blocks * heads, 1)], out_sems.at[2 * blocks]
    )
    for load in loads:
        load.start()
    ids_store.start()
    for load, store in zip(loads, stores):
        load.wait()
        store.start()
    for store in stores:
        store.wait()
    ids_store.wait()


def tiles(array):
    rows, width = array.shape
    return array.reshape(rows // PIECE, PIECE, width // DH, DH).transpose(0, 2, 1, 3)


def pack(mem_keys, mem_values, ids_tile, blocks, heads):
    devices = 2 * MB // PIECE
    return pl.pallas_call(
        functools.partial(pack_kernel, blocks, heads),
        out_shape=pltpu.HBM((devices, blocks * heads + 1, PIECE, DH), BF),
        in_specs=[ANY, ANY, WHOLE],
        out_specs=ANY,
        scratch_shapes=[
            pltpu.VMEM((2 * blocks * MB // PIECE, heads, PIECE, DH), BF),
            pltpu.SemaphoreType.DMA((2 * blocks,)),
            pltpu.SemaphoreType.DMA((2 * blocks + 1,)),
        ],
        compiler_params=params(8),
        cost_estimate=cost(2),
        name="pack_pieces",
    )(
        in_hbm(tiles(mem_keys)),
        in_hbm(tiles(mem_values)),
        jnp.broadcast_to(ids_tile, (devices, 1, PIECE, DH)),
    )


def gather_kernel(
    blocks, heads, wanted, store_ref, out_ref, ids, rows_v, rows_s, store, stage, ids_sem, sems, out_sems
):
    devices, stride = store_ref.shape[:2]
    parts = sems.shape[0]
    groups = out_sems.shape[0]
    size = devices // groups
    ids_load = pltpu.make_async_copy(store_ref.at[:, stride - 1], ids, ids_sem.at[0])
    ids_load.start()
    loads, stores = [], []
    for part in range(parts):
        span = pl.ds(part * (devices // parts), devices // parts)
        loads.append(pltpu.make_async_copy(store_ref.at[span], store.at[span], sems.at[part]))
    for group in range(groups):
        span = pl.ds(group * size, size)
        stores.append(pltpu.make_async_copy(stage.at[span], out_ref.at[span], out_sems.at[group]))
    for load in loads:
        load.start()
    ids_load.wait()
    row = lax.broadcasted_iota(jnp.int32, (devices, PIECE, DH), 1)
    block = jnp.sum(jnp.where(row == 0, ids[...].astype(F32), 0.0), axis=1).astype(jnp.int32)
    lane = lax.broadcasted_iota(jnp.int32, (devices, DH), 1)
    head = lane // TOPK % heads
    rows_v[...] = block // blocks * stride + block % blocks * heads + head
    rows_copy = pltpu.make_async_copy(rows_v, rows_s, ids_sem.at[1])
    rows_copy.start()
    rows_copy.wait()
    for load in loads:
        load.wait()
    flat = store.reshape(devices * stride, PIECE, DH)
    for group in range(groups):

        @pl.loop(group * size, (group + 1) * size)
        def _(device):
            for request in range(wanted):
                stage[device, request] = flat[rows_s[device, request]]

        stores[group].start()
    for store_copy in stores:
        store_copy.wait()


def gather(store, blocks, heads, wanted):
    devices = store.shape[0]
    return pl.pallas_call(
        functools.partial(gather_kernel, blocks, heads, wanted),
        out_shape=pltpu.HBM((devices, wanted, PIECE, DH), BF),
        in_specs=[ANY],
        out_specs=ANY,
        scratch_shapes=[
            pltpu.VMEM((devices, PIECE, DH), BF),
            pltpu.VMEM((devices, DH), jnp.int32),
            pltpu.SMEM((devices, DH), jnp.int32),
            pltpu.VMEM(store.shape, BF),
            pltpu.VMEM((devices, wanted, PIECE, DH), BF),
            pltpu.SemaphoreType.DMA((2,)),
            pltpu.SemaphoreType.DMA((4,)),
            pltpu.SemaphoreType.DMA((8,)),
        ],
        compiler_params=params(16),
        cost_estimate=cost(6),
        name="gather_pieces",
    )(in_hbm(store))


def dot_t(a, b):
    return lax.dot_general(a, b, (((1,), (1,)), ((), ())), preferred_element_type=F32)


def dot(a, b):
    return jnp.dot(a, b, preferred_element_type=F32)


def with_ones(values):
    return jnp.concatenate([values, jnp.ones_like(values)], axis=1)


def triangle():
    row = lax.broadcasted_iota(jnp.int32, (EDGE, EDGE), 0)
    col = lax.broadcasted_iota(jnp.int32, (EDGE, EDGE), 1)
    return col <= row


def own_kernel(scale, heads, q_ref, k_ref, v_ref, low_ref, lse_ref, out_ref):
    lower = triangle()
    c = scale * LOG2E
    lanes = lax.broadcasted_iota(jnp.int32, (EDGE, DH), 1)
    for head in range(heads):
        cols = pl.ds(head * DH, DH)
        for i in range(WIN // EDGE):
            rows = pl.ds(i * EDGE, EDGE)
            seen = pl.ds(0, (i + 1) * EDGE)
            s = dot_t(q_ref[rows, cols], k_ref[seen, cols])
            diag = jnp.where(lower, s[:, i * EDGE :], NEG)
            if i:
                s = jnp.concatenate([s[:, : i * EDGE], diag], axis=1)
            else:
                s = diag
            top = jnp.max(s, axis=1, keepdims=True)
            p = jnp.exp2((s - top) * c).astype(BF)
            acc = dot(p, with_ones(v_ref[seen, cols]))
            total = acc[:, DH:]
            low_ref[rows, cols] = acc[:, :DH] / total
            lse_ref[rows, :] = jnp.where(lanes == head, top * c + jnp.log2(total), lse_ref[rows, :])
        for i in range(WIN // EDGE, q_ref.shape[0] // EDGE):
            rows = pl.ds(i * EDGE, EDGE)
            seen = pl.ds(i * EDGE - WIN, WIN + EDGE)
            s = dot_t(q_ref[rows, cols], k_ref[seen, cols])
            ends = jnp.where(lower, s[:, WIN:], s[:, :EDGE])
            mid = s[:, EDGE:WIN]
            top = jnp.maximum(
                jnp.max(ends, axis=1, keepdims=True), jnp.max(mid, axis=1, keepdims=True)
            )
            ends = jnp.exp2((ends - top) * c)
            mid = jnp.exp2((mid - top) * c).astype(BF)
            first = jnp.where(lower, 0.0, ends).astype(BF)
            last = jnp.where(lower, ends, 0.0).astype(BF)
            acc = dot(jnp.concatenate([first, mid, last], axis=1), with_ones(v_ref[seen, cols]))
            out_ref[rows, cols] = (acc[:, :DH] / acc[:, DH:]).astype(BF)


def own_attention(queries, keys, values, heads, scale):
    tokens, width = queries.shape
    return pl.pallas_call(
        functools.partial(own_kernel, scale, heads),
        out_shape=(
            jax.ShapeDtypeStruct((WIN, width), F32),
            jax.ShapeDtypeStruct((WIN, DH), F32),
            jax.ShapeDtypeStruct((tokens, width), BF),
        ),
        in_specs=[WHOLE] * 3,
        out_specs=(WHOLE,) * 3,
        compiler_params=params(30),
        cost_estimate=cost(1),
        name="own_attention",
    )(queries, keys, values)


def edge_part(scale, slots, tail, q_ref, k_ref, v_ref, out_ref, lse_ref):
    lower = triangle()
    c = scale * LOG2E
    lanes = lax.broadcasted_iota(jnp.int32, (EDGE, DH), 1)
    count = len(slots)
    lse_ref[...] = jnp.zeros_like(lse_ref)
    for slot, (q_head, k_head, v_head) in enumerate(slots):
        q_cols = pl.ds(q_head * DH, DH)
        k_cols = pl.ds(k_head * DH, DH)
        v_cols = pl.ds(v_head * DH, DH)
        for i in range(WIN // EDGE):
            rows = pl.ds(i * EDGE, EDGE)
            seen = pl.ds(tail + i * EDGE, WIN - i * EDGE)
            s = dot_t(q_ref[rows, q_cols], k_ref[seen, k_cols])
            edge = jnp.where(lower, NEG, s[:, :EDGE])
            if s.shape[1] > EDGE:
                s = jnp.concatenate([edge, s[:, EDGE:]], axis=1)
            else:
                s = edge
            top = jnp.max(s, axis=1, keepdims=True)
            p = jnp.exp2((s - top) * c).astype(BF)
            acc = dot(p, with_ones(v_ref[seen, v_cols]))
            total = acc[:, DH:]
            out_ref[rows, pl.ds(slot * DH, DH)] = (acc[:, :DH] / total).astype(BF)
            lse_ref[rows, :] = jnp.where(lanes == slot, top * c + jnp.log2(total), lse_ref[rows, :])
    stat = lse_ref[...]
    high = stat.astype(BF).astype(F32)
    mid = (stat - high).astype(BF).astype(F32)
    low = (stat - high - mid).astype(BF).astype(F32)
    packed = high + pltpu.roll(mid, count, 1) + pltpu.roll(low, 2 * count, 1)
    out_ref[:, pl.ds(count * DH, DH)] = packed.astype(BF)


def edge_kernel(
    scale, heads, far_q_ref, near_kv_ref, q_ref, k_ref, v_ref, far_ref, near_ref, lse_ref
):
    far = [(head - FORWARD, head, head) for head in range(FORWARD, heads)]
    near = [(head, head, FORWARD + head) for head in range(FORWARD)]
    tail = k_ref.shape[0] - WIN
    edge_part(scale, far, tail, far_q_ref, k_ref, v_ref, far_ref, lse_ref)
    edge_part(scale, near, 0, q_ref, near_kv_ref, near_kv_ref, near_ref, lse_ref)


def edge_attention(far_q, near_kv, queries, keys, values, heads, scale):
    return pl.pallas_call(
        functools.partial(edge_kernel, scale, heads),
        out_shape=(
            jax.ShapeDtypeStruct((WIN, (heads - FORWARD + 1) * DH), BF),
            jax.ShapeDtypeStruct((WIN, (FORWARD + 1) * DH), BF),
        ),
        in_specs=[WHOLE] * 5,
        out_specs=(WHOLE,) * 2,
        scratch_shapes=[pltpu.VMEM((WIN, DH), F32)],
        compiler_params=params(24),
        cost_estimate=cost(60),
        name="edge_attention",
    )(far_q, near_kv, queries, keys, values)


def unpacked(stat, count):
    return stat + pltpu.roll(stat, DH - count, 1) + pltpu.roll(stat, DH - 2 * count, 1)


def merge_kernel(heads, first_ref, low_ref, lse_ref, near_ref, far_ref, into_ref, out_ref):
    del into_ref
    lanes = lax.broadcasted_iota(jnp.int32, (EDGE, DH), 1)
    behind = heads - FORWARD
    for i in range(WIN // EDGE):
        rows = pl.ds(i * EDGE, EDGE)
        near_stat = unpacked(near_ref[rows, pl.ds(FORWARD * DH, DH)].astype(F32), FORWARD)
        far_stat = unpacked(far_ref[rows, pl.ds(behind * DH, DH)].astype(F32), behind)
        other = jnp.where(lanes < FORWARD, near_stat, pltpu.roll(far_stat, FORWARD, 1))
        other = jnp.where(first_ref[0] == 0, NEG, other)
        own = jnp.where(lanes < heads, lse_ref[rows, :], 0.0)
        shares = 1.0 / (1.0 + jnp.exp2(other - own))
        for head in range(heads):
            ref, slot = (near_ref, head) if head < FORWARD else (far_ref, head - FORWARD)
            share = shares[:, head : head + 1]
            cols = pl.ds(head * DH, DH)
            mine = low_ref[rows, cols]
            there = ref[rows, pl.ds(slot * DH, DH)].astype(F32)
            out_ref[rows, cols] = (there + (mine - there) * share).astype(BF)


def merge(first, low, lse, near, far, local, heads):
    width = low.shape[1]
    whole = lambda array: pl.BlockSpec(array.shape, lambda i: (0, 0))
    return pl.pallas_call(
        functools.partial(merge_kernel, heads),
        out_shape=pltpu.HBM(local.shape, BF),
        grid=(1,),
        in_specs=[SMALL, whole(low), whole(lse), whole(near), whole(far), ANY],
        out_specs=pl.BlockSpec((WIN, width), lambda i: (0, 0)),
        input_output_aliases={5: 0},
        compiler_params=params(16),
        cost_estimate=cost(60),
        name="merge_local",
    )(first, low, lse, near, far, in_hbm(local))


def final_kernel(
    scale, heads, gate_ref, q_hbm, kv_hbm, local_hbm, out_hbm, q_ref, kv_ref, local_ref, out_ref, sems, out_sems
):
    c = scale * LOG2E
    pieces = MB // PIECE
    blocks = q_hbm.shape[0] // QB
    step = heads // HALVES
    chunks = [(block, half) for block in range(blocks) for half in range(HALVES)]
    loads, stores = [], []
    for index, (block, half) in enumerate(chunks):
        area = (pl.ds(block * QB, QB), pl.ds(half * step * DH, step * DH))
        mine = (slice(None), pl.ds((block * heads + half * step) * TOPK, step * TOPK))
        loads.append(
            [
                pltpu.make_async_copy(source.at[where], target.at[where], sems.at[index, kind])
                for kind, (source, target, where) in enumerate(
                    ((kv_hbm, kv_ref, mine), (q_hbm, q_ref, area), (local_hbm, local_ref, area))
                )
            ]
        )
        stores.append(pltpu.make_async_copy(out_ref.at[area], out_hbm.at[area], out_sems.at[index]))
    for index in range(DEPTH):
        for load in loads[index]:
            load.start()
    for index, (block, half) in enumerate(chunks):
        for load in loads[index]:
            load.wait()
        if index + DEPTH < len(chunks):
            for load in loads[index + DEPTH]:
                load.start()
        rows = pl.ds(block * QB, QB)
        for head in range(half * step, (half + 1) * step):
            cols = pl.ds(head * DH, DH)
            mine = pl.ds((block * heads + head) * TOPK, TOPK)
            keys = kv_ref[0:pieces, mine].astype(F32).reshape(TOPK * MB, DH).astype(BF)
            values = kv_ref[pieces : 2 * pieces, mine].astype(F32).reshape(TOPK * MB, DH).astype(BF)
            s = dot_t(q_ref[rows, cols], keys)
            top = jnp.max(s, axis=1, keepdims=True)
            p = jnp.exp2((s - top) * c).astype(BF)
            acc = dot(p, with_ones(values))
            gate = gate_ref[head]
            remote = acc[:, :DH] * (gate / acc[:, DH:])
            local = local_ref[rows, cols].astype(F32)
            out_ref[rows, cols] = (remote + (1.0 - gate) * local).astype(BF)
        stores[index].start()
    for store in stores:
        store.wait()


def final_attention(gate, queries, kv, local, heads, scale):
    chunks = queries.shape[0] // QB * HALVES
    return pl.pallas_call(
        functools.partial(final_kernel, scale, heads),
        out_shape=pltpu.HBM(queries.shape, BF),
        in_specs=[SMALL, ANY, ANY, ANY],
        out_specs=ANY,
        scratch_shapes=[
            pltpu.VMEM(queries.shape, BF),
            pltpu.VMEM(kv.shape, BF),
            pltpu.VMEM(queries.shape, BF),
            pltpu.VMEM(queries.shape, BF),
            pltpu.SemaphoreType.DMA((chunks, 3)),
            pltpu.SemaphoreType.DMA((chunks,)),
        ],
        compiler_params=params(24),
        cost_estimate=cost(7),
        name="final_attention",
    )(gate, in_hbm(queries), in_hbm(kv), in_hbm(local))


def body(queries, token_keys, token_values, mem_keys, mem_values, retrieved, gate_bias):
    tokens = queries.shape[0]
    heads = gate_bias.shape[0]
    scale = DH ** (-0.5)
    devices = lax.axis_size("seq")
    blocks = mem_keys.shape[0] // MB
    q_blocks = tokens // QB
    wanted = q_blocks * heads * TOPK
    upward = [(i, i + 1) for i in range(devices - 1)]
    downward = [(i, i - 1) for i in range(1, devices)]
    split = FORWARD * DH
    tail = tokens - WIN
    back_q = cut([queries], [(0, split)], heads * DH - split, "cut_queries")
    far_q = lax.ppermute(back_q, "seq", downward)
    ahead_kv = cut([token_keys, token_values], [(tail, 0)] * 2, 2 * split, "cut_tails")
    near_kv = lax.ppermute(ahead_kv, "seq", upward)
    ids = retrieved.reshape(-1)
    ids_tile = jnp.zeros((PIECE * DH,), BF).at[:wanted].set(ids.astype(BF)).reshape(PIECE, DH)
    ids_tile, _, _ = lax.optimization_barrier((ids_tile, back_q, ahead_kv))
    sent = pack(mem_keys, mem_values, ids_tile, blocks, heads)
    store = lax.all_to_all(sent, "seq", split_axis=0, concat_axis=0, tiled=True)
    gate_share = 1.0 / (1.0 + jnp.exp(-gate_bias))
    first = lax.axis_index("seq").reshape(1).astype(jnp.int32)
    low, lse, local = own_attention(queries, token_keys, token_values, heads, scale)
    low, edge_q, edge_k, edge_v = lax.optimization_barrier(
        (low, queries, token_keys, token_values)
    )
    far_part, near = edge_attention(in_hbm(far_q), in_hbm(near_kv), edge_q, edge_k, edge_v, heads, scale)
    far = lax.ppermute(far_part, "seq", upward)
    store, low, lse, local, near, _ = lax.optimization_barrier(
        (store, low, lse, local, near, far_part)
    )
    pieces = gather(store, blocks, heads, wanted)
    kv = lax.all_to_all(pieces, "seq", split_axis=0, concat_axis=0, tiled=True)
    local = merge(first, low, lse, near, far, local, heads)
    kv, local = lax.optimization_barrier((kv, local))
    return final_attention(gate_share, queries, kv, local, heads, scale)


def solution(mesh):
    in_specs = (
        P("seq", "head"),
        P("seq", "head"),
        P("seq", "head"),
        P("seq", "head"),
        P("seq", "head"),
        P("seq", "head", None),
        P("head"),
    )
    return jax.shard_map(
        body, mesh=mesh, in_specs=in_specs, out_specs=P("seq", "head"), check_vma=False
    )
```
